32 devices in a mesh: cfg: 2 (over y), win: 16 (over z, x, core).
Axes of the slice: x: 2, y: 2, z: 4, core: 2. Of those that a mesh axis runs over, the one named last changes fastest.
Arguments:
- latent: float32 [512, 4, 32], P('win'), may hold values from -6 to 6
- text_kv: bfloat16 [2, 2, 120, 576], P(None, None, None, 'cfg'), may hold values from -200 to 200, as said below
- modulation: float32 [20, 4, 1152], replicated, may hold values from -3 to 3
- qkv_weight: bfloat16 [1152, 3, 576], P(None, None, 'cfg'), may hold values from -0.1875 to 0.1875
- out_weight: bfloat16 [576, 1152], P('cfg'), may hold values from -0.25 to 0.25
- patch_weight: bfloat16 [16, 1152], replicated, may hold values from -1.5 to 1.5
- final_weight: bfloat16 [1152, 16], replicated, may hold values from -0.1875 to 0.1875
- offsets: int32 [16], P('win'), may hold values from 1 to 16
- blend_weights: int32 [16], P('win'), may hold values from 1 to 4
- step_index: int32 [1], replicated, may hold values from 0 to 999
Outputs:
- previous: float32 [512, 4, 32], P('win', None, 'cfg')
- noise: float32 [512, 4, 32], P('win', None, 'cfg')
The draws below stay inside these ranges and needn't reach their ends.
Inputs may be any that keep to these rules, and one draw needn't show every extreme that they name: Window i starts offsets[i] columns before column i * 32. `text_kv`: keys and values of caption tokens.
All inputs are finite; a program needn't handle non-finite values.
Results may differ from the reference program's by a relative error of at most 0.024.
Values may be sent and summed in bfloat16 or wider, within the bound.
No kernel may reach another device: no remote copies, remote signals or barrier semaphores. Data moves between devices by JAX's collectives and lax.ppermute only.
A program may use at most 64 MiB of HBM per device.

```python
import math
import jax
import jax.numpy as jnp
from jax import lax

D = 1152
HEAD_DIM = 72
CHANNELS = 4
CTX = 120
SLAB = 32
LAT_H = 32
STEPS = 20
ATTN = 576
LAT_W = 512
N_WIN = 16


def draw_text_kv(key, part):
    base = jax.random.normal(jax.random.fold_in(key, 11), (2, 2, CTX, ATTN), jnp.float32)
    base = jnp.clip(base, -4.0, 4.0)
    return base.astype(jnp.bfloat16)


def set_ends(drawn, key, low, high):
    shape = drawn.shape
    index_at = [jax.random.randint(jax.random.fold_in(key, axis), (), 0, shape[axis]) for axis in range(len(shape))]
    drawn = drawn.at[tuple(index_at)].set(low)
    longest = shape.index(max(shape))
    index_at[longest] = (index_at[longest] + 1) % shape[longest]
    return drawn.at[tuple(index_at)].set(high)


def block_scale(key, shape, split, least, largest):
    level = 1.0
    for dim, parts in split:
        draws = jax.random.uniform(jax.random.fold_in(jax.random.fold_in(key, 6), dim), (parts,), jnp.float32, least / len(split), largest / len(split))
        level = level * jnp.repeat(jnp.exp(draws), shape[dim] // parts).reshape((-1,) + (1,) * (len(shape) - 1 - dim))
    return level


def normal_values(key, shape, scale, bound, shards=(), kind=jnp.bfloat16):
    entries = scale * jax.random.normal(key, shape, jnp.float32)
    if shards:
        entries = entries * block_scale(key, shape, shards, -0.22, 0.18)
    return jnp.clip(entries, -bound, bound).astype(kind)


def setup_inputs(seed: int = 0) -> dict:
    key_of = jax.random.split(jax.random.key(seed), 11)
    latent = normal_values(key_of[0], (LAT_W, CHANNELS, LAT_H), 1.0, 6.0, ((0, 16),), jnp.float32)
    text_kv = draw_text_kv(jax.random.fold_in(key_of[10], 71), 0)
    modulation = normal_values(key_of[2], (STEPS, 4, D), 0.5, 3.0, (), jnp.float32)
    qkv_weight = normal_values(key_of[3], (D, 3, ATTN), D ** -0.5, 0.1875, ((2, 2),))
    out_weight = normal_values(key_of[4], (ATTN, D), ATTN ** -0.5, 0.25, ((0, 2),))
    patch_weight = normal_values(key_of[5], (4 * CHANNELS, D), (4 * CHANNELS) ** -0.5, 1.5)
    final_weight = normal_values(key_of[6], (D, 4 * CHANNELS), D ** -0.5, 0.1875)
    offsets = set_ends(jax.random.randint(key_of[7], (N_WIN,), 1, SLAB // 2 + 1), jax.random.fold_in(key_of[7], 1), 1, (SLAB // 2 + 1) - 1).astype(jnp.int32)
    blend_weights = set_ends(jax.random.randint(key_of[8], (N_WIN,), 1, 5), jax.random.fold_in(key_of[8], 1), 1, 4).astype(jnp.int32)
    step_index = jax.random.randint(key_of[9], (1,), 0, 1000).astype(jnp.int32)
    return {"latent": latent, "text_kv": text_kv, "modulation": modulation, "qkv_weight": qkv_weight, "out_weight": out_weight, "patch_weight": patch_weight, "final_weight": final_weight, "offsets": offsets, "blend_weights": blend_weights, "step_index": step_index}


guidance_scale = 4.5
plan_length = 1000
norm_eps = 1e-06

def layer_norm(values):
    average = lax.optimization_barrier(jnp.mean(values, axis=-1, keepdims=True))
    centered = values - average
    variance = lax.optimization_barrier(jnp.mean(centered * centered, axis=-1, keepdims=True))
    return centered * lax.rsqrt(variance + norm_eps)

def positions(col_pairs, row_couples, model_width):
    quarter = model_width // 4
    frequency = jnp.exp(-math.log(10000.0) * jnp.arange(quarter, dtype=jnp.float32) / quarter)
    col_pos = jnp.arange(col_pairs, dtype=jnp.float32)[:, None] * frequency[None, :]
    row_pos = jnp.arange(row_couples, dtype=jnp.float32)[:, None] * frequency[None, :]
    col_part = jnp.concatenate([jnp.sin(col_pos), jnp.cos(col_pos)], axis=1)
    row_part = jnp.concatenate([jnp.sin(row_pos), jnp.cos(row_pos)], axis=1)
    half_width = model_width // 2
    pos_table = jnp.concatenate([jnp.broadcast_to(row_part[None, :, :], (col_pairs, row_couples, half_width)), jnp.broadcast_to(col_part[:, None, :], (col_pairs, row_couples, half_width))], axis=2)
    return pos_table.reshape(col_pairs * row_couples, model_width)

def plan(moment):
    train_grid = jnp.arange(plan_length, dtype=jnp.int32)
    beta_values = 0.0001 + (0.02 - 0.0001) * train_grid.astype(jnp.float32) / (plan_length - 1)
    alpha_bar = jnp.exp(jnp.cumsum(jnp.log(1.0 - beta_values)))
    stride = plan_length // STEPS
    earlier = moment - stride
    alpha_now = jnp.sum(jnp.where(train_grid == moment, alpha_bar, 0.0))
    alpha_before = jnp.sum(jnp.where(train_grid == earlier, alpha_bar, 0.0)) + jnp.where(earlier < 0, 1.0, 0.0)
    return (alpha_now, alpha_before)

def predict_pair(window, modulate, w_qkv, w_out, text_kv, patch_weight, final_weight):
    col_count, channels, row_count = window.shape
    col_pairs = col_count // 2
    row_couples = row_count // 2
    model_width = patch_weight.shape[1]
    attn_width = w_out.shape[0]
    half_attn = attn_width // 2
    head_count = attn_width // HEAD_DIM
    patches = window.reshape(col_pairs, 2, channels, row_couples, 2).transpose(0, 3, 1, 2, 4)
    patches = patches.reshape(col_pairs * row_couples, 4 * channels).astype(jnp.bfloat16)
    embedded = jnp.dot(patches, patch_weight, preferred_element_type=jnp.float32) + positions(col_pairs, row_couples, model_width)
    normed = (layer_norm(embedded) * (1.0 + modulate[1]) + modulate[0]).astype(jnp.bfloat16)
    projected = jnp.dot(normed, w_qkv, preferred_element_type=jnp.float32).astype(jnp.bfloat16)
    tokens = projected.shape[0]
    queries = projected[:, :attn_width].reshape(tokens, head_count, HEAD_DIM).astype(jnp.float32)
    results = []
    for branch_index in range(2):
        keys_all = jnp.concatenate([projected[:, attn_width:2 * attn_width], text_kv[branch_index, 0]], axis=0)
        keys_all = keys_all.reshape(-1, head_count, HEAD_DIM).astype(jnp.float32)
        values_all = jnp.concatenate([projected[:, 2 * attn_width:], text_kv[branch_index, 1]], axis=0)
        values_all = values_all.reshape(-1, head_count, HEAD_DIM).astype(jnp.float32)
        scores = jnp.einsum('qhd,khd->hqk', queries, keys_all) * (1.0 / math.sqrt(HEAD_DIM))
        highest = lax.optimization_barrier(jnp.max(scores, axis=-1, keepdims=True))
        exponent = jnp.exp(scores - highest)
        soft_weights = (exponent / lax.optimization_barrier(jnp.sum(exponent, axis=-1, keepdims=True))).astype(jnp.bfloat16)
        attended = jnp.einsum('hqk,khd->qhd', soft_weights.astype(jnp.float32), values_all)
        attended = attended.reshape(tokens, attn_width).astype(jnp.bfloat16)
        part_low = jnp.dot(attended[:, :half_attn], w_out[:half_attn], preferred_element_type=jnp.float32).astype(jnp.bfloat16)
        part_high = jnp.dot(attended[:, half_attn:], w_out[half_attn:], preferred_element_type=jnp.float32).astype(jnp.bfloat16)
        part_low, part_high = lax.optimization_barrier((part_low, part_high))
        mixed_sum = part_low.astype(jnp.float32) + part_high.astype(jnp.float32)
        residual = embedded + modulate[2] * mixed_sum
        final_norm = (layer_norm(residual) * (1.0 + modulate[3])).astype(jnp.bfloat16)
        noise_tokens = jnp.dot(final_norm, final_weight, preferred_element_type=jnp.float32)
        unpacked = noise_tokens.reshape(col_pairs, row_couples, 2, channels, 2).transpose(0, 2, 3, 1, 4)
        results.append(unpacked.reshape(col_count, channels, row_count))
    return (results[0], results[1])

def reference(latent, text_kv, modulation, qkv_weight, out_weight, patch_weight, final_weight, offsets, blend_weights, step_index):
    model_width = patch_weight.shape[1]
    attn_width = out_weight.shape[0]
    w_qkv = qkv_weight.reshape(model_width, 3 * attn_width)
    moment = step_index[0]
    selected = jnp.arange(STEPS, dtype=jnp.int32) == moment * STEPS // plan_length
    modulate = lax.optimization_barrier(jnp.sum(jnp.where(selected[:, None, None], modulation, 0.0), axis=0))
    columns_all = latent.shape[0]
    span_index = jnp.arange(2 * SLAB, dtype=jnp.int32)

    def one_window(window_index):
        start_at = window_index * SLAB - offsets[window_index]
        column_list = ((start_at + span_index) % columns_all).astype(jnp.int32)
        window = jnp.take(latent, column_list, axis=0)
        conditional, unconditional = predict_pair(window, modulate, w_qkv, out_weight, text_kv, patch_weight, final_weight)
        return unconditional + guidance_scale * (conditional - unconditional)
    guided = lax.map(one_window, jnp.arange(N_WIN, dtype=jnp.int32))
    weight_values = blend_weights.astype(jnp.float32)
    window_columns = (jnp.arange(N_WIN, dtype=jnp.int32)[:, None] * SLAB - offsets[:, None] + span_index[None, :]) % columns_all
    window_columns = window_columns.reshape(-1).astype(jnp.int32)
    weighted = (weight_values[:, None, None, None] * guided).reshape(-1, CHANNELS, LAT_H)
    numerator = jnp.zeros_like(latent).at[window_columns].add(weighted)
    spread_weights = jnp.broadcast_to(weight_values[:, None], (N_WIN, 2 * SLAB)).reshape(-1)
    denominator = jnp.zeros((columns_all,), latent.dtype).at[window_columns].add(spread_weights)
    blended = numerator / denominator[:, None, None]
    alpha_now, alpha_before = plan(moment)
    previous = jnp.sqrt(alpha_before) * (latent - jnp.sqrt(1.0 - alpha_now) * blended) / jnp.sqrt(alpha_now) + jnp.sqrt(1.0 - alpha_before) * blended
    return (previous, blended)
```

```python
import functools
import math

import jax
import jax.numpy as jnp
from jax import lax
from jax.experimental import pallas as pl
from jax.experimental.pallas import tpu as pltpu
from jax.sharding import PartitionSpec as P

HEAD_DIM = 72
STEPS = 20


guidance_scale = 4.5
plan_length = 1000
norm_eps = 1e-06

VM = pl.BlockSpec(memory_space=pltpu.VMEM)
SM = pl.BlockSpec(memory_space=pltpu.SMEM)


def shift(array, axis, by):
    size = lax.axis_size(axis)
    return lax.ppermute(array, axis, [(i, (i + by) % size) for i in range(size)])


def swap(array, axis):
    return lax.ppermute(array, axis, [(0, 1), (1, 0)])


def layer_norm(values):
    average = jnp.mean(values, axis=-1, keepdims=True)
    centered = values - average
    variance = jnp.mean(centered * centered, axis=-1, keepdims=True)
    return centered * lax.rsqrt(variance + norm_eps)


def position_tables(col_pairs, row_couples, model_width):
    quarter = model_width // 4
    frequency = jnp.exp(-math.log(10000.0) * jnp.arange(quarter, dtype=jnp.float32) / quarter)
    col_pos = jnp.arange(col_pairs, dtype=jnp.float32)[:, None] * frequency[None, :]
    row_pos = jnp.arange(row_couples, dtype=jnp.float32)[:, None] * frequency[None, :]
    half = 2 * quarter
    row_part = jnp.concatenate(
        [jnp.sin(row_pos), jnp.cos(row_pos), jnp.zeros((row_couples, half), jnp.float32)], axis=1
    )
    col_part = jnp.concatenate(
        [jnp.zeros((col_pairs, half), jnp.float32), jnp.sin(col_pos), jnp.cos(col_pos)], axis=1
    )
    return row_part, col_part


def plan(moment):
    train_grid = jnp.arange(plan_length, dtype=jnp.int32)
    beta_values = 0.0001 + (0.02 - 0.0001) * train_grid.astype(jnp.float32) / (plan_length - 1)
    alpha_bar = jnp.exp(jnp.cumsum(jnp.log(1.0 - beta_values)))
    stride = plan_length // STEPS
    earlier = moment - stride
    alpha_now = jnp.sum(jnp.where(train_grid == moment, alpha_bar, 0.0))
    alpha_before = jnp.sum(jnp.where(train_grid == earlier, alpha_bar, 0.0)) + jnp.where(
        earlier < 0, 1.0, 0.0
    )
    return (alpha_now, alpha_before)


def repeat_pairs(weight, repeats):
    rows, width = weight.shape
    values = weight.astype(jnp.float32)
    even = lax.broadcasted_iota(jnp.int32, (2 * repeats, width), 0) % 2 == 0
    parts = []
    for pair in range(rows // 2):
        parts.append(
            jnp.where(even, values[2 * pair : 2 * pair + 1, :], values[2 * pair + 1 : 2 * pair + 2, :])
        )
    return jnp.concatenate(parts, axis=0).astype(jnp.bfloat16)


def attend(proj_ref, text_ref, first, count):
    heads = proj_ref.shape[0] // 3
    branches = text_ref.shape[0]
    factor = math.log2(math.e) / math.sqrt(HEAD_DIM)
    feature = (((0,), (0,)), ((), ()))
    results = [[] for _ in range(branches)]
    for head in range(heads):
        rows = slice(head * HEAD_DIM, (head + 1) * HEAD_DIM)
        queries = proj_ref[head, :, pl.ds(first, count)]
        own_scores = lax.dot_general(
            proj_ref[heads + head], queries, feature, preferred_element_type=jnp.float32
        )
        own_highest = jnp.max(own_scores, axis=0, keepdims=True)
        own_exp = jnp.exp2((own_scores - own_highest) * factor)
        own_total = jnp.sum(own_exp, axis=0, keepdims=True)
        own_mix = jnp.dot(
            proj_ref[2 * heads + head],
            own_exp.astype(jnp.bfloat16),
            preferred_element_type=jnp.float32,
        )
        for branch in range(branches):
            text_scores = lax.dot_general(
                text_ref[branch, 0, rows, :], queries, feature, preferred_element_type=jnp.float32
            )
            highest = jnp.maximum(own_highest, jnp.max(text_scores, axis=0, keepdims=True))
            text_exp = jnp.exp2((text_scores - highest) * factor)
            lowered = jnp.exp2((own_highest - highest) * factor)
            total = lowered * own_total + jnp.sum(text_exp, axis=0, keepdims=True)
            text_mix = jnp.dot(
                text_ref[branch, 1, rows, :],
                text_exp.astype(jnp.bfloat16),
                preferred_element_type=jnp.float32,
            )
            results[branch].append((lowered * own_mix + text_mix) * (1.0 / total))
    return [jnp.concatenate(parts, axis=0).astype(jnp.bfloat16) for parts in results]


def project_kernel(
    step_ref,
    side_ref,
    offset_ref,
    modulation_ref,
    before_ref,
    own_ref,
    after_ref,
    row_ref,
    col_ref,
    patch_ref,
    weight_ref,
    text_ref,
    proj_ref,
    embedded_ref,
    sent_ref,
    extended_ref,
):
    slab_cols, channels, row_count = own_ref.shape
    col_pairs, row_couples = slab_cols, row_count // 2
    tokens = col_pairs * row_couples
    own_tokens = tokens // 2
    wide = 2 * channels * row_count
    for place, source in enumerate((before_ref, own_ref, after_ref)):
        for channel in range(channels):
            extended_ref[
                place * slab_cols : (place + 1) * slab_cols,
                channel * row_count : (channel + 1) * row_count,
            ] = source[:, channel, :]
    extended = extended_ref[...].astype(jnp.bfloat16)
    start_at = slab_cols - offset_ref[0]
    chosen = lax.broadcasted_iota(jnp.int32, (2 * col_pairs, 3 * slab_cols), 0)
    column = lax.broadcasted_iota(jnp.int32, (2 * col_pairs, 3 * slab_cols), 1)
    target = jnp.where(
        chosen < col_pairs, 2 * chosen, 2 * (chosen - col_pairs) + 1
    )
    pick = jnp.where(column == target + start_at, 1.0, 0.0).astype(jnp.bfloat16)
    picked = jnp.dot(pick, extended, preferred_element_type=jnp.float32)
    picked = jnp.concatenate([picked[:col_pairs], picked[col_pairs:]], axis=1)
    lane_couple = lax.broadcasted_iota(jnp.int32, (col_pairs, wide), 1) % row_count // 2
    spread = jnp.concatenate(
        [jnp.where(lane_couple == couple, picked, 0.0) for couple in range(row_couples)], axis=0
    ).astype(jnp.bfloat16)
    patch_wide = repeat_pairs(patch_ref[...], row_couples)
    embedded = jnp.dot(spread, patch_wide, preferred_element_type=jnp.float32)
    position = jnp.concatenate(
        [row_ref[couple : couple + 1, :] + col_ref[...] for couple in range(row_couples)], axis=0
    )
    embedded = embedded + position
    side = side_ref[0]
    normed = (
        layer_norm(embedded) * (1.0 + modulation_ref[0, 1:2, :]) + modulation_ref[0, 0:1, :]
    ).astype(jnp.bfloat16)

    @pl.when(side == 0)
    def _():
        embedded_ref[...] = embedded[:own_tokens]

    @pl.when(side != 0)
    def _():
        embedded_ref[...] = embedded[own_tokens:]

    heads = proj_ref.shape[0] // 3
    for kind in range(3):
        projected = lax.dot_general(
            weight_ref[kind],
            normed,
            (((1,), (1,)), ((), ())),
            preferred_element_type=jnp.float32,
        )
        for head in range(heads):
            proj_ref[kind * heads + head] = projected[
                head * HEAD_DIM : (head + 1) * HEAD_DIM
            ].astype(jnp.bfloat16)
    first = pl.multiple_of((1 - side) * own_tokens, own_tokens)
    for branch, value in enumerate(attend(proj_ref, text_ref, first, own_tokens)):
        sent_ref[branch] = value


def attend_kernel(side_ref, proj_ref, text_ref, weight_ref, mixed_ref):
    tokens = proj_ref.shape[2]
    own_tokens = tokens // 2
    first = pl.multiple_of(side_ref[0] * own_tokens, own_tokens)
    for branch, value in enumerate(attend(proj_ref, text_ref, first, own_tokens)):
        mixed_ref[branch] = lax.dot_general(
            value, weight_ref[...], (((0,), (0,)), ((), ())), preferred_element_type=jnp.float32
        ).astype(jnp.bfloat16)


def finish_kernel(
    step_ref,
    offset_ref,
    blend_ref,
    modulation_ref,
    embedded_ref,
    mixed_ref,
    received_ref,
    weight_ref,
    final_ref,
    left_ref,
    center_ref,
    right_ref,
    buffer_ref,
):
    slab_cols = left_ref.shape[0]
    col_pairs = slab_cols
    own_tokens = embedded_ref.shape[0]
    couples = own_tokens // col_pairs
    final_wide = repeat_pairs(final_ref[...], couples)
    wide = final_wide.shape[0]
    predicted = []
    for branch in range(2):
        other = lax.dot_general(
            received_ref[branch],
            weight_ref[...],
            (((0,), (0,)), ((), ())),
            preferred_element_type=jnp.float32,
        ).astype(jnp.bfloat16)
        mixed = mixed_ref[branch].astype(jnp.float32) + other.astype(jnp.float32)
        residual = embedded_ref[...] + modulation_ref[0, 2:3, :] * mixed
        final_norm = (layer_norm(residual) * (1.0 + modulation_ref[0, 3:4, :])).astype(jnp.bfloat16)
        predicted.append(
            lax.dot_general(
                final_norm,
                final_wide,
                (((1,), (1,)), ((), ())),
                preferred_element_type=jnp.float32,
            )
        )
    conditional, unconditional = predicted
    guided = unconditional + guidance_scale * (conditional - unconditional)
    lane_couple = lax.broadcasted_iota(jnp.int32, (col_pairs, wide), 1) % (2 * couples) // 2
    pairs = jnp.zeros((col_pairs, wide), jnp.float32)
    for couple in range(couples):
        pairs = pairs + jnp.where(
            lane_couple == couple, guided[couple * col_pairs : (couple + 1) * col_pairs], 0.0
        )
    weight_value = blend_ref[0].astype(jnp.float32)
    half = wide // 2
    is_noise = lax.broadcasted_iota(jnp.int32, (col_pairs, wide), 1) < half
    even = jnp.where(is_noise, weight_value * pairs, weight_value)
    odd = jnp.where(is_noise, weight_value * pltpu.roll(pairs, half, 1), weight_value)
    start_at = slab_cols - offset_ref[0]
    buffer_ref[...] = jnp.zeros_like(buffer_ref)
    buffer_ref[pl.ds(start_at, col_pairs, stride=2), :] = even
    buffer_ref[pl.ds(start_at + 1, col_pairs, stride=2), :] = odd
    left_ref[...] = buffer_ref[:slab_cols]
    center_ref[...] = buffer_ref[slab_cols : 2 * slab_cols]
    right_ref[...] = buffer_ref[2 * slab_cols : 3 * slab_cols]


def blend_kernel(
    side_ref, plan_ref, center_ref, left_ref, right_ref, latent_ref, previous_ref, noise_ref
):
    channels, half_rows = noise_ref.shape[1:]
    total = center_ref[...] + left_ref[...] + right_ref[...]
    blended = total / pltpu.roll(total, total.shape[1] // 2, 1)
    first = side_ref[0] == 0
    for channel in range(channels):
        noise = blended[:, channel * half_rows : (channel + 1) * half_rows]
        rows = latent_ref[:, channel, :]
        rows = jnp.where(first, rows[:, :half_rows], rows[:, half_rows:])
        noise_ref[:, channel, :] = noise
        previous_ref[:, channel, :] = (
            plan_ref[0] * (rows - plan_ref[1] * noise) / plan_ref[2] + plan_ref[3] * noise
        )


def on_device(
    latent,
    text_kv,
    modulation,
    qkv_weight,
    out_weight,
    patch_weight,
    final_weight,
    offsets,
    blend_weights,
    step_index,
):
    slab_cols, channels, row_count = latent.shape
    model_width = patch_weight.shape[1]
    half_attn = out_weight.shape[0]
    heads = half_attn // HEAD_DIM
    branches = text_kv.shape[0]
    col_pairs, row_couples = slab_cols, row_count // 2
    tokens = col_pairs * row_couples
    own_tokens = tokens // 2
    half_rows = row_count // 2
    side = lax.axis_index("cfg").astype(jnp.int32).reshape(1)

    before = shift(latent, "win", 1)
    after = shift(latent, "win", -1)
    other_weight = swap(out_weight, "cfg")

    row_part, col_part = position_tables(col_pairs, row_couples, model_width)
    weight = jnp.transpose(qkv_weight, (1, 2, 0))
    text = jnp.transpose(text_kv, (0, 1, 3, 2))
    final = jnp.transpose(final_weight, (1, 0))
    moment = step_index[0]
    alpha_now, alpha_before = plan(moment)
    plan_values = jnp.stack(
        [
            jnp.sqrt(alpha_before),
            jnp.sqrt(1.0 - alpha_now),
            jnp.sqrt(alpha_now),
            jnp.sqrt(1.0 - alpha_before),
        ]
    )

    modulation_spec = pl.BlockSpec(
        (1, 4, model_width), lambda i, step: (step[0] * STEPS // plan_length, 0, 0)
    )
    bf16, f32 = jnp.bfloat16, jnp.float32
    shape = jax.ShapeDtypeStruct
    projected, embedded, sent = pl.pallas_call(
        project_kernel,
        out_shape=(
            shape((3 * heads, HEAD_DIM, tokens), bf16),
            shape((own_tokens, model_width), f32),
            shape((branches, half_attn, own_tokens), bf16),
        ),
        grid_spec=pltpu.PrefetchScalarGridSpec(
            num_scalar_prefetch=1,
            grid=(1,),
            in_specs=[SM, SM, modulation_spec] + [VM] * 8,
            out_specs=(VM, VM, VM),
            scratch_shapes=[pltpu.VMEM((3 * slab_cols, channels * row_count), f32)],
        ),
        name="project",
        cost_estimate=pl.CostEstimate(flops=2 * 10**9, bytes_accessed=8 * 10**6, transcendentals=10**6),
    )(
        step_index, side, offsets, modulation, before, latent, after,
        row_part, col_part, patch_weight, weight, text,
    )
    received = swap(sent, "cfg")
    mixed = pl.pallas_call(
        attend_kernel,
        out_shape=shape((branches, own_tokens, model_width), bf16),
        in_specs=[SM] + [VM] * 3,
        out_specs=VM,
        name="attend",
        cost_estimate=pl.CostEstimate(flops=10**9, bytes_accessed=8 * 10**6, transcendentals=10**6),
    )(side, projected, text, out_weight)
    left, center, right = pl.pallas_call(
        finish_kernel,
        out_shape=tuple(shape((slab_cols, 2 * channels * half_rows), f32) for _ in range(3)),
        grid_spec=pltpu.PrefetchScalarGridSpec(
            num_scalar_prefetch=1,
            grid=(1,),
            in_specs=[SM, SM, modulation_spec] + [VM] * 5,
            out_specs=(VM, VM, VM),
            scratch_shapes=[pltpu.VMEM((3 * slab_cols + 8, 2 * channels * half_rows), f32)],
        ),
        name="finish",
        cost_estimate=pl.CostEstimate(flops=10**9, bytes_accessed=4 * 10**6, transcendentals=10**3),
    )(
        step_index, offsets, blend_weights, modulation, embedded, mixed, received,
        other_weight, final,
    )
    from_left = shift(right, "win", 1)
    from_right = shift(left, "win", -1)
    previous, noise = pl.pallas_call(
        blend_kernel,
        out_shape=tuple(shape((slab_cols, channels, half_rows), f32) for _ in range(2)),
        in_specs=[SM, SM] + [VM] * 4,
        out_specs=(VM, VM),
        name="blend",
    )(side, plan_values, center, from_left, from_right, latent)
    return (previous, noise)


def solution(mesh):
    in_specs = (
        P("win", None, None),
        P(None, None, None, "cfg"),
        P(),
        P(None, None, "cfg"),
        P("cfg", None),
        P(),
        P(),
        P("win"),
        P("win"),
        P(),
    )
    out_specs = (P("win", None, "cfg"), P("win", None, "cfg"))
    return jax.shard_map(
        on_device, mesh=mesh, in_specs=in_specs, out_specs=out_specs, check_vma=False
    )
```

```python
import math

import jax
import jax.numpy as jnp
from jax import lax
from jax.experimental import pallas as pl
from jax.experimental.pallas import tpu as pltpu
from jax.sharding import PartitionSpec as P


HEAD_DIM = 72
STEPS = 20


guidance_scale = 4.5
plan_length = 1000
norm_eps = 1e-06

VM = pl.BlockSpec(memory_space=pltpu.VMEM)
SM = pl.BlockSpec(memory_space=pltpu.SMEM)
GRANT = 24 * 2**20


def swap_ring(array, axis, odd):
    size = lax.axis_size(axis)
    pairs = []
    for left in range(odd, size, 2):
        right = (left + 1) % size
        pairs += [(left, right), (right, left)]
    return lax.ppermute(array, axis, pairs)


def swap(array, axis):
    return lax.ppermute(array, axis, [(0, 1), (1, 0)])


def layer_norm(values):
    average = jnp.mean(values, axis=-1, keepdims=True)
    centered = values - average
    variance = jnp.mean(centered * centered, axis=-1, keepdims=True)
    return centered * lax.rsqrt(variance + norm_eps)


def repeat_pairs(weight, repeats):
    rows, width = weight.shape
    values = weight.astype(jnp.float32)
    even = lax.broadcasted_iota(jnp.int32, (2 * repeats, width), 0) % 2 == 0
    parts = []
    for pair in range(rows // 2):
        parts.append(
            jnp.where(even, values[2 * pair : 2 * pair + 1, :], values[2 * pair + 1 : 2 * pair + 2, :])
        )
    return jnp.concatenate(parts, axis=0).astype(jnp.bfloat16)


def prepare_kernel(
    step_ref,
    blend_ref,
    latent_source,
    patch_source,
    modulation_ref,
    weight_ref,
    text_ref,
    out_ref,
    final_ref,
    position_ref,
    patch_wide_ref,
    plan_ref,
    rows_ref,
    modulate_copy,
    weight_copy,
    text_copy,
    out_copy,
    final_copy,
    latent_ref,
    patch_ref,
    semaphores,
):
    row = step_ref[0] * STEPS // plan_length
    copies = [
        pltpu.make_async_copy(source, target, semaphores.at[place])
        for place, (source, target) in enumerate(
            (
                (latent_source, latent_ref),
                (patch_source, patch_ref),
                (modulation_ref.at[row], modulate_copy),
                (weight_ref, weight_copy),
                (text_ref, text_copy),
                (out_ref, out_copy),
                (final_ref, final_copy),
            )
        )
    ]
    for copy in copies:
        copy.start()
    _, model_width = position_ref.shape
    slab_cols, channels, row_count = latent_ref.shape
    row_couples = row_count // 2
    quarter = model_width // 4

    def table(count, first):
        lane = lax.broadcasted_iota(jnp.int32, (count, model_width), 1)
        place = lax.broadcasted_iota(jnp.int32, (count, model_width), 0).astype(jnp.float32)
        frequency = jnp.exp(-math.log(10000.0) * (lane % quarter).astype(jnp.float32) / quarter)
        angle = place * frequency
        values = jnp.where(lane // quarter % 2 == 0, jnp.sin(angle), jnp.cos(angle))
        return jnp.where(lane // (2 * quarter) == first, values, 0.0)

    plan_ref[4:5, :] = jnp.full((1, plan_ref.shape[1]), blend_ref[0].astype(jnp.float32))
    row_part = table(row_couples, 0)
    col_part = table(slab_cols, 1)
    for couple in range(row_couples):
        position_ref[couple * slab_cols : (couple + 1) * slab_cols, :] = (
            row_part[couple : couple + 1, :] + col_part
        )
    copies[1].wait()
    patch_wide_ref[...] = repeat_pairs(patch_ref[...], row_couples)

    moment = step_ref[0]
    index = lax.broadcasted_iota(jnp.int32, (8, 128), 0) * 128 + lax.broadcasted_iota(
        jnp.int32, (8, 128), 1
    )
    train = jnp.minimum(index, plan_length - 1).astype(jnp.float32)
    beta_values = 0.0001 + (0.02 - 0.0001) * train / (plan_length - 1)
    logs = jnp.log(1.0 - beta_values)

    def alpha_bar(last):
        kept = jnp.where((index <= last) & (index < plan_length), logs, 0.0)
        kept = jnp.sum(jnp.sum(kept, axis=0, keepdims=True), axis=1, keepdims=True)
        return jnp.exp(kept)

    alpha_now = alpha_bar(moment)
    alpha_before = alpha_bar(moment - plan_length // STEPS)
    for place, value in enumerate(
        (
            jnp.sqrt(alpha_before),
            jnp.sqrt(1.0 - alpha_now),
            jnp.sqrt(alpha_now),
            jnp.sqrt(1.0 - alpha_before),
        )
    ):
        plan_ref[place : place + 1, :] = jnp.broadcast_to(value, (1, plan_ref.shape[1]))

    half_rows = row_count // 2
    side = lax.axis_index("cfg")
    copies[0].wait()
    for channel in range(channels):
        turned = jnp.transpose(latent_ref[:, channel, :], (1, 0))
        rows_ref[channel * half_rows : (channel + 1) * half_rows, :] = jnp.where(
            side == 0, turned[:half_rows], turned[half_rows:]
        )
    for copy in copies[2:]:
        copy.wait()


def attend(proj_ref, text_ref, first, count):
    heads = proj_ref.shape[0] // 3
    branches = text_ref.shape[0]
    factor = math.log2(math.e) / math.sqrt(HEAD_DIM)
    feature = (((0,), (0,)), ((), ()))
    results = [[] for _ in range(branches)]
    for head in range(heads):
        rows = slice(head * HEAD_DIM, (head + 1) * HEAD_DIM)
        queries = proj_ref[head, :, pl.ds(first, count)]
        own_scores = lax.dot_general(
            proj_ref[heads + head], queries, feature, preferred_element_type=jnp.float32
        )
        own_highest = jnp.max(own_scores, axis=0, keepdims=True)
        own_exp = jnp.exp2((own_scores - own_highest) * factor)
        own_total = jnp.sum(own_exp, axis=0, keepdims=True)
        own_mix = jnp.dot(
            proj_ref[2 * heads + head],
            own_exp.astype(jnp.bfloat16),
            preferred_element_type=jnp.float32,
        )
        for branch in range(branches):
            text_scores = lax.dot_general(
                text_ref[branch, 0, rows, :], queries, feature, preferred_element_type=jnp.float32
            )
            highest = jnp.maximum(own_highest, jnp.max(text_scores, axis=0, keepdims=True))
            text_exp = jnp.exp2((text_scores - highest) * factor)
            lowered = jnp.exp2((own_highest - highest) * factor)
            total = lowered * own_total + jnp.sum(text_exp, axis=0, keepdims=True)
            text_mix = jnp.dot(
                text_ref[branch, 1, rows, :],
                text_exp.astype(jnp.bfloat16),
                preferred_element_type=jnp.float32,
            )
            results[branch].append((lowered * own_mix + text_mix) * (1.0 / total))
    return [jnp.concatenate(parts, axis=0).astype(jnp.bfloat16) for parts in results]


def project_kernel(
    offset_ref,
    modulation_ref,
    near_ref,
    own_ref,
    far_ref,
    position_ref,
    patch_ref,
    weight_ref,
    text_ref,
    proj_ref,
    embedded_ref,
    sent_ref,
    extended_ref,
):
    slab_cols, channels, row_count = own_ref.shape
    col_pairs, row_couples = slab_cols, row_count // 2
    tokens = col_pairs * row_couples
    own_tokens = tokens // 2
    wide = 2 * channels * row_count
    even = lax.axis_index("win") % 2 == 0
    for channel in range(channels):
        near, far = near_ref[:, channel, :], far_ref[:, channel, :]
        values = (jnp.where(even, far, near), own_ref[:, channel, :], jnp.where(even, near, far))
        for place, value in enumerate(values):
            extended_ref[
                place * slab_cols : (place + 1) * slab_cols,
                channel * row_count : (channel + 1) * row_count,
            ] = value
    extended = extended_ref[...].astype(jnp.bfloat16)
    start_at = slab_cols - offset_ref[0]
    chosen = lax.broadcasted_iota(jnp.int32, (2 * col_pairs, 3 * slab_cols), 0)
    column = lax.broadcasted_iota(jnp.int32, (2 * col_pairs, 3 * slab_cols), 1)
    target = jnp.where(
        chosen < col_pairs, 2 * chosen, 2 * (chosen - col_pairs) + 1
    )
    pick = jnp.where(column == target + start_at, 1.0, 0.0).astype(jnp.bfloat16)
    picked = jnp.dot(pick, extended, preferred_element_type=jnp.float32)
    picked = jnp.concatenate([picked[:col_pairs], picked[col_pairs:]], axis=1)
    lane_couple = lax.broadcasted_iota(jnp.int32, (col_pairs, wide), 1) % row_count // 2
    spread = jnp.concatenate(
        [jnp.where(lane_couple == couple, picked, 0.0) for couple in range(row_couples)], axis=0
    ).astype(jnp.bfloat16)
    embedded = jnp.dot(spread, patch_ref[...], preferred_element_type=jnp.float32)
    embedded = embedded + position_ref[...]
    side = lax.axis_index("cfg")
    normed = (
        layer_norm(embedded) * (1.0 + modulation_ref[1:2, :]) + modulation_ref[0:1, :]
    ).astype(jnp.bfloat16)

    @pl.when(side == 0)
    def _():
        embedded_ref[...] = embedded[:own_tokens]

    @pl.when(side != 0)
    def _():
        embedded_ref[...] = embedded[own_tokens:]

    heads = proj_ref.shape[0] // 3
    for kind in range(3):
        projected = lax.dot_general(
            weight_ref[kind],
            normed,
            (((1,), (1,)), ((), ())),
            preferred_element_type=jnp.float32,
        )
        for head in range(heads):
            proj_ref[kind * heads + head] = projected[
                head * HEAD_DIM : (head + 1) * HEAD_DIM
            ].astype(jnp.bfloat16)
    first = pl.multiple_of((1 - side) * own_tokens, own_tokens)
    for branch, value in enumerate(attend(proj_ref, text_ref, first, own_tokens)):
        sent_ref[branch] = value


def attend_kernel(proj_ref, text_ref, weight_ref, mixed_ref):
    tokens = proj_ref.shape[2]
    own_tokens = tokens // 2
    first = pl.multiple_of(lax.axis_index("cfg") * own_tokens, own_tokens)
    for branch, value in enumerate(attend(proj_ref, text_ref, first, own_tokens)):
        mixed_ref[branch] = lax.dot_general(
            value, weight_ref[...], (((0,), (0,)), ((), ())), preferred_element_type=jnp.float32
        ).astype(jnp.bfloat16)


def finish_kernel(
    offset_ref,
    plan_ref,
    modulation_ref,
    embedded_ref,
    mixed_ref,
    received_ref,
    weight_ref,
    final_ref,
    near_ref,
    center_ref,
    far_ref,
    buffer_ref,
):
    slab_cols = center_ref.shape[0]
    col_pairs = slab_cols
    own_tokens = embedded_ref.shape[0]
    couples = own_tokens // col_pairs
    final_wide = repeat_pairs(final_ref[...], couples)
    wide = final_wide.shape[0]
    predicted = []
    for branch in range(2):
        other = lax.dot_general(
            received_ref[branch],
            weight_ref[...],
            (((0,), (0,)), ((), ())),
            preferred_element_type=jnp.float32,
        ).astype(jnp.bfloat16)
        mixed = mixed_ref[branch].astype(jnp.float32) + other.astype(jnp.float32)
        residual = embedded_ref[...] + modulation_ref[2:3, :] * mixed
        final_norm = (layer_norm(residual) * (1.0 + modulation_ref[3:4, :])).astype(jnp.bfloat16)
        predicted.append(
            lax.dot_general(
                final_norm,
                final_wide,
                (((1,), (1,)), ((), ())),
                preferred_element_type=jnp.float32,
            )
        )
    conditional, unconditional = predicted
    guided = unconditional + guidance_scale * (conditional - unconditional)
    lane_couple = lax.broadcasted_iota(jnp.int32, (col_pairs, wide), 1) % (2 * couples) // 2
    pairs = jnp.zeros((col_pairs, wide), jnp.float32)
    for couple in range(couples):
        pairs = pairs + jnp.where(
            lane_couple == couple, guided[couple * col_pairs : (couple + 1) * col_pairs], 0.0
        )
    weight_value = plan_ref[4:5, :wide]
    half = wide // 2
    is_noise = lax.broadcasted_iota(jnp.int32, (col_pairs, wide), 1) < half
    even = jnp.where(is_noise, weight_value * pairs, weight_value)
    odd = jnp.where(is_noise, weight_value * pltpu.roll(pairs, half, 1), weight_value)
    start_at = slab_cols - offset_ref[0]
    buffer_ref[...] = jnp.zeros_like(buffer_ref)
    buffer_ref[pl.ds(start_at, col_pairs, stride=2), :] = even
    buffer_ref[pl.ds(start_at + 1, col_pairs, stride=2), :] = odd
    center_ref[...] = buffer_ref[slab_cols : 2 * slab_cols]
    even_place = lax.axis_index("win") % 2 == 0
    left, right = buffer_ref[:slab_cols], buffer_ref[2 * slab_cols : 3 * slab_cols]
    near_ref[...] = jnp.where(even_place, right, left)
    far_ref[...] = jnp.where(even_place, left, right)


def blend_kernel(plan_ref, center_ref, near_ref, far_ref, rows_ref, previous_ref, noise_ref):
    channels, half_rows, slab_cols = noise_ref.shape
    total = jnp.transpose(center_ref[...] + near_ref[...] + far_ref[...], (1, 0))
    half = total.shape[0] // 2
    noise = total[:half] / total[half:]
    scale = plan_ref[:, :slab_cols]
    previous = (
        scale[0:1] * (rows_ref[...] - scale[1:2] * noise) / scale[2:3] + scale[3:4] * noise
    )
    for channel in range(channels):
        rows = slice(channel * half_rows, (channel + 1) * half_rows)
        noise_ref[channel] = noise[rows]
        previous_ref[channel] = previous[rows]


def on_device(
    latent,
    text_kv,
    modulation,
    qkv_weight,
    out_weight,
    patch_weight,
    final_weight,
    offsets,
    blend_weights,
    step_index,
):
    slab_cols, channels, row_count = latent.shape
    model_width = patch_weight.shape[1]
    half_attn = out_weight.shape[0]
    heads = half_attn // HEAD_DIM
    branches = text_kv.shape[0]
    col_pairs, row_couples = slab_cols, row_count // 2
    tokens = col_pairs * row_couples
    own_tokens = tokens // 2
    half_rows = row_count // 2
    far = swap_ring(latent, "win", 1)
    near = swap_ring(latent, "win", 0)
    other_weight = swap(out_weight, "cfg")

    weight = jnp.transpose(qkv_weight, (1, 2, 0))
    text = jnp.transpose(text_kv, (0, 1, 3, 2))
    final = jnp.transpose(final_weight, (1, 0))

    bf16, f32 = jnp.bfloat16, jnp.float32
    shape = jax.ShapeDtypeStruct
    wide = 2 * channels * half_rows
    position, patch_wide, plan_values, rows, modulate, weight, text, out_own, final, own = pl.pallas_call(
        prepare_kernel,
        out_shape=(
            shape((tokens, model_width), f32),
            shape((2 * channels * row_count, model_width), bf16),
            shape((8, max(wide, slab_cols)), f32),
            shape((channels * half_rows, slab_cols), f32),
            shape(modulation.shape[1:], f32),
            shape(weight.shape, bf16),
            shape(text.shape, bf16),
            shape(out_weight.shape, bf16),
            shape(final.shape, bf16),
            shape(latent.shape, f32),
        ),
        in_specs=[SM, SM] + [pl.BlockSpec(memory_space=pltpu.HBM)] * 7,
        out_specs=(VM,) * 10,
        scratch_shapes=[
            pltpu.VMEM(patch_weight.shape, bf16),
            pltpu.SemaphoreType.DMA((7,)),
        ],
        name="prepare",
        compiler_params=pltpu.CompilerParams(vmem_limit_bytes=GRANT),
        cost_estimate=pl.CostEstimate(flops=10**7, bytes_accessed=10**6, transcendentals=10**5),
    )(
        step_index,
        blend_weights,
        *(
            pltpu.with_memory_space_constraint(array, pltpu.HBM)
            for array in (latent, patch_weight, modulation, weight, text, out_weight, final)
        ),
    )
    projected, embedded, sent = pl.pallas_call(
        project_kernel,
        out_shape=(
            shape((3 * heads, HEAD_DIM, tokens), bf16),
            shape((own_tokens, model_width), f32),
            shape((branches, half_attn, own_tokens), bf16),
        ),
        in_specs=[SM] + [VM] * 8,
        out_specs=(VM, VM, VM),
        scratch_shapes=[pltpu.VMEM((3 * slab_cols, channels * row_count), f32)],
        name="project",
        compiler_params=pltpu.CompilerParams(vmem_limit_bytes=GRANT),
        cost_estimate=pl.CostEstimate(flops=2 * 10**9, bytes_accessed=8 * 10**6, transcendentals=10**6),
    )(offsets, modulate, near, own, far, position, patch_wide, weight, text)
    received = swap(sent, "cfg")
    mixed = pl.pallas_call(
        attend_kernel,
        out_shape=shape((branches, own_tokens, model_width), bf16),
        in_specs=[VM] * 3,
        out_specs=VM,
        name="attend",
        compiler_params=pltpu.CompilerParams(vmem_limit_bytes=GRANT),
        cost_estimate=pl.CostEstimate(flops=10**9, bytes_accessed=8 * 10**6, transcendentals=10**6),
    )(projected, text, out_own)
    to_near, center, to_far = pl.pallas_call(
        finish_kernel,
        out_shape=tuple(shape((slab_cols, wide), f32) for _ in range(3)),
        in_specs=[SM] + [VM] * 7,
        out_specs=(VM, VM, VM),
        scratch_shapes=[pltpu.VMEM((3 * slab_cols + 8, wide), f32)],
        name="finish",
        compiler_params=pltpu.CompilerParams(vmem_limit_bytes=GRANT),
        cost_estimate=pl.CostEstimate(flops=10**9, bytes_accessed=4 * 10**6, transcendentals=10**3),
    )(
        offsets, plan_values, modulate, embedded, mixed, received,
        other_weight, final,
    )
    from_far = swap_ring(to_far, "win", 1)
    from_near = swap_ring(to_near, "win", 0)
    previous, noise = pl.pallas_call(
        blend_kernel,
        out_shape=tuple(shape((channels, half_rows, slab_cols), f32) for _ in range(2)),
        in_specs=[VM] * 5,
        out_specs=(VM, VM),
        name="blend",
        compiler_params=pltpu.CompilerParams(vmem_limit_bytes=GRANT),
    )(plan_values, center, from_near, from_far, rows)
    return (jnp.transpose(previous, (2, 0, 1)), jnp.transpose(noise, (2, 0, 1)))


def solution(mesh):
    in_specs = (
        P("win", None, None),
        P(None, None, None, "cfg"),
        P(),
        P(None, None, "cfg"),
        P("cfg", None),
        P(),
        P(),
        P("win"),
        P("win"),
        P(),
    )
    out_specs = (P("win", None, "cfg"), P("win", None, "cfg"))
    return jax.shard_map(
        on_device, mesh=mesh, in_specs=in_specs, out_specs=out_specs, check_vma=False
    )
```

```python
import functools
import math

import jax
import jax.numpy as jnp
from jax import lax
from jax.experimental import pallas as pl
from jax.experimental.pallas import tpu as pltpu
from jax.sharding import PartitionSpec as P


HEAD_DIM = 72
STEPS = 20


guidance_scale = 4.5
plan_length = 1000
norm_eps = 1e-06

VM = pl.BlockSpec(memory_space=pltpu.VMEM)
SM = pl.BlockSpec(memory_space=pltpu.SMEM)
GRANT = 24 * 2**20


def swap_ring(array, axis, odd):
    size = lax.axis_size(axis)
    pairs = []
    for left in range(odd, size, 2):
        right = (left + 1) % size
        pairs += [(left, right), (right, left)]
    return lax.ppermute(array, axis, pairs)


def swap(array, axis):
    return lax.ppermute(array, axis, [(0, 1), (1, 0)])


def layer_norm(values):
    average = jnp.mean(values, axis=-1, keepdims=True)
    centered = values - average
    variance = jnp.mean(centered * centered, axis=-1, keepdims=True)
    return centered * lax.rsqrt(variance + norm_eps)


def repeat_pairs(weight, repeats):
    rows, width = weight.shape
    values = weight.astype(jnp.float32)
    even = lax.broadcasted_iota(jnp.int32, (2 * repeats, width), 0) % 2 == 0
    parts = []
    for pair in range(rows // 2):
        parts.append(
            jnp.where(even, values[2 * pair : 2 * pair + 1, :], values[2 * pair + 1 : 2 * pair + 2, :])
        )
    return jnp.concatenate(parts, axis=0).astype(jnp.bfloat16)


def cut_kernel(weight_ref, part_ref, semaphore):
    count = part_ref.shape[0]
    first = pl.multiple_of(lax.axis_index("win") % 2 * count, count)
    copy = pltpu.make_async_copy(weight_ref.at[pl.ds(first, count)], part_ref, semaphore)
    copy.start()
    copy.wait()


def prepare_kernel(
    step_ref,
    latent_source,
    patch_source,
    modulation_ref,
    weight_ref,
    text_ref,
    out_ref,
    final_ref,
    position_ref,
    patch_wide_ref,
    plan_ref,
    rows_ref,
    modulate_copy,
    weight_copy,
    text_copy,
    out_copy,
    final_copy,
    latent_ref,
    patch_ref,
    semaphores,
):
    row = step_ref[0] * STEPS // plan_length
    copies = [
        pltpu.make_async_copy(source, target, semaphores.at[place])
        for place, (source, target) in enumerate(
            (
                (latent_source, latent_ref),
                (patch_source, patch_ref),
                (modulation_ref.at[row], modulate_copy),
                (weight_ref, weight_copy),
                (text_ref, text_copy),
                (out_ref, out_copy),
                (final_ref, final_copy),
            )
        )
    ]
    for copy in copies:
        copy.start()
    _, model_width = position_ref.shape
    slab_cols, channels, row_count = latent_ref.shape
    row_couples = row_count // 2
    quarter = model_width // 4

    half = 2 * quarter

    def table(count, first, lanes):
        lane = first + lax.broadcasted_iota(jnp.int32, (count, lanes), 1)
        place = lax.broadcasted_iota(jnp.int32, (count, lanes), 0).astype(jnp.float32)
        frequency = jnp.exp(-math.log(10000.0) * (lane % quarter).astype(jnp.float32) / quarter)
        phase = jnp.where(lane // quarter % 2 == 0, 0.0, 0.5 * math.pi)
        return jnp.sin(place * frequency + phase)

    below, above = half // 128 * 128, -(-half // 128) * 128
    row_part = table(row_couples, 0, above)
    col_part = table(slab_cols, below, model_width - below)
    lane = below + lax.broadcasted_iota(jnp.int32, (slab_cols, above - below), 1)
    for couple in range(row_couples):
        rows = slice(couple * slab_cols, (couple + 1) * slab_cols)
        line = jnp.broadcast_to(row_part[couple : couple + 1, :], (slab_cols, above))
        position_ref[rows, :below] = line[:, :below]
        position_ref[rows, below:above] = jnp.where(
            lane < half, line[:, below:], col_part[:, : above - below]
        )
        position_ref[rows, above:] = col_part[:, above - below :]
    copies[1].wait()
    patch_wide_ref[...] = repeat_pairs(patch_ref[...], row_couples)

    moment = step_ref[0]
    index = lax.broadcasted_iota(jnp.int32, (8, 128), 0) * 128 + lax.broadcasted_iota(
        jnp.int32, (8, 128), 1
    )
    train = jnp.minimum(index, plan_length - 1).astype(jnp.float32)
    beta_values = 0.0001 + (0.02 - 0.0001) * train / (plan_length - 1)
    logs = jnp.log(1.0 - beta_values)

    def alpha_bar(last):
        kept = jnp.where((index <= last) & (index < plan_length), logs, 0.0)
        kept = jnp.sum(jnp.sum(kept, axis=0, keepdims=True), axis=1, keepdims=True)
        return jnp.exp(kept)

    alpha_now = alpha_bar(moment)
    alpha_before = alpha_bar(moment - plan_length // STEPS)
    for place, value in enumerate(
        (
            jnp.sqrt(alpha_before),
            jnp.sqrt(1.0 - alpha_now),
            jnp.sqrt(alpha_now),
            jnp.sqrt(1.0 - alpha_before),
        )
    ):
        plan_ref[place : place + 1, :] = jnp.broadcast_to(value, (1, plan_ref.shape[1]))

    half_rows = row_count // 2
    side = lax.axis_index("cfg")
    copies[0].wait()
    for channel in range(channels):
        turned = jnp.transpose(latent_ref[:, channel, :], (1, 0))
        rows_ref[channel * half_rows : (channel + 1) * half_rows, :] = jnp.where(
            side == 0, turned[:half_rows], turned[half_rows:]
        )
    for copy in copies[2:]:
        copy.wait()


def attend(proj_ref, text_ref, first, count):
    heads = proj_ref.shape[0] // 3
    branches = text_ref.shape[0]
    factor = math.log2(math.e) / math.sqrt(HEAD_DIM)
    feature = (((0,), (0,)), ((), ()))
    results = [[] for _ in range(branches)]
    for head in range(heads):
        rows = slice(head * HEAD_DIM, (head + 1) * HEAD_DIM)
        queries = proj_ref[head, :, pl.ds(first, count)]
        own_scores = lax.dot_general(
            proj_ref[heads + head], queries, feature, preferred_element_type=jnp.float32
        )
        own_highest = jnp.max(own_scores, axis=0, keepdims=True)
        own_exp = jnp.exp2((own_scores - own_highest) * factor)
        own_total = jnp.sum(own_exp, axis=0, keepdims=True)
        own_mix = jnp.dot(
            proj_ref[2 * heads + head],
            own_exp.astype(jnp.bfloat16),
            preferred_element_type=jnp.float32,
        )
        for branch in range(branches):
            text_scores = lax.dot_general(
                text_ref[branch, 0, rows, :], queries, feature, preferred_element_type=jnp.float32
            )
            highest = jnp.maximum(own_highest, jnp.max(text_scores, axis=0, keepdims=True))
            text_exp = jnp.exp2((text_scores - highest) * factor)
            lowered = jnp.exp2((own_highest - highest) * factor)
            total = lowered * own_total + jnp.sum(text_exp, axis=0, keepdims=True)
            text_mix = jnp.dot(
                text_ref[branch, 1, rows, :],
                text_exp.astype(jnp.bfloat16),
                preferred_element_type=jnp.float32,
            )
            results[branch].append((lowered * own_mix + text_mix) * (1.0 / total))
    return [jnp.concatenate(parts, axis=0).astype(jnp.bfloat16) for parts in results]


def project_kernel(
    offset_ref,
    modulation_ref,
    near_ref,
    own_ref,
    far_ref,
    position_ref,
    patch_ref,
    weight_ref,
    text_ref,
    proj_ref,
    embedded_ref,
    sent_ref,
    extended_ref,
):
    slab_cols, channels, row_count = own_ref.shape
    col_pairs, row_couples = slab_cols, row_count // 2
    tokens = col_pairs * row_couples
    own_tokens = tokens // 2
    wide = 2 * channels * row_count
    even = lax.axis_index("win") % 2 == 0
    for channel in range(channels):
        near, far = near_ref[:, channel, :], far_ref[:, channel, :]
        values = (jnp.where(even, far, near), own_ref[:, channel, :], jnp.where(even, near, far))
        for place, value in enumerate(values):
            extended_ref[
                place * slab_cols : (place + 1) * slab_cols,
                channel * row_count : (channel + 1) * row_count,
            ] = value
    extended = extended_ref[...].astype(jnp.bfloat16)
    start_at = slab_cols - offset_ref[0]
    chosen = lax.broadcasted_iota(jnp.int32, (2 * col_pairs, 3 * slab_cols), 0)
    column = lax.broadcasted_iota(jnp.int32, (2 * col_pairs, 3 * slab_cols), 1)
    target = jnp.where(
        chosen < col_pairs, 2 * chosen, 2 * (chosen - col_pairs) + 1
    )
    pick = jnp.where(column == target + start_at, 1.0, 0.0).astype(jnp.bfloat16)
    picked = jnp.dot(pick, extended, preferred_element_type=jnp.float32)
    picked = jnp.concatenate([picked[:col_pairs], picked[col_pairs:]], axis=1)
    lane_couple = lax.broadcasted_iota(jnp.int32, (col_pairs, wide), 1) % row_count // 2
    spread = jnp.concatenate(
        [jnp.where(lane_couple == couple, picked, 0.0) for couple in range(row_couples)], axis=0
    ).astype(jnp.bfloat16)
    embedded = jnp.dot(spread, patch_ref[...], preferred_element_type=jnp.float32)
    embedded = embedded + position_ref[...]
    side = lax.axis_index("cfg")
    normed = (
        layer_norm(embedded) * (1.0 + modulation_ref[1:2, :]) + modulation_ref[0:1, :]
    ).astype(jnp.bfloat16)

    @pl.when(side == 0)
    def _():
        embedded_ref[...] = embedded[:own_tokens]

    @pl.when(side != 0)
    def _():
        embedded_ref[...] = embedded[own_tokens:]

    heads = proj_ref.shape[0] // 3
    for kind in range(3):
        projected = lax.dot_general(
            weight_ref[kind],
            normed,
            (((1,), (1,)), ((), ())),
            preferred_element_type=jnp.float32,
        )
        for head in range(heads):
            proj_ref[kind * heads + head] = projected[
                head * HEAD_DIM : (head + 1) * HEAD_DIM
            ].astype(jnp.bfloat16)
    first = pl.multiple_of((1 - side) * own_tokens, own_tokens)
    for branch, value in enumerate(attend(proj_ref, text_ref, first, own_tokens)):
        sent_ref[branch] = value


def attend_kernel(proj_ref, text_ref, weight_ref, mixed_ref):
    tokens = proj_ref.shape[2]
    own_tokens = tokens // 2
    first = pl.multiple_of(lax.axis_index("cfg") * own_tokens, own_tokens)
    for branch, value in enumerate(attend(proj_ref, text_ref, first, own_tokens)):
        mixed_ref[branch] = lax.dot_general(
            value, weight_ref[...], (((0,), (0,)), ((), ())), preferred_element_type=jnp.float32
        ).astype(jnp.bfloat16)


def finish_kernel(
    offset_ref,
    blend_ref,
    modulation_ref,
    embedded_ref,
    mixed_ref,
    received_ref,
    weight_ref,
    neighbour_ref,
    final_ref,
    near_ref,
    center_ref,
    far_ref,
    buffer_ref,
):
    count = weight_ref.shape[0]
    parity = lax.axis_index("win") % 2
    mine = pl.multiple_of(parity * count, count)
    theirs = pl.multiple_of((1 - parity) * count, count)
    feature = (((0,), (0,)), ((), ()))
    slab_cols = center_ref.shape[0]
    col_pairs = slab_cols
    own_tokens = embedded_ref.shape[0]
    couples = own_tokens // col_pairs
    final_wide = repeat_pairs(final_ref[...], couples)
    wide = final_wide.shape[0]
    predicted = []
    for branch in range(2):
        other = lax.dot_general(
            received_ref[branch, pl.ds(mine, count), :],
            weight_ref[...],
            feature,
            preferred_element_type=jnp.float32,
        ) + lax.dot_general(
            received_ref[branch, pl.ds(theirs, count), :],
            neighbour_ref[...],
            feature,
            preferred_element_type=jnp.float32,
        )
        mixed = mixed_ref[branch].astype(jnp.float32) + other
        residual = embedded_ref[...] + modulation_ref[2:3, :] * mixed
        final_norm = (layer_norm(residual) * (1.0 + modulation_ref[3:4, :])).astype(jnp.bfloat16)
        predicted.append(
            lax.dot_general(
                final_norm,
                final_wide,
                (((1,), (1,)), ((), ())),
                preferred_element_type=jnp.float32,
            )
        )
    conditional, unconditional = predicted
    guided = unconditional + guidance_scale * (conditional - unconditional)
    lane_couple = lax.broadcasted_iota(jnp.int32, (col_pairs, wide), 1) % (2 * couples) // 2
    pairs = jnp.zeros((col_pairs, wide), jnp.float32)
    for couple in range(couples):
        pairs = pairs + jnp.where(
            lane_couple == couple, guided[couple * col_pairs : (couple + 1) * col_pairs], 0.0
        )
    weight_value = blend_ref[0].astype(jnp.float32)
    half = wide // 2
    is_noise = lax.broadcasted_iota(jnp.int32, (col_pairs, wide), 1) < half
    even = jnp.where(is_noise, weight_value * pairs, weight_value)
    odd = jnp.where(is_noise, weight_value * pltpu.roll(pairs, half, 1), weight_value)
    start_at = slab_cols - offset_ref[0]
    buffer_ref[...] = jnp.zeros_like(buffer_ref)
    buffer_ref[pl.ds(start_at, col_pairs, stride=2), :] = even
    buffer_ref[pl.ds(start_at + 1, col_pairs, stride=2), :] = odd
    center_ref[...] = buffer_ref[slab_cols : 2 * slab_cols]
    even_place = lax.axis_index("win") % 2 == 0
    left, right = buffer_ref[:slab_cols], buffer_ref[2 * slab_cols : 3 * slab_cols]
    near_ref[...] = jnp.where(even_place, right, left)
    far_ref[...] = jnp.where(even_place, left, right)


def blend_kernel(plan_ref, center_ref, near_ref, far_ref, rows_ref, previous_ref, noise_ref):
    channels, half_rows, slab_cols = noise_ref.shape
    total = jnp.transpose(center_ref[...] + near_ref[...] + far_ref[...], (1, 0))
    half = total.shape[0] // 2
    noise = total[:half] / total[half:]
    scale = plan_ref[:, :slab_cols]
    previous = (
        scale[0:1] * (rows_ref[...] - scale[1:2] * noise) / scale[2:3] + scale[3:4] * noise
    )
    for channel in range(channels):
        rows = slice(channel * half_rows, (channel + 1) * half_rows)
        noise_ref[channel] = noise[rows]
        previous_ref[channel] = previous[rows]


def on_device(
    latent,
    text_kv,
    modulation,
    qkv_weight,
    out_weight,
    patch_weight,
    final_weight,
    offsets,
    blend_weights,
    step_index,
):
    slab_cols, channels, row_count = latent.shape
    model_width = patch_weight.shape[1]
    half_attn = out_weight.shape[0]
    heads = half_attn // HEAD_DIM
    branches = text_kv.shape[0]
    col_pairs, row_couples = slab_cols, row_count // 2
    tokens = col_pairs * row_couples
    own_tokens = tokens // 2
    half_rows = row_count // 2
    far = swap_ring(latent, "win", 1)
    near = swap_ring(latent, "win", 0)
    hbm = pl.BlockSpec(memory_space=pltpu.HBM)
    keep = functools.partial(pltpu.with_memory_space_constraint, memory_space=pltpu.HBM)
    part = pl.pallas_call(
        cut_kernel,
        out_shape=jax.ShapeDtypeStruct((half_attn // 2, model_width), out_weight.dtype),
        in_specs=[hbm],
        out_specs=VM,
        scratch_shapes=[pltpu.SemaphoreType.DMA],
        name="cut",
        compiler_params=pltpu.CompilerParams(vmem_limit_bytes=GRANT),
    )(keep(out_weight))
    other_weight = swap(part, "cfg")

    weight = jnp.transpose(qkv_weight, (1, 2, 0))
    text = jnp.transpose(text_kv, (0, 1, 3, 2))
    final = jnp.transpose(final_weight, (1, 0))

    bf16, f32 = jnp.bfloat16, jnp.float32
    shape = jax.ShapeDtypeStruct
    wide = 2 * channels * half_rows
    position, patch_wide, plan_values, rows, modulate, weight, text, out_own, final, own = pl.pallas_call(
        prepare_kernel,
        out_shape=(
            shape((tokens, model_width), f32),
            shape((2 * channels * row_count, model_width), bf16),
            shape((8, max(wide, slab_cols)), f32),
            shape((channels * half_rows, slab_cols), f32),
            shape(modulation.shape[1:], f32),
            shape(weight.shape, bf16),
            shape(text.shape, bf16),
            shape(out_weight.shape, bf16),
            shape(final.shape, bf16),
            shape(latent.shape, f32),
        ),
        in_specs=[SM] + [hbm] * 7,
        out_specs=(VM,) * 10,
        scratch_shapes=[
            pltpu.VMEM(patch_weight.shape, bf16),
            pltpu.SemaphoreType.DMA((7,)),
        ],
        name="prepare",
        compiler_params=pltpu.CompilerParams(vmem_limit_bytes=GRANT),
        cost_estimate=pl.CostEstimate(flops=10**7, bytes_accessed=10**6, transcendentals=10**5),
    )(
        step_index,
        *map(keep, (latent, patch_weight, modulation, weight, text, out_weight, final)),
    )
    projected, embedded, sent = pl.pallas_call(
        project_kernel,
        out_shape=(
            shape((3 * heads, HEAD_DIM, tokens), bf16),
            shape((own_tokens, model_width), f32),
            shape((branches, half_attn, own_tokens), bf16),
        ),
        in_specs=[SM] + [VM] * 8,
        out_specs=(VM, VM, VM),
        scratch_shapes=[pltpu.VMEM((3 * slab_cols, channels * row_count), f32)],
        name="project",
        compiler_params=pltpu.CompilerParams(vmem_limit_bytes=GRANT),
        cost_estimate=pl.CostEstimate(flops=2 * 10**9, bytes_accessed=8 * 10**6, transcendentals=10**6),
    )(offsets, modulate, near, own, far, position, patch_wide, weight, text)
    received = swap(sent, "cfg")
    neighbour_weight = swap_ring(other_weight, "win", 0)
    mixed = pl.pallas_call(
        attend_kernel,
        out_shape=shape((branches, own_tokens, model_width), bf16),
        in_specs=[VM] * 3,
        out_specs=VM,
        name="attend",
        compiler_params=pltpu.CompilerParams(vmem_limit_bytes=GRANT),
        cost_estimate=pl.CostEstimate(flops=10**9, bytes_accessed=8 * 10**6, transcendentals=10**6),
    )(projected, text, out_own)
    to_near, center, to_far = pl.pallas_call(
        finish_kernel,
        out_shape=tuple(shape((slab_cols, wide), f32) for _ in range(3)),
        in_specs=[SM, SM] + [VM] * 7,
        out_specs=(VM, VM, VM),
        scratch_shapes=[pltpu.VMEM((3 * slab_cols + 8, wide), f32)],
        name="finish",
        compiler_params=pltpu.CompilerParams(vmem_limit_bytes=GRANT),
        cost_estimate=pl.CostEstimate(flops=10**9, bytes_accessed=4 * 10**6, transcendentals=10**3),
    )(
        offsets, blend_weights, modulate, embedded, mixed, received,
        other_weight, neighbour_weight, final,
    )
    from_far = swap_ring(to_far, "win", 1)
    from_near = swap_ring(to_near, "win", 0)
    previous, noise = pl.pallas_call(
        blend_kernel,
        out_shape=tuple(shape((channels, half_rows, slab_cols), f32) for _ in range(2)),
        in_specs=[VM] * 5,
        out_specs=(VM, VM),
        name="blend",
        compiler_params=pltpu.CompilerParams(vmem_limit_bytes=GRANT),
    )(plan_values, center, from_near, from_far, rows)
    return (jnp.transpose(previous, (2, 0, 1)), jnp.transpose(noise, (2, 0, 1)))


def solution(mesh):
    in_specs = (
        P("win", None, None),
        P(None, None, None, "cfg"),
        P(),
        P(None, None, "cfg"),
        P("cfg", None),
        P(),
        P(),
        P("win"),
        P("win"),
        P(),
    )
    out_specs = (P("win", None, "cfg"), P("win", None, "cfg"))
    return jax.shard_map(
        on_device, mesh=mesh, in_specs=in_specs, out_specs=out_specs, check_vma=False
    )
```

```python
import functools
import math

import jax
import jax.numpy as jnp
from jax import lax
from jax.experimental import pallas as pl
from jax.experimental.pallas import tpu as pltpu
from jax.sharding import PartitionSpec as P


HEAD_DIM = 72
STEPS = 20


guidance_scale = 4.5
plan_length = 1000
norm_eps = 1e-06

VM = pl.BlockSpec(memory_space=pltpu.VMEM)
SM = pl.BlockSpec(memory_space=pltpu.SMEM)
GRANT = 24 * 2**20


def swap_ring(array, axis, odd):
    size = lax.axis_size(axis)
    pairs = []
    for left in range(odd, size, 2):
        right = (left + 1) % size
        pairs += [(left, right), (right, left)]
    return lax.ppermute(array, axis, pairs)


def swap(array, axis):
    return lax.ppermute(array, axis, [(0, 1), (1, 0)])


def swap_even(array, axis, ring):
    size = lax.axis_size(ring)
    pairs = [
        (side * size + place, (1 - side) * size + place)
        for side in range(2)
        for place in range(0, size, 2)
    ]
    return lax.ppermute(array, (axis, ring), pairs)


def even_to_odd(array, axis):
    size = lax.axis_size(axis)
    return lax.ppermute(array, axis, [(place, place + 1) for place in range(0, size, 2)])


def layer_norm(values):
    average = jnp.mean(values, axis=-1, keepdims=True)
    centered = values - average
    variance = jnp.mean(centered * centered, axis=-1, keepdims=True)
    return centered * lax.rsqrt(variance + norm_eps)


def repeat_pairs(weight, repeats):
    rows, width = weight.shape
    values = weight.astype(jnp.float32)
    even = lax.broadcasted_iota(jnp.int32, (2 * repeats, width), 0) % 2 == 0
    parts = []
    for pair in range(rows // 2):
        parts.append(
            jnp.where(even, values[2 * pair : 2 * pair + 1, :], values[2 * pair + 1 : 2 * pair + 2, :])
        )
    return jnp.concatenate(parts, axis=0).astype(jnp.bfloat16)


def prepare_kernel(
    step_ref,
    latent_source,
    patch_source,
    modulation_ref,
    position_ref,
    patch_wide_ref,
    plan_ref,
    rows_ref,
    modulate_copy,
    latent_ref,
    patch_ref,
    semaphores,
):
    row = step_ref[0] * STEPS // plan_length
    copies = [
        pltpu.make_async_copy(source, target, semaphores.at[place])
        for place, (source, target) in enumerate(
            (
                (latent_source, latent_ref),
                (patch_source, patch_ref),
                (modulation_ref.at[row], modulate_copy),
            )
        )
    ]
    for copy in copies:
        copy.start()
    _, model_width = position_ref.shape
    slab_cols, channels, row_count = latent_ref.shape
    row_couples = row_count // 2
    quarter = model_width // 4

    half = 2 * quarter

    def table(count, first, lanes):
        lane = first + lax.broadcasted_iota(jnp.int32, (count, lanes), 1)
        place = lax.broadcasted_iota(jnp.int32, (count, lanes), 0).astype(jnp.float32)
        frequency = jnp.exp(-math.log(10000.0) * (lane % quarter).astype(jnp.float32) / quarter)
        phase = jnp.where(lane // quarter % 2 == 0, 0.0, 0.5 * math.pi)
        return jnp.sin(place * frequency + phase)

    below, above = half // 128 * 128, -(-half // 128) * 128
    row_part = table(row_couples, 0, above)
    col_part = table(slab_cols, below, model_width - below)
    lane = below + lax.broadcasted_iota(jnp.int32, (slab_cols, above - below), 1)
    for couple in range(row_couples):
        rows = slice(couple * slab_cols, (couple + 1) * slab_cols)
        line = jnp.broadcast_to(row_part[couple : couple + 1, :], (slab_cols, above))
        position_ref[rows, :below] = line[:, :below]
        position_ref[rows, below:above] = jnp.where(
            lane < half, line[:, below:], col_part[:, : above - below]
        )
        position_ref[rows, above:] = col_part[:, above - below :]
    copies[1].wait()
    patch_wide_ref[...] = repeat_pairs(patch_ref[...], row_couples)

    moment = step_ref[0]
    index = lax.broadcasted_iota(jnp.int32, (8, 128), 0) * 128 + lax.broadcasted_iota(
        jnp.int32, (8, 128), 1
    )
    train = jnp.minimum(index, plan_length - 1).astype(jnp.float32)
    beta_values = 0.0001 + (0.02 - 0.0001) * train / (plan_length - 1)
    logs = jnp.log(1.0 - beta_values)

    def alpha_bar(last):
        kept = jnp.where((index <= last) & (index < plan_length), logs, 0.0)
        kept = jnp.sum(jnp.sum(kept, axis=0, keepdims=True), axis=1, keepdims=True)
        return jnp.exp(kept)

    alpha_now = alpha_bar(moment)
    alpha_before = alpha_bar(moment - plan_length // STEPS)
    for place, value in enumerate(
        (
            jnp.sqrt(alpha_before),
            jnp.sqrt(1.0 - alpha_now),
            jnp.sqrt(alpha_now),
            jnp.sqrt(1.0 - alpha_before),
        )
    ):
        plan_ref[place : place + 1, :] = jnp.broadcast_to(value, (1, plan_ref.shape[1]))

    half_rows = row_count // 2
    side = lax.axis_index("cfg")
    copies[0].wait()
    for channel in range(channels):
        turned = jnp.transpose(latent_ref[:, channel, :], (1, 0))
        rows_ref[channel * half_rows : (channel + 1) * half_rows, :] = jnp.where(
            side == 0, turned[:half_rows], turned[half_rows:]
        )
    for copy in copies[2:]:
        copy.wait()


def attend(proj_ref, text_ref, first, count, chosen):
    heads = proj_ref.shape[0] // 3
    branches = text_ref.shape[0]
    factor = math.log2(math.e) / math.sqrt(HEAD_DIM)
    feature = (((0,), (0,)), ((), ()))
    results = [[] for _ in range(branches)]
    for head in chosen:
        rows = slice(head * HEAD_DIM, (head + 1) * HEAD_DIM)
        queries = proj_ref[head, :, pl.ds(first, count)]
        own_scores = lax.dot_general(
            proj_ref[heads + head], queries, feature, preferred_element_type=jnp.float32
        )
        own_highest = jnp.max(own_scores, axis=0, keepdims=True)
        own_exp = jnp.exp2((own_scores - own_highest) * factor)
        own_total = jnp.sum(own_exp, axis=0, keepdims=True)
        own_mix = jnp.dot(
            proj_ref[2 * heads + head],
            own_exp.astype(jnp.bfloat16),
            preferred_element_type=jnp.float32,
        )
        for branch in range(branches):
            text_scores = lax.dot_general(
                text_ref[branch, 0, rows, :], queries, feature, preferred_element_type=jnp.float32
            )
            highest = jnp.maximum(own_highest, jnp.max(text_scores, axis=0, keepdims=True))
            text_exp = jnp.exp2((text_scores - highest) * factor)
            lowered = jnp.exp2((own_highest - highest) * factor)
            total = lowered * own_total + jnp.sum(text_exp, axis=0, keepdims=True)
            text_mix = jnp.dot(
                text_ref[branch, 1, rows, :],
                text_exp.astype(jnp.bfloat16),
                preferred_element_type=jnp.float32,
            )
            results[branch].append((lowered * own_mix + text_mix) * (1.0 / total))
    return [jnp.concatenate(parts, axis=0).astype(jnp.bfloat16) for parts in results]


def project_kernel(
    offset_ref,
    modulation_ref,
    near_ref,
    own_ref,
    far_ref,
    position_ref,
    patch_ref,
    weight_source,
    text_source,
    proj_ref,
    embedded_ref,
    text_ref,
    sent_ref,
    extended_ref,
    weight_ref,
    semaphores,
):
    weight_copy = pltpu.make_async_copy(weight_source, weight_ref, semaphores.at[0])
    text_copy = pltpu.make_async_copy(text_source, text_ref, semaphores.at[1])
    weight_copy.start()
    text_copy.start()
    slab_cols, channels, row_count = own_ref.shape
    col_pairs, row_couples = slab_cols, row_count // 2
    tokens = col_pairs * row_couples
    own_tokens = tokens // 2
    wide = 2 * channels * row_count
    even = lax.axis_index("win") % 2 == 0
    for channel in range(channels):
        near, far = near_ref[:, channel, :], far_ref[:, channel, :]
        values = (jnp.where(even, far, near), own_ref[:, channel, :], jnp.where(even, near, far))
        for place, value in enumerate(values):
            extended_ref[
                place * slab_cols : (place + 1) * slab_cols,
                channel * row_count : (channel + 1) * row_count,
            ] = value
    extended = extended_ref[...].astype(jnp.bfloat16)
    start_at = slab_cols - offset_ref[0]
    chosen = lax.broadcasted_iota(jnp.int32, (2 * col_pairs, 3 * slab_cols), 0)
    column = lax.broadcasted_iota(jnp.int32, (2 * col_pairs, 3 * slab_cols), 1)
    target = jnp.where(
        chosen < col_pairs, 2 * chosen, 2 * (chosen - col_pairs) + 1
    )
    pick = jnp.where(column == target + start_at, 1.0, 0.0).astype(jnp.bfloat16)
    picked = jnp.dot(pick, extended, preferred_element_type=jnp.float32)
    picked = jnp.concatenate([picked[:col_pairs], picked[col_pairs:]], axis=1)
    lane_couple = lax.broadcasted_iota(jnp.int32, (col_pairs, wide), 1) % row_count // 2
    spread = jnp.concatenate(
        [jnp.where(lane_couple == couple, picked, 0.0) for couple in range(row_couples)], axis=0
    ).astype(jnp.bfloat16)
    embedded = jnp.dot(spread, patch_ref[...], preferred_element_type=jnp.float32)
    embedded = embedded + position_ref[...]
    side = lax.axis_index("cfg")
    normed = (
        layer_norm(embedded) * (1.0 + modulation_ref[1:2, :]) + modulation_ref[0:1, :]
    ).astype(jnp.bfloat16)

    @pl.when(side == 0)
    def _():
        embedded_ref[...] = embedded[:own_tokens]

    @pl.when(side != 0)
    def _():
        embedded_ref[...] = embedded[own_tokens:]

    heads = proj_ref.shape[0] // 3
    weight_copy.wait()
    for kind in range(3):
        projected = lax.dot_general(
            weight_ref[kind],
            normed,
            (((1,), (1,)), ((), ())),
            preferred_element_type=jnp.float32,
        )
        for head in range(heads):
            proj_ref[kind * heads + head] = projected[
                head * HEAD_DIM : (head + 1) * HEAD_DIM
            ].astype(jnp.bfloat16)
    first = pl.multiple_of((1 - side) * own_tokens, own_tokens)
    text_copy.wait()
    for branch, value in enumerate(
        attend(proj_ref, text_ref, first, own_tokens, range(heads // 2))
    ):
        sent_ref[branch] = value


def second_kernel(proj_ref, text_ref, sent_ref):
    heads = proj_ref.shape[0] // 3
    own_tokens = proj_ref.shape[2] // 2
    first = pl.multiple_of((1 - lax.axis_index("cfg")) * own_tokens, own_tokens)
    for branch, value in enumerate(
        attend(proj_ref, text_ref, first, own_tokens, range(heads // 2, heads))
    ):
        sent_ref[branch] = value


def attend_kernel(proj_ref, text_ref, weight_source, mixed_ref, weight_ref, semaphore):
    weight_copy = pltpu.make_async_copy(weight_source, weight_ref, semaphore)
    weight_copy.start()
    heads = proj_ref.shape[0] // 3
    tokens = proj_ref.shape[2]
    own_tokens = tokens // 2
    first = pl.multiple_of(lax.axis_index("cfg") * own_tokens, own_tokens)
    values = attend(proj_ref, text_ref, first, own_tokens, range(heads))
    weight_copy.wait()
    for branch, value in enumerate(values):
        mixed_ref[branch] = lax.dot_general(
            value, weight_ref[...], (((0,), (0,)), ((), ())), preferred_element_type=jnp.float32
        ).astype(jnp.bfloat16)


def finish_kernel(
    offset_ref,
    blend_ref,
    modulation_ref,
    embedded_ref,
    mixed_ref,
    early_ref,
    late_ref,
    weight_ref,
    neighbour_ref,
    final_ref,
    near_ref,
    center_ref,
    far_ref,
    buffer_ref,
):
    even_place = lax.axis_index("win") % 2 == 0
    other_weight = jnp.where(even_place, weight_ref[...], neighbour_ref[...])
    count = early_ref.shape[1]
    feature = (((0,), (0,)), ((), ()))
    slab_cols = center_ref.shape[0]
    col_pairs = slab_cols
    own_tokens = embedded_ref.shape[0]
    couples = own_tokens // col_pairs
    final_wide = repeat_pairs(final_ref[...], couples)
    wide = final_wide.shape[0]
    predicted = []
    for branch in range(2):
        other = lax.dot_general(
            early_ref[branch],
            other_weight[:count],
            feature,
            preferred_element_type=jnp.float32,
        ) + lax.dot_general(
            late_ref[branch],
            other_weight[count:],
            feature,
            preferred_element_type=jnp.float32,
        )
        mixed = mixed_ref[branch].astype(jnp.float32) + other
        residual = embedded_ref[...] + modulation_ref[2:3, :] * mixed
        final_norm = (layer_norm(residual) * (1.0 + modulation_ref[3:4, :])).astype(jnp.bfloat16)
        predicted.append(
            lax.dot_general(
                final_norm,
                final_wide,
                (((1,), (1,)), ((), ())),
                preferred_element_type=jnp.float32,
            )
        )
    conditional, unconditional = predicted
    guided = unconditional + guidance_scale * (conditional - unconditional)
    lane_couple = lax.broadcasted_iota(jnp.int32, (col_pairs, wide), 1) % (2 * couples) // 2
    pairs = jnp.zeros((col_pairs, wide), jnp.float32)
    for couple in range(couples):
        pairs = pairs + jnp.where(
            lane_couple == couple, guided[couple * col_pairs : (couple + 1) * col_pairs], 0.0
        )
    weight_value = blend_ref[0].astype(jnp.float32)
    half = wide // 2
    is_noise = lax.broadcasted_iota(jnp.int32, (col_pairs, wide), 1) < half
    even = jnp.where(is_noise, weight_value * pairs, weight_value)
    odd = jnp.where(is_noise, weight_value * pltpu.roll(pairs, half, 1), weight_value)
    start_at = slab_cols - offset_ref[0]
    buffer_ref[...] = jnp.zeros_like(buffer_ref)
    buffer_ref[pl.ds(start_at, col_pairs, stride=2), :] = even
    buffer_ref[pl.ds(start_at + 1, col_pairs, stride=2), :] = odd
    center_ref[...] = buffer_ref[slab_cols : 2 * slab_cols]
    left, right = buffer_ref[:slab_cols], buffer_ref[2 * slab_cols : 3 * slab_cols]
    near_ref[...] = jnp.where(even_place, right, left)
    far_ref[...] = jnp.where(even_place, left, right)


def blend_kernel(plan_ref, center_ref, near_ref, far_ref, rows_ref, previous_ref, noise_ref):
    channels, half_rows, slab_cols = noise_ref.shape
    total = jnp.transpose(center_ref[...] + near_ref[...] + far_ref[...], (1, 0))
    half = total.shape[0] // 2
    noise = total[:half] / total[half:]
    scale = plan_ref[:, :slab_cols]
    previous = (
        scale[0:1] * (rows_ref[...] - scale[1:2] * noise) / scale[2:3] + scale[3:4] * noise
    )
    for channel in range(channels):
        rows = slice(channel * half_rows, (channel + 1) * half_rows)
        noise_ref[channel] = noise[rows]
        previous_ref[channel] = previous[rows]


def on_device(
    latent,
    text_kv,
    modulation,
    qkv_weight,
    out_weight,
    patch_weight,
    final_weight,
    offsets,
    blend_weights,
    step_index,
):
    slab_cols, channels, row_count = latent.shape
    model_width = patch_weight.shape[1]
    half_attn = out_weight.shape[0]
    heads = half_attn // HEAD_DIM
    branches = text_kv.shape[0]
    col_pairs, row_couples = slab_cols, row_count // 2
    tokens = col_pairs * row_couples
    own_tokens = tokens // 2
    half_rows = row_count // 2
    far = swap_ring(latent, "win", 1)
    near = swap_ring(latent, "win", 0)
    hbm = pl.BlockSpec(memory_space=pltpu.HBM)
    keep = functools.partial(pltpu.with_memory_space_constraint, memory_space=pltpu.HBM)
    other_weight = swap_even(out_weight, "cfg", "win")

    weight = jnp.transpose(qkv_weight, (1, 2, 0))
    text = jnp.transpose(text_kv, (0, 1, 3, 2))
    final = jnp.transpose(final_weight, (1, 0))

    bf16, f32 = jnp.bfloat16, jnp.float32
    shape = jax.ShapeDtypeStruct
    wide = 2 * channels * half_rows
    position, patch_wide, plan_values, rows, modulate, own = pl.pallas_call(
        prepare_kernel,
        out_shape=(
            shape((tokens, model_width), f32),
            shape((2 * channels * row_count, model_width), bf16),
            shape((8, max(wide, slab_cols)), f32),
            shape((channels * half_rows, slab_cols), f32),
            shape(modulation.shape[1:], f32),
            shape(latent.shape, f32),
        ),
        in_specs=[SM] + [hbm] * 3,
        out_specs=(VM,) * 6,
        scratch_shapes=[
            pltpu.VMEM(patch_weight.shape, bf16),
            pltpu.SemaphoreType.DMA((3,)),
        ],
        name="prepare",
        compiler_params=pltpu.CompilerParams(vmem_limit_bytes=GRANT),
        cost_estimate=pl.CostEstimate(flops=10**7, bytes_accessed=10**6, transcendentals=10**5),
    )(
        step_index,
        *map(keep, (latent, patch_weight, modulation)),
    )
    projected, embedded, text, sent = pl.pallas_call(
        project_kernel,
        out_shape=(
            shape((3 * heads, HEAD_DIM, tokens), bf16),
            shape((own_tokens, model_width), f32),
            shape(text.shape, bf16),
            shape((branches, half_attn // 2, own_tokens), bf16),
        ),
        in_specs=[SM] + [VM] * 6 + [hbm] * 2,
        out_specs=(VM,) * 4,
        scratch_shapes=[
            pltpu.VMEM((3 * slab_cols, channels * row_count), f32),
            pltpu.VMEM(weight.shape, bf16),
            pltpu.SemaphoreType.DMA((2,)),
        ],
        name="project",
        compiler_params=pltpu.CompilerParams(vmem_limit_bytes=GRANT),
        cost_estimate=pl.CostEstimate(flops=2 * 10**9, bytes_accessed=8 * 10**6, transcendentals=10**6),
    )(offsets, modulate, near, own, far, position, patch_wide, keep(weight), keep(text))
    early = swap(sent, "cfg")
    sent = pl.pallas_call(
        second_kernel,
        out_shape=shape((branches, half_attn // 2, own_tokens), bf16),
        in_specs=[VM] * 2,
        out_specs=VM,
        name="second",
        compiler_params=pltpu.CompilerParams(vmem_limit_bytes=GRANT),
        cost_estimate=pl.CostEstimate(flops=10**9, bytes_accessed=10**6, transcendentals=10**6),
    )(projected, text)
    late = swap(sent, "cfg")
    neighbour_weight = even_to_odd(other_weight, "win")
    mixed = pl.pallas_call(
        attend_kernel,
        out_shape=shape((branches, own_tokens, model_width), bf16),
        in_specs=[VM] * 2 + [hbm],
        out_specs=VM,
        scratch_shapes=[pltpu.VMEM(out_weight.shape, bf16), pltpu.SemaphoreType.DMA],
        name="attend",
        compiler_params=pltpu.CompilerParams(vmem_limit_bytes=GRANT),
        cost_estimate=pl.CostEstimate(flops=10**9, bytes_accessed=8 * 10**6, transcendentals=10**6),
    )(projected, text, keep(out_weight))
    to_near, center, to_far = pl.pallas_call(
        finish_kernel,
        out_shape=tuple(shape((slab_cols, wide), f32) for _ in range(3)),
        in_specs=[SM, SM] + [VM] * 8,
        out_specs=(VM, VM, VM),
        scratch_shapes=[pltpu.VMEM((3 * slab_cols + 8, wide), f32)],
        name="finish",
        compiler_params=pltpu.CompilerParams(vmem_limit_bytes=GRANT),
        cost_estimate=pl.CostEstimate(flops=10**9, bytes_accessed=4 * 10**6, transcendentals=10**3),
    )(
        offsets, blend_weights, modulate, embedded, mixed, early, late,
        other_weight, neighbour_weight, final,
    )
    from_far = swap_ring(to_far, "win", 1)
    from_near = swap_ring(to_near, "win", 0)
    previous, noise = pl.pallas_call(
        blend_kernel,
        out_shape=tuple(shape((channels, half_rows, slab_cols), f32) for _ in range(2)),
        in_specs=[VM] * 5,
        out_specs=(VM, VM),
        name="blend",
        compiler_params=pltpu.CompilerParams(vmem_limit_bytes=GRANT),
    )(plan_values, center, from_near, from_far, rows)
    return (jnp.transpose(previous, (2, 0, 1)), jnp.transpose(noise, (2, 0, 1)))


def solution(mesh):
    in_specs = (
        P("win", None, None),
        P(None, None, None, "cfg"),
        P(),
        P(None, None, "cfg"),
        P("cfg", None),
        P(),
        P(),
        P("win"),
        P("win"),
        P(),
    )
    out_specs = (P("win", None, "cfg"), P("win", None, "cfg"))
    return jax.shard_map(
        on_device, mesh=mesh, in_specs=in_specs, out_specs=out_specs, check_vma=False
    )
```

```python
import functools
import math

import jax
import jax.numpy as jnp
from jax import lax
from jax.experimental import pallas as pl
from jax.experimental.pallas import tpu as pltpu
from jax.sharding import PartitionSpec as P


HEAD_DIM = 72
STEPS = 20


guidance_scale = 4.5
plan_length = 1000
norm_eps = 1e-06

VM = pl.BlockSpec(memory_space=pltpu.VMEM)
SM = pl.BlockSpec(memory_space=pltpu.SMEM)
GRANT = 24 * 2**20


def swap_ring(array, axis, odd):
    size = lax.axis_size(axis)
    pairs = []
    for left in range(odd, size, 2):
        right = (left + 1) % size
        pairs += [(left, right), (right, left)]
    return lax.ppermute(array, axis, pairs)


def swap(array, axis):
    return lax.ppermute(array, axis, [(0, 1), (1, 0)])


def swap_across(array, axis, step):
    size = lax.axis_size(axis)
    return lax.ppermute(array, axis, [(place, place ^ step) for place in range(size)])


def layer_norm(values):
    average = jnp.mean(values, axis=-1, keepdims=True)
    centered = values - average
    variance = jnp.mean(centered * centered, axis=-1, keepdims=True)
    return centered * lax.rsqrt(variance + norm_eps)


def repeat_pairs(weight, repeats):
    rows, width = weight.shape
    values = weight.astype(jnp.float32)
    even = lax.broadcasted_iota(jnp.int32, (2 * repeats, width), 0) % 2 == 0
    parts = []
    for pair in range(rows // 2):
        parts.append(
            jnp.where(even, values[2 * pair : 2 * pair + 1, :], values[2 * pair + 1 : 2 * pair + 2, :])
        )
    return jnp.concatenate(parts, axis=0).astype(jnp.bfloat16)


def prepare_kernel(
    step_ref,
    offset_ref,
    latent_source,
    patch_source,
    modulation_ref,
    out_source,
    row_ref,
    col_ref,
    patch_wide_ref,
    start_ref,
    modulate_copy,
    latent_copy,
    quarter_copy,
    patch_ref,
    semaphores,
):
    count = quarter_copy.shape[0]
    quarter_first = pl.multiple_of(lax.axis_index("win") % 4 * count, 8)
    row = step_ref[0] * STEPS // plan_length
    copies = [
        pltpu.make_async_copy(source, target, semaphores.at[place])
        for place, (source, target) in enumerate(
            (
                (patch_source, patch_ref),
                (modulation_ref.at[row], modulate_copy),
                (latent_source, latent_copy),
                (out_source.at[pl.ds(quarter_first, count)], quarter_copy),
            )
        )
    ]
    for copy in copies:
        copy.start()
    slab_cols, _, row_count = latent_copy.shape
    model_width = patch_ref.shape[1]
    quarter = model_width // 4

    def table(target_ref, first):
        count, lanes = target_ref.shape
        lane = first + lax.broadcasted_iota(jnp.int32, (count, lanes), 1)
        place = lax.broadcasted_iota(jnp.int32, (count, lanes), 0).astype(jnp.float32)
        frequency = jnp.exp(-math.log(10000.0) * (lane % quarter).astype(jnp.float32) / quarter)
        phase = jnp.where(lane // quarter % 2 == 0, 0.0, 0.5 * math.pi)
        target_ref[...] = jnp.sin(place * frequency + phase)

    table(row_ref, 0)
    table(col_ref, model_width - col_ref.shape[1])
    is_start = lax.broadcasted_iota(jnp.int32, start_ref.shape, 0) == 0
    start_ref[...] = jnp.where(is_start, slab_cols - offset_ref[0], step_ref[0])
    copies[0].wait()
    patch_wide_ref[...] = repeat_pairs(patch_ref[...], row_count // 2)
    for copy in copies[1:]:
        copy.wait()


def coefficient_kernel(start_ref, latent_ref, plan_ref, rows_ref):
    _, channels, row_count = latent_ref.shape
    moment = start_ref[1:2, :128]
    index = lax.broadcasted_iota(jnp.int32, (8, 128), 0) * 128 + lax.broadcasted_iota(
        jnp.int32, (8, 128), 1
    )
    train = jnp.minimum(index, plan_length - 1).astype(jnp.float32)
    beta_values = 0.0001 + (0.02 - 0.0001) * train / (plan_length - 1)
    logs = jnp.log(1.0 - beta_values)

    def alpha_bar(last):
        kept = jnp.where((index <= last) & (index < plan_length), logs, 0.0)
        kept = jnp.sum(jnp.sum(kept, axis=0, keepdims=True), axis=1, keepdims=True)
        return jnp.exp(kept)

    alpha_now = alpha_bar(moment)
    alpha_before = alpha_bar(moment - plan_length // STEPS)
    for place, value in enumerate(
        (
            jnp.sqrt(alpha_before),
            jnp.sqrt(1.0 - alpha_now),
            jnp.sqrt(alpha_now),
            jnp.sqrt(1.0 - alpha_before),
        )
    ):
        plan_ref[place : place + 1, :] = jnp.broadcast_to(value, (1, plan_ref.shape[1]))

    half_rows = row_count // 2
    side = lax.axis_index("cfg")
    for channel in range(channels):
        turned = jnp.transpose(latent_ref[:, channel, :], (1, 0))
        rows_ref[channel * half_rows : (channel + 1) * half_rows, :] = jnp.where(
            side == 0, turned[:half_rows], turned[half_rows:]
        )


def attend(proj_ref, text_ref, first, count, chosen, finished):
    heads = proj_ref.shape[0] // 3
    branches = text_ref.shape[0]
    feature = (((0,), (0,)), ((), ()))

    def score(head):
        rows = slice(head * HEAD_DIM, (head + 1) * HEAD_DIM)
        queries = proj_ref[head, :, pl.ds(first, count)]
        return [
            lax.dot_general(keys, queries, feature, preferred_element_type=jnp.float32)
            for keys in [proj_ref[heads + head]]
            + [text_ref[branch, 0, rows, :] for branch in range(branches)]
        ]

    def weigh(scores):
        own_highest = jnp.max(scores[0], axis=0, keepdims=True)
        own_exp = jnp.exp2(scores[0] - own_highest)
        own = (own_exp.astype(jnp.bfloat16), jnp.sum(own_exp, axis=0, keepdims=True))
        texts = []
        for text_scores in scores[1:]:
            highest = jnp.maximum(own_highest, jnp.max(text_scores, axis=0, keepdims=True))
            text_exp = jnp.exp2(text_scores - highest)
            lowered = jnp.exp2(own_highest - highest)
            total = lowered * own[1] + jnp.sum(text_exp, axis=0, keepdims=True)
            texts.append((text_exp.astype(jnp.bfloat16), lowered, 1.0 / total))
        return own[0], texts

    def mix(head, own_exp, texts):
        rows = slice(head * HEAD_DIM, (head + 1) * HEAD_DIM)
        own_mix = jnp.dot(
            proj_ref[2 * heads + head], own_exp, preferred_element_type=jnp.float32
        )
        results = []
        for branch, (text_exp, lowered, inverse) in enumerate(texts):
            text_mix = jnp.dot(
                text_ref[branch, 1, rows, :], text_exp, preferred_element_type=jnp.float32
            )
            results.append((lowered * own_mix + text_mix) * inverse)
        return jnp.concatenate(results, axis=1)

    chosen = list(chosen)
    mixed = []

    def take(place, weights):
        mixed.append(mix(chosen[place], *weights))
        if place % 2:
            finished(place // 2, jnp.concatenate(mixed[-2:], axis=0).astype(jnp.bfloat16))

    ahead = score(chosen[0])
    before = None
    for place, head in enumerate(chosen):
        scores = ahead
        if place + 1 < len(chosen):
            ahead = score(chosen[place + 1])
        weights = weigh(scores)
        if before is not None:
            take(place - 1, before)
        before = weights
    take(len(chosen) - 1, before)


def keep_pair(target_ref, place, pair):
    target_ref[...] = pair


def project_kernel(
    start_ref,
    modulation_ref,
    near_ref,
    own_ref,
    far_ref,
    row_ref,
    col_ref,
    patch_ref,
    weight_source,
    text_source,
    proj_ref,
    embedded_ref,
    text_ref,
    sent_ref,
    extended_ref,
    weight_ref,
    semaphores,
):
    weight_copy = pltpu.make_async_copy(weight_source, weight_ref, semaphores.at[0])
    text_copy = pltpu.make_async_copy(text_source, text_ref, semaphores.at[1])
    weight_copy.start()
    text_copy.start()
    slab_cols, channels, row_count = own_ref.shape
    col_pairs, row_couples = slab_cols, row_count // 2
    tokens = col_pairs * row_couples
    own_tokens = tokens // 2
    wide = 2 * channels * row_count
    even = lax.axis_index("win") % 2 == 0
    for channel in range(channels):
        near, far = near_ref[:, channel, :], far_ref[:, channel, :]
        values = (jnp.where(even, far, near), own_ref[:, channel, :], jnp.where(even, near, far))
        for place, value in enumerate(values):
            extended_ref[
                place * slab_cols : (place + 1) * slab_cols,
                channel * row_count : (channel + 1) * row_count,
            ] = value
    extended = extended_ref[...].astype(jnp.bfloat16)
    start_at = start_ref[0:1, : 3 * slab_cols]
    chosen = lax.broadcasted_iota(jnp.int32, (2 * col_pairs, 3 * slab_cols), 0)
    column = lax.broadcasted_iota(jnp.int32, (2 * col_pairs, 3 * slab_cols), 1)
    target = jnp.where(
        chosen < col_pairs, 2 * chosen, 2 * (chosen - col_pairs) + 1
    )
    pick = jnp.where(column == target + start_at, 1.0, 0.0).astype(jnp.bfloat16)
    picked = jnp.dot(pick, extended, preferred_element_type=jnp.float32)
    picked = jnp.concatenate([picked[:col_pairs], picked[col_pairs:]], axis=1)
    lane_couple = lax.broadcasted_iota(jnp.int32, (col_pairs, wide), 1) % row_count // 2
    spread = jnp.concatenate(
        [jnp.where(lane_couple == couple, picked, 0.0) for couple in range(row_couples)], axis=0
    ).astype(jnp.bfloat16)
    side = lax.axis_index("cfg")
    heads = proj_ref.shape[0] // 3
    chunks = [slice(place * own_tokens, (place + 1) * own_tokens) for place in range(2)]

    couples = row_couples // 2
    model_width = patch_ref.shape[1]
    below, above = model_width - col_ref.shape[1], row_ref.shape[1]
    is_row = below + lax.broadcasted_iota(jnp.int32, (col_pairs, above - below), 1)
    is_row = is_row < model_width // 2

    def position(couple):
        line = jnp.broadcast_to(row_ref[couple : couple + 1, :], (col_pairs, above))
        column = col_ref[...]
        both = jnp.where(is_row, line[:, below:], column[:, : above - below])
        return jnp.concatenate([line[:, :below], both, column[:, above - below :]], axis=1)

    def embed(place):
        chunk = chunks[place]
        embedded = jnp.dot(spread[chunk], patch_ref[...], preferred_element_type=jnp.float32)
        embedded = embedded + jnp.concatenate(
            [position(couple) for couple in range(row_couples)[place * couples :][:couples]], axis=0
        )

        @pl.when(side == place)
        def _():
            embedded_ref[...] = embedded

        return embedded

    def norm(embedded):
        return (
            layer_norm(embedded) * (1.0 + modulation_ref[1:2, :]) + modulation_ref[0:1, :]
        ).astype(jnp.bfloat16)

    def project(place, normed):
        projected = lax.dot_general(
            weight_ref[...],
            normed,
            (((1,), (1,)), ((), ())),
            preferred_element_type=jnp.float32,
        )
        for head in range(3 * heads):
            part = projected[head * HEAD_DIM : (head + 1) * HEAD_DIM]
            if head < heads:
                part = part * (math.log2(math.e) / math.sqrt(HEAD_DIM))
            proj_ref[head, :, chunks[place]] = part.astype(jnp.bfloat16)

    normed = norm(embed(0))
    later = embed(1)
    weight_copy.wait()
    project(0, normed)
    project(1, norm(later))
    first = pl.multiple_of((1 - side) * own_tokens, own_tokens)
    text_copy.wait()
    attend(proj_ref, text_ref, first, own_tokens, range(heads // 2), functools.partial(keep_pair, sent_ref))


def second_kernel(proj_ref, text_ref, sent_ref):
    heads = proj_ref.shape[0] // 3
    own_tokens = proj_ref.shape[2] // 2
    first = pl.multiple_of((1 - lax.axis_index("cfg")) * own_tokens, own_tokens)
    attend(proj_ref, text_ref, first, own_tokens, range(heads // 2, heads), functools.partial(keep_pair, sent_ref))


def attend_kernel(proj_ref, text_ref, weight_source, mixed_ref, weight_ref, semaphore):
    weight_copy = pltpu.make_async_copy(weight_source, weight_ref, semaphore)
    weight_copy.start()
    heads = proj_ref.shape[0] // 3
    tokens = proj_ref.shape[2]
    own_tokens = tokens // 2
    first = pl.multiple_of(lax.axis_index("cfg") * own_tokens, own_tokens)
    weight_copy.wait()
    pairs = []

    def finished(place, pair):
        pairs.append(pair)

    attend(proj_ref, text_ref, first, own_tokens, range(heads), finished)
    mixed_ref[...] = lax.dot_general(
        jnp.concatenate(pairs, axis=0),
        weight_ref[...],
        (((0,), (0,)), ((), ())),
        preferred_element_type=jnp.float32,
    ).astype(jnp.bfloat16)


def finish_kernel(
    start_source,
    blend_ref,
    modulation_ref,
    embedded_ref,
    mixed_ref,
    early_ref,
    late_ref,
    weight_ref,
    core_ref,
    cross_ref,
    core_cross_ref,
    final_ref,
    near_ref,
    center_ref,
    far_ref,
    buffer_ref,
    start_ref,
    semaphore,
):
    start_copy = pltpu.make_async_copy(start_source, start_ref, semaphore)
    start_copy.start()
    even_place = lax.axis_index("win") % 2 == 0
    lower_pair = lax.axis_index("win") % 4 < 2

    def join(mine, neighbour):
        mine, neighbour = mine[...].astype(jnp.float32), neighbour[...].astype(jnp.float32)
        first = jnp.where(even_place, mine, neighbour)
        second = jnp.where(even_place, neighbour, mine)
        return jnp.concatenate([first, second], axis=0).astype(jnp.bfloat16)

    feature = (((0,), (0,)), ((), ()))
    early, late = early_ref[...], late_ref[...]
    other = lax.dot_general(
        jnp.where(lower_pair, early, late),
        join(weight_ref, core_ref),
        feature,
        preferred_element_type=jnp.float32,
    ) + lax.dot_general(
        jnp.where(lower_pair, late, early),
        join(cross_ref, core_cross_ref),
        feature,
        preferred_element_type=jnp.float32,
    )
    slab_cols = center_ref.shape[0]
    col_pairs = slab_cols
    own_tokens = embedded_ref.shape[0]
    couples = own_tokens // col_pairs
    final_wide = repeat_pairs(final_ref[...], couples)
    wide = final_wide.shape[0]
    predicted = []
    for branch in range(2):
        rows = slice(branch * own_tokens, (branch + 1) * own_tokens)
        mixed = mixed_ref[rows, :].astype(jnp.float32) + other[rows]
        residual = embedded_ref[...] + modulation_ref[2:3, :] * mixed
        final_norm = (layer_norm(residual) * (1.0 + modulation_ref[3:4, :])).astype(jnp.bfloat16)
        predicted.append(
            lax.dot_general(
                final_norm,
                final_wide,
                (((1,), (1,)), ((), ())),
                preferred_element_type=jnp.float32,
            )
        )
    conditional, unconditional = predicted
    guided = unconditional + guidance_scale * (conditional - unconditional)
    lane_couple = lax.broadcasted_iota(jnp.int32, (col_pairs, wide), 1) % (2 * couples) // 2
    pairs = jnp.zeros((col_pairs, wide), jnp.float32)
    for couple in range(couples):
        pairs = pairs + jnp.where(
            lane_couple == couple, guided[couple * col_pairs : (couple + 1) * col_pairs], 0.0
        )
    weight_value = blend_ref[0].astype(jnp.float32)
    half = wide // 2
    is_noise = lax.broadcasted_iota(jnp.int32, (col_pairs, wide), 1) < half
    even = jnp.where(is_noise, weight_value * pairs, weight_value)
    odd = jnp.where(is_noise, weight_value * pltpu.roll(pairs, half, 1), weight_value)
    start_copy.wait()
    start_at = start_ref[0, 0]
    buffer_ref[...] = jnp.zeros_like(buffer_ref)
    buffer_ref[pl.ds(start_at, col_pairs, stride=2), :] = even
    buffer_ref[pl.ds(start_at + 1, col_pairs, stride=2), :] = odd
    center_ref[...] = buffer_ref[slab_cols : 2 * slab_cols]
    left, right = buffer_ref[:slab_cols], buffer_ref[2 * slab_cols : 3 * slab_cols]
    near_ref[...] = jnp.where(even_place, right, left)
    far_ref[...] = jnp.where(even_place, left, right)


def blend_kernel(plan_ref, center_ref, near_ref, far_ref, rows_ref, previous_ref, noise_ref):
    channels, half_rows, slab_cols = noise_ref.shape
    total = jnp.transpose(center_ref[...] + near_ref[...] + far_ref[...], (1, 0))
    half = total.shape[0] // 2
    noise = total[:half] / total[half:]
    scale = plan_ref[:, :slab_cols]
    previous = (
        scale[0:1] * (rows_ref[...] - scale[1:2] * noise) / scale[2:3] + scale[3:4] * noise
    )
    for channel in range(channels):
        rows = slice(channel * half_rows, (channel + 1) * half_rows)
        noise_ref[channel] = noise[rows]
        previous_ref[channel] = previous[rows]


def on_device(
    latent,
    text_kv,
    modulation,
    qkv_weight,
    out_weight,
    patch_weight,
    final_weight,
    offsets,
    blend_weights,
    step_index,
):
    slab_cols, channels, row_count = latent.shape
    model_width = patch_weight.shape[1]
    half_attn = out_weight.shape[0]
    heads = half_attn // HEAD_DIM
    branches = text_kv.shape[0]
    col_pairs, row_couples = slab_cols, row_count // 2
    tokens = col_pairs * row_couples
    own_tokens = tokens // 2
    half_rows = row_count // 2
    far = swap_ring(latent, "win", 1)
    near = swap_ring(latent, "win", 0)
    hbm = pl.BlockSpec(memory_space=pltpu.HBM)
    keep = functools.partial(pltpu.with_memory_space_constraint, memory_space=pltpu.HBM)
    weight = jnp.transpose(qkv_weight, (1, 2, 0)).reshape(3 * half_attn, model_width)
    text = jnp.transpose(text_kv, (0, 1, 3, 2))
    final = jnp.transpose(final_weight, (1, 0))

    bf16, f32 = jnp.bfloat16, jnp.float32
    shape = jax.ShapeDtypeStruct
    wide = 2 * channels * half_rows
    half_width = model_width // 2
    below, above = half_width // 128 * 128, -(-half_width // 128) * 128
    row_part, col_part, patch_wide, start, modulate, own, quarter = pl.pallas_call(
        prepare_kernel,
        out_shape=(
            shape((row_couples, above), f32),
            shape((col_pairs, model_width - below), f32),
            shape((2 * channels * row_count, model_width), bf16),
            shape((8, -(-3 * slab_cols // 128) * 128), jnp.int32),
            shape(modulation.shape[1:], f32),
            shape(latent.shape, f32),
            shape((half_attn // 4, model_width), bf16),
        ),
        grid_spec=pltpu.PrefetchScalarGridSpec(
            num_scalar_prefetch=2,
            grid=(1,),
            in_specs=[hbm] * 4,
            out_specs=(VM,) * 7,
            scratch_shapes=[
                pltpu.VMEM(patch_weight.shape, bf16),
                pltpu.SemaphoreType.DMA((4,)),
            ],
        ),
        name="prepare",
        compiler_params=pltpu.CompilerParams(vmem_limit_bytes=GRANT),
        cost_estimate=pl.CostEstimate(flops=10**7, bytes_accessed=10**6, transcendentals=10**5),
    )(step_index, offsets, *map(keep, (latent, patch_weight, modulation, out_weight)))
    other_weight = swap(quarter, "cfg")
    projected, embedded, text, sent = pl.pallas_call(
        project_kernel,
        out_shape=(
            shape((3 * heads, HEAD_DIM, tokens), bf16),
            shape((own_tokens, model_width), f32),
            shape(text.shape, bf16),
            shape((half_attn // 2, branches * own_tokens), bf16),
        ),
        in_specs=[VM] * 8 + [hbm] * 2,
        out_specs=(VM,) * 4,
        scratch_shapes=[
            pltpu.VMEM((3 * slab_cols, channels * row_count), f32),
            pltpu.VMEM(weight.shape, bf16),
            pltpu.SemaphoreType.DMA((2,)),
        ],
        name="project",
        compiler_params=pltpu.CompilerParams(vmem_limit_bytes=GRANT),
        cost_estimate=pl.CostEstimate(flops=2 * 10**9, bytes_accessed=8 * 10**6, transcendentals=10**6),
    )(
        start, modulate, near, own, far, row_part, col_part, patch_wide, keep(weight), keep(text)
    )
    early = swap(sent, "cfg")
    sent = pl.pallas_call(
        second_kernel,
        out_shape=shape((half_attn // 2, branches * own_tokens), bf16),
        in_specs=[VM] * 2,
        out_specs=VM,
        name="second",
        compiler_params=pltpu.CompilerParams(vmem_limit_bytes=GRANT),
        cost_estimate=pl.CostEstimate(flops=10**9, bytes_accessed=10**6, transcendentals=10**6),
    )(projected, text)
    late = swap(sent, "cfg")
    cross_weight = swap_across(other_weight, "win", 2)
    core_weight = swap_across(other_weight, "win", 1)
    core_cross_weight = swap_across(cross_weight, "win", 1)
    mixed = pl.pallas_call(
        attend_kernel,
        out_shape=shape((branches * own_tokens, model_width), bf16),
        in_specs=[VM] * 2 + [hbm],
        out_specs=VM,
        scratch_shapes=[pltpu.VMEM(out_weight.shape, bf16), pltpu.SemaphoreType.DMA],
        name="attend",
        compiler_params=pltpu.CompilerParams(vmem_limit_bytes=GRANT),
        cost_estimate=pl.CostEstimate(flops=10**9, bytes_accessed=8 * 10**6, transcendentals=10**6),
    )(projected, text, keep(out_weight))
    plan_values, rows = pl.pallas_call(
        coefficient_kernel,
        out_shape=(
            shape((8, -(-slab_cols // 128) * 128), f32),
            shape((channels * half_rows, slab_cols), f32),
        ),
        in_specs=[VM, VM],
        out_specs=(VM, VM),
        name="coefficient",
        compiler_params=pltpu.CompilerParams(vmem_limit_bytes=GRANT),
        cost_estimate=pl.CostEstimate(flops=10**5, bytes_accessed=10**5, transcendentals=10**4),
    )(start, own)
    to_near, center, to_far = pl.pallas_call(
        finish_kernel,
        out_shape=tuple(shape((slab_cols, wide), f32) for _ in range(3)),
        in_specs=[VM, SM] + [VM] * 10,
        out_specs=(VM, VM, VM),
        scratch_shapes=[
            pltpu.VMEM((3 * slab_cols + 8, wide), f32),
            pltpu.SMEM(start.shape, jnp.int32),
            pltpu.SemaphoreType.DMA,
        ],
        name="finish",
        compiler_params=pltpu.CompilerParams(vmem_limit_bytes=GRANT),
        cost_estimate=pl.CostEstimate(flops=10**9, bytes_accessed=4 * 10**6, transcendentals=10**3),
    )(
        start, blend_weights, modulate, embedded, mixed, early, late,
        other_weight, core_weight, cross_weight, core_cross_weight, final,
    )
    from_far = swap_ring(to_far, "win", 1)
    from_near = swap_ring(to_near, "win", 0)
    previous, noise = pl.pallas_call(
        blend_kernel,
        out_shape=tuple(shape((channels, half_rows, slab_cols), f32) for _ in range(2)),
        in_specs=[VM] * 5,
        out_specs=(VM, VM),
        name="blend",
        compiler_params=pltpu.CompilerParams(vmem_limit_bytes=GRANT),
    )(plan_values, center, from_near, from_far, rows)
    return (jnp.transpose(previous, (2, 0, 1)), jnp.transpose(noise, (2, 0, 1)))


def solution(mesh):
    in_specs = (
        P("win", None, None),
        P(None, None, None, "cfg"),
        P(),
        P(None, None, "cfg"),
        P("cfg", None),
        P(),
        P(),
        P("win"),
        P("win"),
        P(),
    )
    out_specs = (P("win", None, "cfg"), P("win", None, "cfg"))
    return jax.shard_map(
        on_device, mesh=mesh, in_specs=in_specs, out_specs=out_specs, check_vma=False
    )
```

```python
import functools
import math

import jax
import jax.numpy as jnp
from jax import lax
from jax.experimental import pallas as pl
from jax.experimental.pallas import tpu as pltpu
from jax.sharding import PartitionSpec as P


HEAD_DIM = 72
STEPS = 20


guidance_scale = 4.5
plan_length = 1000
norm_eps = 1e-06

VM = pl.BlockSpec(memory_space=pltpu.VMEM)
SM = pl.BlockSpec(memory_space=pltpu.SMEM)
GRANT = 24 * 2**20


def swap_ring(array, axis, odd):
    size = lax.axis_size(axis)
    pairs = []
    for left in range(odd, size, 2):
        right = (left + 1) % size
        pairs += [(left, right), (right, left)]
    return lax.ppermute(array, axis, pairs)


def swap(array, axis):
    return lax.ppermute(array, axis, [(0, 1), (1, 0)])


def swap_across(array, axis, step):
    size = lax.axis_size(axis)
    return lax.ppermute(array, axis, [(place, place ^ step) for place in range(size)])


def layer_norm(values):
    average = jnp.mean(values, axis=-1, keepdims=True)
    centered = values - average
    variance = jnp.mean(centered * centered, axis=-1, keepdims=True)
    return centered * lax.rsqrt(variance + norm_eps)


def repeat_pairs(weight, repeats):
    rows, width = weight.shape
    values = weight.astype(jnp.float32)
    even = lax.broadcasted_iota(jnp.int32, (2 * repeats, width), 0) % 2 == 0
    parts = []
    for pair in range(rows // 2):
        parts.append(
            jnp.where(even, values[2 * pair : 2 * pair + 1, :], values[2 * pair + 1 : 2 * pair + 2, :])
        )
    return jnp.concatenate(parts, axis=0).astype(jnp.bfloat16)


def prepare_kernel(
    latent_source,
    patch_source,
    modulation_ref,
    out_source,
    row_ref,
    col_ref,
    patch_wide_ref,
    modulation_copy,
    latent_copy,
    quarter_copy,
    patch_ref,
    semaphores,
):
    count = quarter_copy.shape[0]
    quarter_first = pl.multiple_of(lax.axis_index("win") % 4 * count, 8)
    copies = [
        pltpu.make_async_copy(source, target, semaphores.at[place])
        for place, (source, target) in enumerate(
            (
                (patch_source, patch_ref),
                (modulation_ref, modulation_copy),
                (latent_source, latent_copy),
                (out_source.at[pl.ds(quarter_first, count)], quarter_copy),
            )
        )
    ]
    for copy in copies:
        copy.start()
    _, _, row_count = latent_copy.shape
    model_width = patch_ref.shape[1]
    quarter = model_width // 4

    def table(target_ref, first):
        count, lanes = target_ref.shape
        lane = first + lax.broadcasted_iota(jnp.int32, (count, lanes), 1)
        place = lax.broadcasted_iota(jnp.int32, (count, lanes), 0).astype(jnp.float32)
        frequency = jnp.exp(-math.log(10000.0) * (lane % quarter).astype(jnp.float32) / quarter)
        phase = jnp.where(lane // quarter % 2 == 0, 0.0, 0.5 * math.pi)
        target_ref[...] = jnp.sin(place * frequency + phase)

    table(row_ref, 0)
    table(col_ref, model_width - col_ref.shape[1])
    copies[0].wait()
    patch_wide_ref[...] = repeat_pairs(patch_ref[...], row_count // 2)
    for copy in copies[1:]:
        copy.wait()


def coefficient_kernel(step_ref, latent_ref, plan_ref, rows_ref):
    _, channels, row_count = latent_ref.shape
    moment = step_ref[0]
    index = lax.broadcasted_iota(jnp.int32, (8, 128), 0) * 128 + lax.broadcasted_iota(
        jnp.int32, (8, 128), 1
    )
    train = jnp.minimum(index, plan_length - 1).astype(jnp.float32)
    beta_values = 0.0001 + (0.02 - 0.0001) * train / (plan_length - 1)
    logs = jnp.log(1.0 - beta_values)

    def alpha_bar(last):
        kept = jnp.where((index <= last) & (index < plan_length), logs, 0.0)
        kept = jnp.sum(jnp.sum(kept, axis=0, keepdims=True), axis=1, keepdims=True)
        return jnp.exp(kept)

    alpha_now = alpha_bar(moment)
    alpha_before = alpha_bar(moment - plan_length // STEPS)
    for place, value in enumerate(
        (
            jnp.sqrt(alpha_before),
            jnp.sqrt(1.0 - alpha_now),
            jnp.sqrt(alpha_now),
            jnp.sqrt(1.0 - alpha_before),
        )
    ):
        plan_ref[place : place + 1, :] = jnp.broadcast_to(value, (1, plan_ref.shape[1]))

    half_rows = row_count // 2
    side = lax.axis_index("cfg")
    for channel in range(channels):
        turned = jnp.transpose(latent_ref[:, channel, :], (1, 0))
        rows_ref[channel * half_rows : (channel + 1) * half_rows, :] = jnp.where(
            side == 0, turned[:half_rows], turned[half_rows:]
        )


def first_pair():
    return lax.axis_index("win") % 4 // 2


def attend(parts, text_ref, first, count, chosen, finished):
    branches = text_ref.shape[0]
    feature = (((0,), (0,)), ((), ()))

    def place_of(head):
        pair = first_pair() if head < 2 else 1 - first_pair()
        return 2 * pair + head % 2

    def score(head):
        queries = parts[head // 2][head % 2, :, pl.ds(first, count)]
        return [
            lax.dot_general(keys, queries, feature, preferred_element_type=jnp.float32)
            for keys in [parts[head // 2][2 + head % 2]]
            + [text_ref[branch, 0, place_of(head)] for branch in range(branches)]
        ]

    def weigh(scores):
        own_highest = jnp.max(scores[0], axis=0, keepdims=True)
        own_exp = jnp.exp2(scores[0] - own_highest)
        own = (own_exp.astype(jnp.bfloat16), jnp.sum(own_exp, axis=0, keepdims=True))
        texts = []
        for text_scores in scores[1:]:
            highest = jnp.maximum(own_highest, jnp.max(text_scores, axis=0, keepdims=True))
            text_exp = jnp.exp2(text_scores - highest)
            lowered = jnp.exp2(own_highest - highest)
            total = lowered * own[1] + jnp.sum(text_exp, axis=0, keepdims=True)
            texts.append((text_exp.astype(jnp.bfloat16), lowered, 1.0 / total))
        return own[0], texts

    def mix(head, own_exp, texts):
        own_mix = jnp.dot(
            parts[head // 2][4 + head % 2], own_exp, preferred_element_type=jnp.float32
        )
        results = []
        for branch, (text_exp, lowered, inverse) in enumerate(texts):
            text_mix = jnp.dot(
                text_ref[branch, 1, place_of(head)], text_exp, preferred_element_type=jnp.float32
            )
            results.append((lowered * own_mix + text_mix) * inverse)
        return jnp.concatenate(results, axis=1)

    chosen = list(chosen)
    mixed = []

    def take(place, weights):
        mixed.append(mix(chosen[place], *weights))
        if place % 2:
            finished(place // 2, jnp.concatenate(mixed[-2:], axis=0).astype(jnp.bfloat16))

    ahead = score(chosen[0])
    before = None
    for place, head in enumerate(chosen):
        scores = ahead
        if place + 1 < len(chosen):
            ahead = score(chosen[place + 1])
        weights = weigh(scores)
        if before is not None:
            take(place - 1, before)
        before = weights
    take(len(chosen) - 1, before)


def keep_pair(target_ref, place, pair):
    target_ref[...] = pair


def weight_copies(weight_source, weight_ref, half, semaphores):
    count = weight_ref.shape[0] // 3
    total = weight_source.shape[0] // 3
    return [
        pltpu.make_async_copy(
            weight_source.at[pl.ds(pl.multiple_of(kind * total + half * count, 16), count)],
            weight_ref.at[pl.ds(kind * count, count)],
            semaphores.at[kind],
        )
        for kind in range(3)
    ]


def project_half(weight_ref, normed, target_ref, lanes):
    projected = lax.dot_general(
        weight_ref[...], normed, (((1,), (1,)), ((), ())), preferred_element_type=jnp.float32
    )
    for block in range(target_ref.shape[0]):
        part = projected[block * HEAD_DIM : (block + 1) * HEAD_DIM]
        if block < target_ref.shape[0] // 3:
            part = part * (math.log2(math.e) / math.sqrt(HEAD_DIM))
        target_ref[block, :, lanes] = part.astype(jnp.bfloat16)


def project_kernel(
    step_ref,
    offset_ref,
    modulations_ref,
    near_ref,
    own_ref,
    far_ref,
    row_ref,
    col_ref,
    patch_ref,
    weight_source,
    text_source,
    proj_ref,
    normed_ref,
    modulation_ref,
    embedded_ref,
    text_ref,
    late_weight_ref,
    sent_ref,
    extended_ref,
    weight_ref,
    semaphores,
):
    pair = first_pair()
    copies = weight_copies(weight_source, weight_ref, pair, semaphores.at[pl.ds(0, 3)])
    late_copies = weight_copies(
        weight_source, late_weight_ref, 1 - pair, semaphores.at[pl.ds(3, 3)]
    )
    text_copy = pltpu.make_async_copy(text_source, text_ref, semaphores.at[6])
    for copy in copies + [text_copy] + late_copies:
        copy.start()
    modulation_ref[...] = modulations_ref[step_ref[0] * STEPS // plan_length]
    slab_cols, channels, row_count = own_ref.shape
    col_pairs, row_couples = slab_cols, row_count // 2
    tokens = col_pairs * row_couples
    own_tokens = tokens // 2
    wide = 2 * channels * row_count
    even = lax.axis_index("win") % 2 == 0
    for channel in range(channels):
        near, far = near_ref[:, channel, :], far_ref[:, channel, :]
        values = (jnp.where(even, far, near), own_ref[:, channel, :], jnp.where(even, near, far))
        for place, value in enumerate(values):
            extended_ref[
                place * slab_cols : (place + 1) * slab_cols,
                channel * row_count : (channel + 1) * row_count,
            ] = value
    extended = extended_ref[...].astype(jnp.bfloat16)
    start_at = slab_cols - offset_ref[0]
    chosen = lax.broadcasted_iota(jnp.int32, (2 * col_pairs, 3 * slab_cols), 0)
    column = lax.broadcasted_iota(jnp.int32, (2 * col_pairs, 3 * slab_cols), 1)
    target = jnp.where(
        chosen < col_pairs, 2 * chosen, 2 * (chosen - col_pairs) + 1
    )
    pick = jnp.where(column == target + start_at, 1.0, 0.0).astype(jnp.bfloat16)
    picked = jnp.dot(pick, extended, preferred_element_type=jnp.float32)
    picked = jnp.concatenate([picked[:col_pairs], picked[col_pairs:]], axis=1)
    lane_couple = lax.broadcasted_iota(jnp.int32, (col_pairs, wide), 1) % row_count // 2
    spread = jnp.concatenate(
        [jnp.where(lane_couple == couple, picked, 0.0) for couple in range(row_couples)], axis=0
    ).astype(jnp.bfloat16)
    side = lax.axis_index("cfg")
    chunks = [slice(place * own_tokens, (place + 1) * own_tokens) for place in range(2)]

    couples = row_couples // 2
    model_width = patch_ref.shape[1]
    below, above = model_width - col_ref.shape[1], row_ref.shape[1]
    is_row = below + lax.broadcasted_iota(jnp.int32, (col_pairs, above - below), 1)
    is_row = is_row < model_width // 2

    def position(couple):
        line = jnp.broadcast_to(row_ref[couple : couple + 1, :], (col_pairs, above))
        column = col_ref[...]
        both = jnp.where(is_row, line[:, below:], column[:, : above - below])
        return jnp.concatenate([line[:, :below], both, column[:, above - below :]], axis=1)

    def embed(place):
        chunk = chunks[place]
        embedded = jnp.dot(spread[chunk], patch_ref[...], preferred_element_type=jnp.float32)
        embedded = embedded + jnp.concatenate(
            [position(couple) for couple in range(row_couples)[place * couples :][:couples]], axis=0
        )

        @pl.when(side == place)
        def _():
            embedded_ref[...] = embedded

        return embedded

    def norm(embedded):
        return (
            layer_norm(embedded) * (1.0 + modulation_ref[1:2, :]) + modulation_ref[0:1, :]
        ).astype(jnp.bfloat16)

    normed = norm(embed(0))
    later = embed(1)
    for copy in copies:
        copy.wait()
    normed_ref[chunks[0], :] = normed
    project_half(weight_ref, normed, proj_ref, chunks[0])
    normed = norm(later)
    normed_ref[chunks[1], :] = normed
    project_half(weight_ref, normed, proj_ref, chunks[1])
    first = pl.multiple_of((1 - side) * own_tokens, own_tokens)
    text_copy.wait()
    attend(
        [proj_ref], text_ref, first, own_tokens, range(2), functools.partial(keep_pair, sent_ref)
    )
    for copy in late_copies:
        copy.wait()


def second_kernel(
    normed_ref, text_ref, weight_ref, out_source, proj_ref, out_ref, sent_ref, semaphore
):
    out_copy = pltpu.make_async_copy(out_source, out_ref, semaphore)
    out_copy.start()
    own_tokens = normed_ref.shape[0] // 2
    for place in range(2):
        chunk = slice(place * own_tokens, (place + 1) * own_tokens)
        project_half(weight_ref, normed_ref[chunk, :], proj_ref, chunk)
    first = pl.multiple_of((1 - lax.axis_index("cfg")) * own_tokens, own_tokens)
    attend(
        [None, proj_ref], text_ref, first, own_tokens, range(2, 4),
        functools.partial(keep_pair, sent_ref),
    )
    out_copy.wait()


def attend_kernel(early_ref, late_ref, text_ref, weight_ref, mixed_ref):
    tokens = early_ref.shape[2]
    own_tokens = tokens // 2
    first = pl.multiple_of(lax.axis_index("cfg") * own_tokens, own_tokens)
    pairs = []

    def finished(place, pair):
        pairs.append(pair)

    attend([early_ref, late_ref], text_ref, first, own_tokens, range(4), finished)
    count = 2 * HEAD_DIM
    mixed = []
    for place, pair in enumerate(pairs):
        chosen = first_pair() if place == 0 else 1 - first_pair()
        rows = pl.ds(pl.multiple_of(chosen * count, count), count)
        mixed.append(contract(pair, weight_ref[rows, :]))
    mixed_ref[...] = mixed[0] + mixed[1]


def contract(features, weight):
    return lax.dot_general(
        features, weight, (((0,), (0,)), ((), ())), preferred_element_type=jnp.float32
    )


def join(mine_ref, neighbour_ref):
    mine, neighbour = mine_ref[...].astype(jnp.float32), neighbour_ref[...].astype(jnp.float32)
    even_place = lax.axis_index("win") % 2 == 0
    first = jnp.where(even_place, mine, neighbour)
    second = jnp.where(even_place, neighbour, mine)
    return jnp.concatenate([first, second], axis=0).astype(jnp.bfloat16)


def partial_kernel(mixed_ref, early_ref, weight_ref, core_ref, summed_ref):
    summed_ref[...] = mixed_ref[...] + contract(early_ref[...], join(weight_ref, core_ref))


def finish_kernel(
    offset_ref,
    blend_ref,
    modulation_ref,
    embedded_ref,
    mixed_ref,
    late_ref,
    cross_ref,
    core_cross_ref,
    final_ref,
    near_ref,
    center_ref,
    far_ref,
    buffer_ref,
):
    even_place = lax.axis_index("win") % 2 == 0
    other = contract(late_ref[...], join(cross_ref, core_cross_ref))
    slab_cols = center_ref.shape[0]
    col_pairs = slab_cols
    own_tokens = embedded_ref.shape[0]
    couples = own_tokens // col_pairs
    final_wide = repeat_pairs(final_ref[...], couples)
    wide = final_wide.shape[0]
    predicted = []
    for branch in range(2):
        rows = slice(branch * own_tokens, (branch + 1) * own_tokens)
        mixed = mixed_ref[rows, :] + other[rows]
        residual = embedded_ref[...] + modulation_ref[2:3, :] * mixed
        final_norm = (layer_norm(residual) * (1.0 + modulation_ref[3:4, :])).astype(jnp.bfloat16)
        predicted.append(
            lax.dot_general(
                final_norm,
                final_wide,
                (((1,), (1,)), ((), ())),
                preferred_element_type=jnp.float32,
            )
        )
    conditional, unconditional = predicted
    guided = unconditional + guidance_scale * (conditional - unconditional)
    lane_couple = lax.broadcasted_iota(jnp.int32, (col_pairs, wide), 1) % (2 * couples) // 2
    pairs = jnp.zeros((col_pairs, wide), jnp.float32)
    for couple in range(couples):
        pairs = pairs + jnp.where(
            lane_couple == couple, guided[couple * col_pairs : (couple + 1) * col_pairs], 0.0
        )
    weight_value = blend_ref[0].astype(jnp.float32)
    half = wide // 2
    is_noise = lax.broadcasted_iota(jnp.int32, (col_pairs, wide), 1) < half
    even = jnp.where(is_noise, weight_value * pairs, weight_value)
    odd = jnp.where(is_noise, weight_value * pltpu.roll(pairs, half, 1), weight_value)
    start_at = slab_cols - offset_ref[0]
    buffer_ref[...] = jnp.zeros_like(buffer_ref)
    buffer_ref[pl.ds(start_at, col_pairs, stride=2), :] = even
    buffer_ref[pl.ds(start_at + 1, col_pairs, stride=2), :] = odd
    center_ref[...] = buffer_ref[slab_cols : 2 * slab_cols]
    left, right = buffer_ref[:slab_cols], buffer_ref[2 * slab_cols : 3 * slab_cols]
    near_ref[...] = jnp.where(even_place, right, left)
    far_ref[...] = jnp.where(even_place, left, right)


def blend_kernel(plan_ref, center_ref, near_ref, far_ref, rows_ref, previous_ref, noise_ref):
    channels, half_rows, slab_cols = noise_ref.shape
    total = jnp.transpose(center_ref[...] + near_ref[...] + far_ref[...], (1, 0))
    half = total.shape[0] // 2
    noise = total[:half] / total[half:]
    scale = plan_ref[:, :slab_cols]
    previous = (
        scale[0:1] * (rows_ref[...] - scale[1:2] * noise) / scale[2:3] + scale[3:4] * noise
    )
    for channel in range(channels):
        rows = slice(channel * half_rows, (channel + 1) * half_rows)
        noise_ref[channel] = noise[rows]
        previous_ref[channel] = previous[rows]


def on_device(
    latent,
    text_kv,
    modulation,
    qkv_weight,
    out_weight,
    patch_weight,
    final_weight,
    offsets,
    blend_weights,
    step_index,
):
    slab_cols, channels, row_count = latent.shape
    model_width = patch_weight.shape[1]
    half_attn = out_weight.shape[0]
    heads = half_attn // HEAD_DIM
    branches, caption = text_kv.shape[0], text_kv.shape[2]
    col_pairs, row_couples = slab_cols, row_count // 2
    tokens = col_pairs * row_couples
    own_tokens = tokens // 2
    half_rows = row_count // 2
    far = swap_ring(latent, "win", 1)
    near = swap_ring(latent, "win", 0)
    hbm = pl.BlockSpec(memory_space=pltpu.HBM)
    keep = functools.partial(pltpu.with_memory_space_constraint, memory_space=pltpu.HBM)
    weight = jnp.transpose(qkv_weight, (1, 2, 0)).reshape(3 * half_attn, model_width)
    text = jnp.transpose(text_kv, (0, 1, 3, 2)).reshape(branches, 2, heads, HEAD_DIM, caption)
    final = jnp.transpose(final_weight, (1, 0))

    bf16, f32 = jnp.bfloat16, jnp.float32
    shape = jax.ShapeDtypeStruct
    wide = 2 * channels * half_rows
    half_width = model_width // 2
    below, above = half_width // 128 * 128, -(-half_width // 128) * 128
    row_part, col_part, patch_wide, modulations, own, quarter = pl.pallas_call(
        prepare_kernel,
        out_shape=(
            shape((row_couples, above), f32),
            shape((col_pairs, model_width - below), f32),
            shape((2 * channels * row_count, model_width), bf16),
            shape(modulation.shape, f32),
            shape(latent.shape, f32),
            shape((half_attn // 4, model_width), bf16),
        ),
        in_specs=[hbm] * 4,
        out_specs=(VM,) * 6,
        scratch_shapes=[pltpu.VMEM(patch_weight.shape, bf16), pltpu.SemaphoreType.DMA((4,))],
        name="prepare",
        compiler_params=pltpu.CompilerParams(vmem_limit_bytes=GRANT),
        cost_estimate=pl.CostEstimate(flops=10**7, bytes_accessed=10**6, transcendentals=10**5),
    )(*map(keep, (latent, patch_weight, modulation, out_weight)))
    other_weight = swap(quarter, "cfg")
    projected, normed, modulate, embedded, text, late_weight, sent = pl.pallas_call(
        project_kernel,
        out_shape=(
            shape((3 * heads // 2, HEAD_DIM, tokens), bf16),
            shape((tokens, model_width), bf16),
            shape(modulation.shape[1:], f32),
            shape((own_tokens, model_width), f32),
            shape(text.shape, bf16),
            shape((weight.shape[0] // 2, model_width), bf16),
            shape((half_attn // 2, branches * own_tokens), bf16),
        ),
        in_specs=[SM, SM] + [VM] * 7 + [hbm] * 2,
        out_specs=(VM,) * 7,
        scratch_shapes=[
            pltpu.VMEM((3 * slab_cols, channels * row_count), f32),
            pltpu.VMEM((weight.shape[0] // 2, model_width), bf16),
            pltpu.SemaphoreType.DMA((7,)),
        ],
        name="project",
        compiler_params=pltpu.CompilerParams(vmem_limit_bytes=GRANT),
        cost_estimate=pl.CostEstimate(flops=2 * 10**9, bytes_accessed=8 * 10**6, transcendentals=10**6),
    )(
        step_index, offsets, modulations, near, own, far, row_part, col_part, patch_wide,
        keep(weight), keep(text),
    )
    early = swap(sent, "cfg")
    projected_late, own_weight, sent = pl.pallas_call(
        second_kernel,
        out_shape=(
            shape((3 * heads // 2, HEAD_DIM, tokens), bf16),
            shape(out_weight.shape, bf16),
            shape((half_attn // 2, branches * own_tokens), bf16),
        ),
        in_specs=[VM] * 3 + [hbm],
        out_specs=(VM,) * 3,
        scratch_shapes=[pltpu.SemaphoreType.DMA],
        name="second",
        compiler_params=pltpu.CompilerParams(vmem_limit_bytes=GRANT),
        cost_estimate=pl.CostEstimate(flops=10**9, bytes_accessed=10**6, transcendentals=10**6),
    )(normed, text, late_weight, keep(out_weight))
    late = swap(sent, "cfg")
    cross_weight = swap_across(other_weight, "win", 2)
    core_weight = swap_across(other_weight, "win", 1)
    core_cross_weight = swap_across(cross_weight, "win", 1)
    mixed = pl.pallas_call(
        attend_kernel,
        out_shape=shape((branches * own_tokens, model_width), f32),
        in_specs=[VM] * 4,
        out_specs=VM,
        name="attend",
        compiler_params=pltpu.CompilerParams(vmem_limit_bytes=GRANT),
        cost_estimate=pl.CostEstimate(flops=10**9, bytes_accessed=8 * 10**6, transcendentals=10**6),
    )(projected, projected_late, text, own_weight)
    mixed = pl.pallas_call(
        partial_kernel,
        out_shape=shape(mixed.shape, f32),
        in_specs=[VM] * 4,
        out_specs=VM,
        name="partial",
        compiler_params=pltpu.CompilerParams(vmem_limit_bytes=GRANT),
        cost_estimate=pl.CostEstimate(flops=2 * 10**8, bytes_accessed=10**6, transcendentals=0),
    )(mixed, early, other_weight, core_weight)
    plan_values, rows = pl.pallas_call(
        coefficient_kernel,
        out_shape=(
            shape((8, -(-slab_cols // 128) * 128), f32),
            shape((channels * half_rows, slab_cols), f32),
        ),
        in_specs=[SM, VM],
        out_specs=(VM, VM),
        name="coefficient",
        compiler_params=pltpu.CompilerParams(vmem_limit_bytes=GRANT),
        cost_estimate=pl.CostEstimate(flops=10**5, bytes_accessed=10**5, transcendentals=10**4),
    )(step_index, own)
    to_near, center, to_far = pl.pallas_call(
        finish_kernel,
        out_shape=tuple(shape((slab_cols, wide), f32) for _ in range(3)),
        in_specs=[SM, SM] + [VM] * 7,
        out_specs=(VM, VM, VM),
        scratch_shapes=[pltpu.VMEM((3 * slab_cols + 8, wide), f32)],
        name="finish",
        compiler_params=pltpu.CompilerParams(vmem_limit_bytes=GRANT),
        cost_estimate=pl.CostEstimate(flops=10**9, bytes_accessed=4 * 10**6, transcendentals=10**3),
    )(
        offsets, blend_weights, modulate, embedded, mixed, late,
        cross_weight, core_cross_weight, final,
    )
    from_far = swap_ring(to_far, "win", 1)
    from_near = swap_ring(to_near, "win", 0)
    previous, noise = pl.pallas_call(
        blend_kernel,
        out_shape=tuple(shape((channels, half_rows, slab_cols), f32) for _ in range(2)),
        in_specs=[VM] * 5,
        out_specs=(VM, VM),
        name="blend",
        compiler_params=pltpu.CompilerParams(vmem_limit_bytes=GRANT),
    )(plan_values, center, from_near, from_far, rows)
    return (jnp.transpose(previous, (2, 0, 1)), jnp.transpose(noise, (2, 0, 1)))


def solution(mesh):
    in_specs = (
        P("win", None, None),
        P(None, None, None, "cfg"),
        P(),
        P(None, None, "cfg"),
        P("cfg", None),
        P(),
        P(),
        P("win"),
        P("win"),
        P(),
    )
    out_specs = (P("win", None, "cfg"), P("win", None, "cfg"))
    return jax.shard_map(
        on_device, mesh=mesh, in_specs=in_specs, out_specs=out_specs, check_vma=False
    )
```

```python
import functools
import math

import jax
import jax.numpy as jnp
from jax import lax
from jax.experimental import pallas as pl
from jax.experimental.pallas import tpu as pltpu
from jax.sharding import PartitionSpec as P


HEAD_DIM = 72
STEPS = 20


guidance_scale = 4.5
plan_length = 1000
norm_eps = 1e-06

VM = pl.BlockSpec(memory_space=pltpu.VMEM)
SM = pl.BlockSpec(memory_space=pltpu.SMEM)
GRANT = 24 * 2**20


def swap_ring(array, axis, odd):
    size = lax.axis_size(axis)
    pairs = []
    for left in range(odd, size, 2):
        right = (left + 1) % size
        pairs += [(left, right), (right, left)]
    return lax.ppermute(array, axis, pairs)


def swap(array, axis):
    return lax.ppermute(array, axis, [(0, 1), (1, 0)])


def swap_across(array, axis, step):
    size = lax.axis_size(axis)
    return lax.ppermute(array, axis, [(place, place ^ step) for place in range(size)])


def layer_norm(values):
    average = jnp.mean(values, axis=-1, keepdims=True)
    centered = values - average
    variance = jnp.mean(centered * centered, axis=-1, keepdims=True)
    return centered * lax.rsqrt(variance + norm_eps)


def repeat_pairs(weight, repeats):
    rows, width = weight.shape
    values = weight.astype(jnp.float32)
    even = lax.broadcasted_iota(jnp.int32, (2 * repeats, width), 0) % 2 == 0
    parts = []
    for pair in range(rows // 2):
        parts.append(
            jnp.where(even, values[2 * pair : 2 * pair + 1, :], values[2 * pair + 1 : 2 * pair + 2, :])
        )
    return jnp.concatenate(parts, axis=0).astype(jnp.bfloat16)


def prepare_kernel(
    latent_source,
    patch_source,
    modulation_ref,
    out_source,
    row_ref,
    col_ref,
    patch_wide_ref,
    modulation_copy,
    latent_copy,
    quarter_copy,
    patch_ref,
    semaphores,
):
    count = quarter_copy.shape[0]
    quarter_first = pl.multiple_of(lax.axis_index("win") % 4 * count, 8)
    copies = [
        pltpu.make_async_copy(source, target, semaphores.at[place])
        for place, (source, target) in enumerate(
            (
                (patch_source, patch_ref),
                (modulation_ref, modulation_copy),
                (latent_source, latent_copy),
                (out_source.at[pl.ds(quarter_first, count)], quarter_copy),
            )
        )
    ]
    for copy in copies:
        copy.start()
    _, _, row_count = latent_copy.shape
    model_width = patch_ref.shape[1]
    quarter = model_width // 4

    def table(target_ref, first):
        count, lanes = target_ref.shape
        lane = first + lax.broadcasted_iota(jnp.int32, (count, lanes), 1)
        place = lax.broadcasted_iota(jnp.int32, (count, lanes), 0).astype(jnp.float32)
        frequency = jnp.exp(-math.log(10000.0) * (lane % quarter).astype(jnp.float32) / quarter)
        phase = jnp.where(lane // quarter % 2 == 0, 0.0, 0.5 * math.pi)
        target_ref[...] = jnp.sin(place * frequency + phase)

    table(row_ref, 0)
    table(col_ref, model_width - col_ref.shape[1])
    copies[0].wait()
    patch_wide_ref[...] = repeat_pairs(patch_ref[...], row_count // 2)
    for copy in copies[1:]:
        copy.wait()


def coefficient_kernel(step_ref, latent_ref, plan_ref, rows_ref):
    _, channels, row_count = latent_ref.shape
    moment = step_ref[0]
    index = lax.broadcasted_iota(jnp.int32, (8, 128), 0) * 128 + lax.broadcasted_iota(
        jnp.int32, (8, 128), 1
    )
    train = jnp.minimum(index, plan_length - 1).astype(jnp.float32)
    beta_values = 0.0001 + (0.02 - 0.0001) * train / (plan_length - 1)
    logs = jnp.log(1.0 - beta_values)

    def alpha_bar(last):
        kept = jnp.where((index <= last) & (index < plan_length), logs, 0.0)
        kept = jnp.sum(jnp.sum(kept, axis=0, keepdims=True), axis=1, keepdims=True)
        return jnp.exp(kept)

    alpha_now = alpha_bar(moment)
    alpha_before = alpha_bar(moment - plan_length // STEPS)
    for place, value in enumerate(
        (
            jnp.sqrt(alpha_before),
            jnp.sqrt(1.0 - alpha_now),
            jnp.sqrt(alpha_now),
            jnp.sqrt(1.0 - alpha_before),
        )
    ):
        plan_ref[place : place + 1, :] = jnp.broadcast_to(value, (1, plan_ref.shape[1]))

    half_rows = row_count // 2
    side = lax.axis_index("cfg")
    for channel in range(channels):
        turned = jnp.transpose(latent_ref[:, channel, :], (1, 0))
        rows_ref[channel * half_rows : (channel + 1) * half_rows, :] = jnp.where(
            side == 0, turned[:half_rows], turned[half_rows:]
        )


def first_pair():
    return lax.axis_index("win") % 4 // 2


def token_lanes(side, tokens):
    return [
        pl.multiple_of(half * (tokens // 2) + side * (tokens // 4), tokens // 4)
        for half in range(2)
    ]


def attend(parts, text_ref, first, count, chosen, finished):
    branches = text_ref.shape[0]
    feature = (((0,), (0,)), ((), ()))

    def place_of(head):
        pair = first_pair() if head < 2 else 1 - first_pair()
        return 2 * pair + head % 2

    def score(head):
        queries = jnp.concatenate(
            [parts[head // 2][head % 2, :, pl.ds(start, count // 2)] for start in first], axis=1
        )
        return [
            lax.dot_general(keys, queries, feature, preferred_element_type=jnp.float32)
            for keys in [parts[head // 2][2 + head % 2]]
            + [text_ref[branch, 0, place_of(head)] for branch in range(branches)]
        ]

    def weigh(scores):
        own_highest = jnp.max(scores[0], axis=0, keepdims=True)
        own_exp = jnp.exp2(scores[0] - own_highest)
        own = (own_exp.astype(jnp.bfloat16), jnp.sum(own_exp, axis=0, keepdims=True))
        texts = []
        for text_scores in scores[1:]:
            highest = jnp.maximum(own_highest, jnp.max(text_scores, axis=0, keepdims=True))
            text_exp = jnp.exp2(text_scores - highest)
            lowered = jnp.exp2(own_highest - highest)
            total = lowered * own[1] + jnp.sum(text_exp, axis=0, keepdims=True)
            texts.append((text_exp.astype(jnp.bfloat16), lowered, 1.0 / total))
        return own[0], texts

    def mix(head, own_exp, texts):
        own_mix = jnp.dot(
            parts[head // 2][4 + head % 2], own_exp, preferred_element_type=jnp.float32
        )
        results = []
        for branch, (text_exp, lowered, inverse) in enumerate(texts):
            text_mix = jnp.dot(
                text_ref[branch, 1, place_of(head)], text_exp, preferred_element_type=jnp.float32
            )
            results.append((lowered * own_mix + text_mix) * inverse)
        return jnp.concatenate(
            [result[:, : count // 2] for result in results]
            + [result[:, count // 2 :] for result in results],
            axis=1,
        )

    chosen = list(chosen)
    mixed = []

    def take(place, weights):
        mixed.append(mix(chosen[place], *weights))
        if place % 2:
            finished(place // 2, jnp.concatenate(mixed[-2:], axis=0).astype(jnp.bfloat16))

    ahead = score(chosen[0])
    before = None
    for place, head in enumerate(chosen):
        scores = ahead
        if place + 1 < len(chosen):
            ahead = score(chosen[place + 1])
        weights = weigh(scores)
        if before is not None:
            take(place - 1, before)
        before = weights
    take(len(chosen) - 1, before)


def keep_pair(target_ref, place, pair):
    target_ref[...] = pair


def weight_copies(weight_source, weight_ref, half, semaphores):
    count = weight_ref.shape[0] // 3
    total = weight_source.shape[0] // 3
    return [
        pltpu.make_async_copy(
            weight_source.at[pl.ds(pl.multiple_of(kind * total + half * count, 16), count)],
            weight_ref.at[pl.ds(kind * count, count)],
            semaphores.at[kind],
        )
        for kind in range(3)
    ]


def project_half(weight_ref, normed, target_ref, lanes):
    projected = lax.dot_general(
        weight_ref[...], normed, (((1,), (1,)), ((), ())), preferred_element_type=jnp.float32
    )
    for block in range(target_ref.shape[0]):
        part = projected[block * HEAD_DIM : (block + 1) * HEAD_DIM]
        if block < target_ref.shape[0] // 3:
            part = part * (math.log2(math.e) / math.sqrt(HEAD_DIM))
        target_ref[block, :, lanes] = part.astype(jnp.bfloat16)


def project_kernel(
    step_ref,
    offset_ref,
    modulations_ref,
    near_ref,
    own_ref,
    far_ref,
    row_ref,
    col_ref,
    patch_ref,
    weight_source,
    text_source,
    proj_ref,
    normed_ref,
    modulation_ref,
    embedded_ref,
    text_ref,
    late_weight_ref,
    sent_ref,
    extended_ref,
    weight_ref,
    semaphores,
):
    pair = first_pair()
    copies = weight_copies(weight_source, weight_ref, pair, semaphores.at[pl.ds(0, 3)])
    late_copies = weight_copies(
        weight_source, late_weight_ref, 1 - pair, semaphores.at[pl.ds(3, 3)]
    )
    text_copy = pltpu.make_async_copy(text_source, text_ref, semaphores.at[6])
    for copy in copies + [text_copy] + late_copies:
        copy.start()
    modulation_ref[...] = modulations_ref[step_ref[0] * STEPS // plan_length]
    slab_cols, channels, row_count = own_ref.shape
    col_pairs, row_couples = slab_cols, row_count // 2
    tokens = col_pairs * row_couples
    own_tokens = tokens // 2
    wide = 2 * channels * row_count
    even = lax.axis_index("win") % 2 == 0
    for channel in range(channels):
        near, far = near_ref[:, channel, :], far_ref[:, channel, :]
        values = (jnp.where(even, far, near), own_ref[:, channel, :], jnp.where(even, near, far))
        for place, value in enumerate(values):
            extended_ref[
                place * slab_cols : (place + 1) * slab_cols,
                channel * row_count : (channel + 1) * row_count,
            ] = value
    extended = extended_ref[...].astype(jnp.bfloat16)
    start_at = slab_cols - offset_ref[0]
    chosen = lax.broadcasted_iota(jnp.int32, (2 * col_pairs, 3 * slab_cols), 0)
    column = lax.broadcasted_iota(jnp.int32, (2 * col_pairs, 3 * slab_cols), 1)
    half_pairs = col_pairs // 2
    parity = lax.axis_index("win") % 2
    near_first, far_first = (1 - parity) * half_pairs, parity * half_pairs
    group, within = chosen // half_pairs, chosen % half_pairs
    target = 2 * (within + jnp.where(group < 2, near_first, far_first)) + group % 2
    pick = jnp.where(column == target + start_at, 1.0, 0.0).astype(jnp.bfloat16)
    picked = jnp.dot(pick, extended, preferred_element_type=jnp.float32)
    groups = [picked[place * half_pairs : (place + 1) * half_pairs] for place in range(4)]
    lane_couple = lax.broadcasted_iota(jnp.int32, (half_pairs, wide), 1) % row_count // 2
    spread = []
    for place in range(2):
        pair = jnp.concatenate(groups[2 * place : 2 * place + 2], axis=1)
        spread.append(
            jnp.concatenate(
                [jnp.where(lane_couple == couple, pair, 0.0) for couple in range(row_couples)],
                axis=0,
            ).astype(jnp.bfloat16)
        )
    side = lax.axis_index("cfg")
    chunks = [slice(place * own_tokens, (place + 1) * own_tokens) for place in range(2)]

    model_width = patch_ref.shape[1]
    below, above = model_width - col_ref.shape[1], row_ref.shape[1]
    is_row = below + lax.broadcasted_iota(jnp.int32, (half_pairs, above - below), 1)
    is_row = is_row < model_width // 2

    def position(place, couple):
        line = jnp.broadcast_to(row_ref[couple : couple + 1, :], (half_pairs, above))
        column_first = near_first if place == 0 else far_first
        column = col_ref[pl.ds(pl.multiple_of(column_first, half_pairs), half_pairs), :]
        both = jnp.where(is_row, line[:, below:], column[:, : above - below])
        return jnp.concatenate([line[:, :below], both, column[:, above - below :]], axis=1)

    gain, shift = 1.0 + modulation_ref[1:2, :], modulation_ref[0:1, :]

    def embed(place):
        return jnp.dot(spread[place], patch_ref[...], preferred_element_type=jnp.float32)

    def norm(place, patches):
        for first_couple in range(0, row_couples, 2):
            rows = slice(first_couple * half_pairs, (first_couple + 2) * half_pairs)
            target = slice(place * own_tokens + rows.start, place * own_tokens + rows.stop)
            embedded = patches[rows] + jnp.concatenate(
                [position(place, first_couple + next_) for next_ in range(2)], axis=0
            )
            embedded_ref[target, :] = embedded
            normed = layer_norm(embedded) * gain + shift
            normed_ref[target, :] = normed.astype(jnp.bfloat16)

    early = embed(0)
    later = embed(1)
    norm(0, early)
    for copy in copies:
        copy.wait()
    project_half(weight_ref, normed_ref[chunks[0], :], proj_ref, chunks[0])
    norm(1, later)
    project_half(weight_ref, normed_ref[chunks[1], :], proj_ref, chunks[1])
    first = token_lanes(1 - side, tokens)
    text_copy.wait()
    attend(
        [proj_ref], text_ref, first, own_tokens, range(2), functools.partial(keep_pair, sent_ref)
    )
    for copy in late_copies:
        copy.wait()


def second_kernel(
    normed_ref, text_ref, weight_ref, out_source, proj_ref, out_ref, sent_ref, semaphore
):
    out_copy = pltpu.make_async_copy(out_source, out_ref, semaphore)
    out_copy.start()
    own_tokens = normed_ref.shape[0] // 2
    for place in range(2):
        chunk = slice(place * own_tokens, (place + 1) * own_tokens)
        project_half(weight_ref, normed_ref[chunk, :], proj_ref, chunk)
    first = token_lanes(1 - lax.axis_index("cfg"), 2 * own_tokens)
    attend(
        [None, proj_ref], text_ref, first, own_tokens, range(2, 4),
        functools.partial(keep_pair, sent_ref),
    )
    out_copy.wait()


def attend_kernel(early_ref, late_ref, text_ref, weight_ref, mixed_ref):
    tokens = early_ref.shape[2]
    own_tokens = tokens // 2
    first = token_lanes(lax.axis_index("cfg"), tokens)
    pairs = []

    def finished(place, pair):
        pairs.append(pair)

    attend([early_ref, late_ref], text_ref, first, own_tokens, range(4), finished)
    count = 2 * HEAD_DIM
    mixed = []
    for place, pair in enumerate(pairs):
        chosen = first_pair() if place == 0 else 1 - first_pair()
        rows = pl.ds(pl.multiple_of(chosen * count, count), count)
        mixed.append(contract(pair, weight_ref[rows, :]))
    mixed_ref[...] = mixed[0] + mixed[1]


def contract(features, weight):
    return lax.dot_general(
        features, weight, (((0,), (0,)), ((), ())), preferred_element_type=jnp.float32
    )


def join(mine_ref, neighbour_ref):
    mine, neighbour = mine_ref[...].astype(jnp.float32), neighbour_ref[...].astype(jnp.float32)
    even_place = lax.axis_index("win") % 2 == 0
    first = jnp.where(even_place, mine, neighbour)
    second = jnp.where(even_place, neighbour, mine)
    return jnp.concatenate([first, second], axis=0).astype(jnp.bfloat16)


def join_kernel(mine_ref, neighbour_ref, joined_ref):
    joined_ref[...] = join(mine_ref, neighbour_ref)


def partial_kernel(mixed_ref, early_ref, weight_ref, core_ref, summed_ref):
    summed_ref[...] = mixed_ref[...] + contract(early_ref[...], join(weight_ref, core_ref))


def finish_kernel(
    half,
    offset_ref,
    blend_ref,
    modulation_ref,
    embedded_ref,
    mixed_ref,
    late_ref,
    weight_ref,
    final_ref,
    sent_ref,
    center_ref,
    buffer_ref,
    final_norm_ref,
):
    slab_cols, wide = center_ref.shape
    half_pairs = slab_cols // 2
    count = embedded_ref.shape[0] // 4
    couples = count // half_pairs
    final_wide = repeat_pairs(final_ref[...], couples)
    gate, gain = modulation_ref[2:3, :], 1.0 + modulation_ref[3:4, :]
    side_first = pl.multiple_of(half * 2 * count + lax.axis_index("cfg") * count, count)
    lanes = slice(half * 2 * count, (half + 1) * 2 * count)
    other = contract(late_ref[:, lanes], weight_ref[...])
    predicted = []
    block = slab_cols
    for branch in range(2):
        for place in range(count // block):
            rows = slice(branch * count + place * block, branch * count + (place + 1) * block)
            mixed = mixed_ref[lanes.start + rows.start : lanes.start + rows.stop, :] + other[rows]
            embedded = embedded_ref[pl.ds(side_first + place * block, block), :]
            residual = embedded + gate * mixed
            final_norm_ref[rows, :] = (layer_norm(residual) * gain).astype(jnp.bfloat16)
        rows = slice(branch * count, (branch + 1) * count)
        predicted.append(
            lax.dot_general(
                final_norm_ref[rows, :],
                final_wide,
                (((1,), (1,)), ((), ())),
                preferred_element_type=jnp.float32,
            )
        )
    conditional, unconditional = predicted
    guided = unconditional + guidance_scale * (conditional - unconditional)
    lane_couple = lax.broadcasted_iota(jnp.int32, (half_pairs, wide), 1) % (2 * couples) // 2
    pairs = jnp.zeros((half_pairs, wide), jnp.float32)
    for couple in range(couples):
        pairs = pairs + jnp.where(
            lane_couple == couple, guided[couple * half_pairs : (couple + 1) * half_pairs], 0.0
        )
    weight_value = blend_ref[0].astype(jnp.float32)
    is_noise = lax.broadcasted_iota(jnp.int32, (half_pairs, wide), 1) < wide // 2
    even = jnp.where(is_noise, weight_value * pairs, weight_value)
    odd = jnp.where(is_noise, weight_value * pltpu.roll(pairs, wide // 2, 1), weight_value)
    parity = lax.axis_index("win") % 2
    right = 1 - parity if half == 0 else parity
    start_at = slab_cols - offset_ref[0] + right * slab_cols
    buffer_ref[...] = jnp.zeros_like(buffer_ref)
    buffer_ref[pl.ds(start_at, half_pairs, stride=2), :] = even
    buffer_ref[pl.ds(start_at + 1, half_pairs, stride=2), :] = odd
    center_ref[...] = buffer_ref[slab_cols : 2 * slab_cols]
    sent_ref[...] = jnp.where(
        right == 1, buffer_ref[2 * slab_cols : 3 * slab_cols], buffer_ref[:slab_cols]
    )


def blend_kernel(
    plan_ref, center_ref, near_ref, far_center_ref, far_ref, rows_ref, previous_ref, noise_ref
):
    channels, half_rows, slab_cols = noise_ref.shape
    total = (center_ref[...] + near_ref[...]) + (far_center_ref[...] + far_ref[...])
    total = jnp.transpose(total, (1, 0))
    half = total.shape[0] // 2
    noise = total[:half] / total[half:]
    scale = plan_ref[:, :slab_cols]
    previous = (
        scale[0:1] * (rows_ref[...] - scale[1:2] * noise) / scale[2:3] + scale[3:4] * noise
    )
    for channel in range(channels):
        rows = slice(channel * half_rows, (channel + 1) * half_rows)
        noise_ref[channel] = noise[rows]
        previous_ref[channel] = previous[rows]


def on_device(
    latent,
    text_kv,
    modulation,
    qkv_weight,
    out_weight,
    patch_weight,
    final_weight,
    offsets,
    blend_weights,
    step_index,
):
    slab_cols, channels, row_count = latent.shape
    model_width = patch_weight.shape[1]
    half_attn = out_weight.shape[0]
    heads = half_attn // HEAD_DIM
    branches, caption = text_kv.shape[0], text_kv.shape[2]
    col_pairs, row_couples = slab_cols, row_count // 2
    tokens = col_pairs * row_couples
    own_tokens = tokens // 2
    half_rows = row_count // 2
    far = swap_ring(latent, "win", 1)
    near = swap_ring(latent, "win", 0)
    hbm = pl.BlockSpec(memory_space=pltpu.HBM)
    keep = functools.partial(pltpu.with_memory_space_constraint, memory_space=pltpu.HBM)
    weight = jnp.transpose(qkv_weight, (1, 2, 0)).reshape(3 * half_attn, model_width)
    text = jnp.transpose(text_kv, (0, 1, 3, 2)).reshape(branches, 2, heads, HEAD_DIM, caption)
    final = jnp.transpose(final_weight, (1, 0))

    bf16, f32 = jnp.bfloat16, jnp.float32
    shape = jax.ShapeDtypeStruct
    wide = 2 * channels * half_rows
    half_width = model_width // 2
    below, above = half_width // 128 * 128, -(-half_width // 128) * 128
    row_part, col_part, patch_wide, modulations, own, quarter = pl.pallas_call(
        prepare_kernel,
        out_shape=(
            shape((row_couples, above), f32),
            shape((col_pairs, model_width - below), f32),
            shape((2 * channels * row_count, model_width), bf16),
            shape(modulation.shape, f32),
            shape(latent.shape, f32),
            shape((half_attn // 4, model_width), bf16),
        ),
        in_specs=[hbm] * 4,
        out_specs=(VM,) * 6,
        scratch_shapes=[pltpu.VMEM(patch_weight.shape, bf16), pltpu.SemaphoreType.DMA((4,))],
        name="prepare",
        compiler_params=pltpu.CompilerParams(vmem_limit_bytes=GRANT),
        cost_estimate=pl.CostEstimate(flops=10**7, bytes_accessed=10**6, transcendentals=10**5),
    )(*map(keep, (latent, patch_weight, modulation, out_weight)))
    other_weight = swap(quarter, "cfg")
    projected, normed, modulate, embedded, text, late_weight, sent = pl.pallas_call(
        project_kernel,
        out_shape=(
            shape((3 * heads // 2, HEAD_DIM, tokens), bf16),
            shape((tokens, model_width), bf16),
            shape(modulation.shape[1:], f32),
            shape((tokens, model_width), f32),
            shape(text.shape, bf16),
            shape((weight.shape[0] // 2, model_width), bf16),
            shape((half_attn // 2, branches * own_tokens), bf16),
        ),
        in_specs=[SM, SM] + [VM] * 7 + [hbm] * 2,
        out_specs=(VM,) * 7,
        scratch_shapes=[
            pltpu.VMEM((3 * slab_cols, channels * row_count), f32),
            pltpu.VMEM((weight.shape[0] // 2, model_width), bf16),
            pltpu.SemaphoreType.DMA((7,)),
        ],
        name="project",
        compiler_params=pltpu.CompilerParams(vmem_limit_bytes=GRANT),
        cost_estimate=pl.CostEstimate(flops=2 * 10**9, bytes_accessed=8 * 10**6, transcendentals=10**6),
    )(
        step_index, offsets, modulations, near, own, far, row_part, col_part, patch_wide,
        keep(weight), keep(text),
    )
    early = swap(sent, "cfg")
    projected_late, own_weight, sent = pl.pallas_call(
        second_kernel,
        out_shape=(
            shape((3 * heads // 2, HEAD_DIM, tokens), bf16),
            shape(out_weight.shape, bf16),
            shape((half_attn // 2, branches * own_tokens), bf16),
        ),
        in_specs=[VM] * 3 + [hbm],
        out_specs=(VM,) * 3,
        scratch_shapes=[pltpu.SemaphoreType.DMA],
        name="second",
        compiler_params=pltpu.CompilerParams(vmem_limit_bytes=GRANT),
        cost_estimate=pl.CostEstimate(flops=10**9, bytes_accessed=10**6, transcendentals=10**6),
    )(normed, text, late_weight, keep(out_weight))
    late = swap(sent, "cfg")
    cross_weight = swap_across(other_weight, "win", 2)
    core_weight = swap_across(other_weight, "win", 1)
    core_cross_weight = swap_across(cross_weight, "win", 1)
    mixed = pl.pallas_call(
        attend_kernel,
        out_shape=shape((branches * own_tokens, model_width), f32),
        in_specs=[VM] * 4,
        out_specs=VM,
        name="attend",
        compiler_params=pltpu.CompilerParams(vmem_limit_bytes=GRANT),
        cost_estimate=pl.CostEstimate(flops=10**9, bytes_accessed=8 * 10**6, transcendentals=10**6),
    )(projected, projected_late, text, own_weight)
    mixed = pl.pallas_call(
        partial_kernel,
        out_shape=shape(mixed.shape, f32),
        in_specs=[VM] * 4,
        out_specs=VM,
        name="partial",
        compiler_params=pltpu.CompilerParams(vmem_limit_bytes=GRANT),
        cost_estimate=pl.CostEstimate(flops=2 * 10**8, bytes_accessed=10**6, transcendentals=0),
    )(mixed, early, other_weight, core_weight)
    plan_values, rows = pl.pallas_call(
        coefficient_kernel,
        out_shape=(
            shape((8, -(-slab_cols // 128) * 128), f32),
            shape((channels * half_rows, slab_cols), f32),
        ),
        in_specs=[SM, VM],
        out_specs=(VM, VM),
        name="coefficient",
        compiler_params=pltpu.CompilerParams(vmem_limit_bytes=GRANT),
        cost_estimate=pl.CostEstimate(flops=10**5, bytes_accessed=10**5, transcendentals=10**4),
    )(step_index, own)
    late_rows = pl.pallas_call(
        join_kernel,
        out_shape=shape((half_attn // 2, model_width), bf16),
        in_specs=[VM] * 2,
        out_specs=VM,
        name="join",
        compiler_params=pltpu.CompilerParams(vmem_limit_bytes=GRANT),
    )(cross_weight, core_cross_weight)

    def finish(half):
        return pl.pallas_call(
            functools.partial(finish_kernel, half),
            out_shape=tuple(shape((slab_cols, wide), f32) for _ in range(2)),
            in_specs=[SM, SM] + [VM] * 6,
            out_specs=(VM, VM),
            scratch_shapes=[
                pltpu.VMEM((3 * slab_cols + 8, wide), f32),
                pltpu.VMEM((own_tokens, model_width), bf16),
            ],
            compiler_params=pltpu.CompilerParams(vmem_limit_bytes=GRANT),
            cost_estimate=pl.CostEstimate(
                flops=5 * 10**8, bytes_accessed=2 * 10**6, transcendentals=10**3
            ),
        )(offsets, blend_weights, modulate, embedded, mixed, late, late_rows, final)

    to_far, far_center = finish(1)
    to_near, center = finish(0)
    from_far = swap_ring(to_far, "win", 1)
    from_near = swap_ring(to_near, "win", 0)
    previous, noise = pl.pallas_call(
        blend_kernel,
        out_shape=tuple(shape((channels, half_rows, slab_cols), f32) for _ in range(2)),
        in_specs=[VM] * 6,
        out_specs=(VM, VM),
        name="blend",
        compiler_params=pltpu.CompilerParams(vmem_limit_bytes=GRANT),
    )(plan_values, center, from_near, far_center, from_far, rows)
    return (jnp.transpose(previous, (2, 0, 1)), jnp.transpose(noise, (2, 0, 1)))


def solution(mesh):
    in_specs = (
        P("win", None, None),
        P(None, None, None, "cfg"),
        P(),
        P(None, None, "cfg"),
        P("cfg", None),
        P(),
        P(),
        P("win"),
        P("win"),
        P(),
    )
    out_specs = (P("win", None, "cfg"), P("win", None, "cfg"))
    return jax.shard_map(
        on_device, mesh=mesh, in_specs=in_specs, out_specs=out_specs, check_vma=False
    )
```

```python
import functools
import math

import jax
import jax.numpy as jnp
from jax import lax
from jax.experimental import pallas as pl
from jax.experimental.pallas import tpu as pltpu
from jax.sharding import PartitionSpec as P


HEAD_DIM = 72
STEPS = 20


guidance_scale = 4.5
plan_length = 1000
norm_eps = 1e-06

VM = pl.BlockSpec(memory_space=pltpu.VMEM)
SM = pl.BlockSpec(memory_space=pltpu.SMEM)
GRANT = 24 * 2**20


def swap_ring(array, axis, odd):
    size = lax.axis_size(axis)
    pairs = []
    for left in range(odd, size, 2):
        right = (left + 1) % size
        pairs += [(left, right), (right, left)]
    return lax.ppermute(array, axis, pairs)


def swap(array, axis):
    return lax.ppermute(array, axis, [(0, 1), (1, 0)])


def swap_across(array, axis, step):
    size = lax.axis_size(axis)
    return lax.ppermute(array, axis, [(place, place ^ step) for place in range(size)])


def layer_norm(values):
    average = jnp.mean(values, axis=-1, keepdims=True)
    centered = values - average
    variance = jnp.mean(centered * centered, axis=-1, keepdims=True)
    return centered * lax.rsqrt(variance + norm_eps)


def repeat_pairs(weight, repeats):
    rows, width = weight.shape
    values = weight.astype(jnp.float32)
    even = lax.broadcasted_iota(jnp.int32, (2 * repeats, width), 0) % 2 == 0
    parts = []
    for pair in range(rows // 2):
        parts.append(
            jnp.where(even, values[2 * pair : 2 * pair + 1, :], values[2 * pair + 1 : 2 * pair + 2, :])
        )
    return jnp.concatenate(parts, axis=0).astype(jnp.bfloat16)


def prepare_kernel(
    row_count,
    patch_source,
    out_source,
    row_ref,
    col_ref,
    patch_wide_ref,
    quarter_ref,
    patch_ref,
    semaphores,
):
    patch_copy = pltpu.make_async_copy(patch_source, patch_ref, semaphores.at[0])
    patch_copy.start()
    count = quarter_ref.shape[0]
    first = pl.multiple_of(lax.axis_index("win") % 4 * count, 8)
    copy = pltpu.make_async_copy(out_source.at[pl.ds(first, count)], quarter_ref, semaphores.at[1])
    copy.start()
    model_width = patch_ref.shape[1]
    quarter = model_width // 4

    def table(target_ref, first):
        count, lanes = target_ref.shape
        lane = first + lax.broadcasted_iota(jnp.int32, (count, lanes), 1)
        place = lax.broadcasted_iota(jnp.int32, (count, lanes), 0).astype(jnp.float32)
        frequency = jnp.exp(-math.log(10000.0) * (lane % quarter).astype(jnp.float32) / quarter)
        phase = jnp.where(lane // quarter % 2 == 0, 0.0, 0.5 * math.pi)
        target_ref[...] = jnp.sin(place * frequency + phase)

    table(row_ref, 0)
    table(col_ref, model_width - col_ref.shape[1])
    patch_copy.wait()
    patch_wide_ref[...] = repeat_pairs(patch_ref[...], row_count // 2)
    copy.wait()


def coefficient_kernel(step_ref, latent_ref, plan_ref, rows_ref):
    _, channels, row_count = latent_ref.shape
    moment = step_ref[0]
    index = lax.broadcasted_iota(jnp.int32, (8, 128), 0) * 128 + lax.broadcasted_iota(
        jnp.int32, (8, 128), 1
    )
    train = jnp.minimum(index, plan_length - 1).astype(jnp.float32)
    beta_values = 0.0001 + (0.02 - 0.0001) * train / (plan_length - 1)
    logs = jnp.log(1.0 - beta_values)

    def alpha_bar(last):
        kept = jnp.where((index <= last) & (index < plan_length), logs, 0.0)
        kept = jnp.sum(jnp.sum(kept, axis=0, keepdims=True), axis=1, keepdims=True)
        return jnp.exp(kept)

    alpha_now = alpha_bar(moment)
    alpha_before = alpha_bar(moment - plan_length // STEPS)
    for place, value in enumerate(
        (
            jnp.sqrt(alpha_before),
            jnp.sqrt(1.0 - alpha_now),
            jnp.sqrt(alpha_now),
            jnp.sqrt(1.0 - alpha_before),
        )
    ):
        plan_ref[place : place + 1, :] = jnp.broadcast_to(value, (1, plan_ref.shape[1]))

    half_rows = row_count // 2
    side = lax.axis_index("cfg")
    for channel in range(channels):
        turned = jnp.transpose(latent_ref[:, channel, :], (1, 0))
        rows_ref[channel * half_rows : (channel + 1) * half_rows, :] = jnp.where(
            side == 0, turned[:half_rows], turned[half_rows:]
        )


def first_pair():
    return lax.axis_index("win") % 4 // 2


def token_lanes(side, tokens):
    return [
        pl.multiple_of(half * (tokens // 2) + side * (tokens // 4), tokens // 4)
        for half in range(2)
    ]


def attend(parts, text_ref, first, count, chosen, finished):
    branches = text_ref.shape[0]
    feature = (((0,), (0,)), ((), ()))

    def place_of(head):
        pair = first_pair() if head < 2 else 1 - first_pair()
        return 2 * pair + head % 2

    def score(head):
        queries = jnp.concatenate(
            [parts[head // 2][head % 2, :, pl.ds(start, count // 2)] for start in first], axis=1
        )
        return [
            lax.dot_general(keys, queries, feature, preferred_element_type=jnp.float32)
            for keys in [parts[head // 2][2 + head % 2]]
            + [text_ref[branch, 0, place_of(head)] for branch in range(branches)]
        ]

    def weigh(scores):
        own_highest = jnp.max(scores[0], axis=0, keepdims=True)
        own_exp = jnp.exp2(scores[0] - own_highest)
        own = (own_exp.astype(jnp.bfloat16), jnp.sum(own_exp, axis=0, keepdims=True))
        texts = []
        for text_scores in scores[1:]:
            highest = jnp.maximum(own_highest, jnp.max(text_scores, axis=0, keepdims=True))
            text_exp = jnp.exp2(text_scores - highest)
            lowered = jnp.exp2(own_highest - highest)
            total = lowered * own[1] + jnp.sum(text_exp, axis=0, keepdims=True)
            texts.append((text_exp.astype(jnp.bfloat16), lowered, 1.0 / total))
        return own[0], texts

    def mix(head, own_exp, texts):
        own_mix = jnp.dot(
            parts[head // 2][4 + head % 2], own_exp, preferred_element_type=jnp.float32
        )
        results = []
        for branch, (text_exp, lowered, inverse) in enumerate(texts):
            text_mix = jnp.dot(
                text_ref[branch, 1, place_of(head)], text_exp, preferred_element_type=jnp.float32
            )
            results.append((lowered * own_mix + text_mix) * inverse)
        return jnp.concatenate(
            [result[:, : count // 2] for result in results]
            + [result[:, count // 2 :] for result in results],
            axis=1,
        )

    chosen = list(chosen)
    mixed = []

    def take(place, weights):
        mixed.append(mix(chosen[place], *weights))
        if place % 2:
            finished(place // 2, jnp.concatenate(mixed[-2:], axis=0).astype(jnp.bfloat16))

    ahead = score(chosen[0])
    before = None
    for place, head in enumerate(chosen):
        scores = ahead
        if place + 1 < len(chosen):
            ahead = score(chosen[place + 1])
        weights = weigh(scores)
        if before is not None:
            take(place - 1, before)
        before = weights
    take(len(chosen) - 1, before)


def keep_pair(target_ref, place, pair):
    target_ref[...] = pair


def pair_rows(weight_ref, pair):
    total = weight_ref.shape[0] // 3
    count = 2 * HEAD_DIM
    return jnp.concatenate(
        [
            weight_ref[pl.ds(pl.multiple_of(kind * total + pair * count, 16), count), :]
            for kind in range(3)
        ],
        axis=0,
    )


def project_half(weight_ref, pair, normed, target_ref, lanes):
    projected = lax.dot_general(
        pair_rows(weight_ref, pair), normed, (((1,), (1,)), ((), ())), preferred_element_type=jnp.float32
    )
    for block in range(target_ref.shape[0]):
        part = projected[block * HEAD_DIM : (block + 1) * HEAD_DIM]
        if block < target_ref.shape[0] // 3:
            part = part * (math.log2(math.e) / math.sqrt(HEAD_DIM))
        target_ref[block, :, lanes] = part.astype(jnp.bfloat16)


def project_kernel(
    step_ref,
    offset_ref,
    modulations_ref,
    near_ref,
    own_ref,
    far_ref,
    row_ref,
    col_ref,
    patch_ref,
    weight_ref,
    text_ref,
    proj_ref,
    normed_ref,
    modulation_ref,
    embedded_ref,
    sent_ref,
    extended_ref,
):
    modulation_ref[...] = modulations_ref[step_ref[0] * STEPS // plan_length]
    slab_cols, channels, row_count = own_ref.shape
    col_pairs, row_couples = slab_cols, row_count // 2
    tokens = col_pairs * row_couples
    own_tokens = tokens // 2
    wide = 2 * channels * row_count
    even = lax.axis_index("win") % 2 == 0
    for channel in range(channels):
        near, far = near_ref[:, channel, :], far_ref[:, channel, :]
        values = (jnp.where(even, far, near), own_ref[:, channel, :], jnp.where(even, near, far))
        for place, value in enumerate(values):
            extended_ref[
                place * slab_cols : (place + 1) * slab_cols,
                channel * row_count : (channel + 1) * row_count,
            ] = value
    extended = extended_ref[...].astype(jnp.bfloat16)
    start_at = slab_cols - offset_ref[0]
    chosen = lax.broadcasted_iota(jnp.int32, (2 * col_pairs, 3 * slab_cols), 0)
    column = lax.broadcasted_iota(jnp.int32, (2 * col_pairs, 3 * slab_cols), 1)
    half_pairs = col_pairs // 2
    parity = lax.axis_index("win") % 2
    near_first, far_first = (1 - parity) * half_pairs, parity * half_pairs
    group, within = chosen // half_pairs, chosen % half_pairs
    target = 2 * (within + jnp.where(group < 2, near_first, far_first)) + group % 2
    pick = jnp.where(column == target + start_at, 1.0, 0.0).astype(jnp.bfloat16)
    picked = jnp.dot(pick, extended, preferred_element_type=jnp.float32)
    groups = [picked[place * half_pairs : (place + 1) * half_pairs] for place in range(4)]
    lane_couple = lax.broadcasted_iota(jnp.int32, (half_pairs, wide), 1) % row_count // 2
    spread = []
    for place in range(2):
        pair = jnp.concatenate(groups[2 * place : 2 * place + 2], axis=1)
        spread.append(
            jnp.concatenate(
                [jnp.where(lane_couple == couple, pair, 0.0) for couple in range(row_couples)],
                axis=0,
            ).astype(jnp.bfloat16)
        )
    side = lax.axis_index("cfg")
    chunks = [slice(place * own_tokens, (place + 1) * own_tokens) for place in range(2)]

    model_width = patch_ref.shape[1]
    below, above = model_width - col_ref.shape[1], row_ref.shape[1]
    is_row = below + lax.broadcasted_iota(jnp.int32, (half_pairs, above - below), 1)
    is_row = is_row < model_width // 2

    def position(place, couple):
        line = jnp.broadcast_to(row_ref[couple : couple + 1, :], (half_pairs, above))
        column_first = near_first if place == 0 else far_first
        column = col_ref[pl.ds(pl.multiple_of(column_first, half_pairs), half_pairs), :]
        both = jnp.where(is_row, line[:, below:], column[:, : above - below])
        return jnp.concatenate([line[:, :below], both, column[:, above - below :]], axis=1)

    gain, shift = 1.0 + modulation_ref[1:2, :], modulation_ref[0:1, :]

    def embed(place):
        return jnp.dot(spread[place], patch_ref[...], preferred_element_type=jnp.float32)

    def norm(place, patches):
        for first_couple in range(0, row_couples, 2):
            rows = slice(first_couple * half_pairs, (first_couple + 2) * half_pairs)
            target = slice(place * own_tokens + rows.start, place * own_tokens + rows.stop)
            embedded = patches[rows] + jnp.concatenate(
                [position(place, first_couple + next_) for next_ in range(2)], axis=0
            )
            embedded_ref[target, :] = embedded
            normed = layer_norm(embedded) * gain + shift
            normed_ref[target, :] = normed.astype(jnp.bfloat16)

    early = embed(0)
    later = embed(1)
    norm(0, early)
    project_half(weight_ref, first_pair(), normed_ref[chunks[0], :], proj_ref, chunks[0])
    norm(1, later)
    project_half(weight_ref, first_pair(), normed_ref[chunks[1], :], proj_ref, chunks[1])
    first = token_lanes(1 - side, tokens)
    attend(
        [proj_ref], text_ref, first, own_tokens, range(2), functools.partial(keep_pair, sent_ref)
    )


def second_kernel(normed_ref, text_ref, weight_ref, proj_ref, sent_ref):
    own_tokens = normed_ref.shape[0] // 2
    for place in range(2):
        chunk = slice(place * own_tokens, (place + 1) * own_tokens)
        project_half(weight_ref, 1 - first_pair(), normed_ref[chunk, :], proj_ref, chunk)
    first = token_lanes(1 - lax.axis_index("cfg"), 2 * own_tokens)
    attend(
        [None, proj_ref], text_ref, first, own_tokens, range(2, 4),
        functools.partial(keep_pair, sent_ref),
    )


def attend_kernel(early_ref, late_ref, text_ref, weight_ref, mixed_ref):
    tokens = early_ref.shape[2]
    own_tokens = tokens // 2
    first = token_lanes(lax.axis_index("cfg"), tokens)
    pairs = []

    def finished(place, pair):
        pairs.append(pair)

    attend([early_ref, late_ref], text_ref, first, own_tokens, range(4), finished)
    count = 2 * HEAD_DIM
    mixed = []
    for place, pair in enumerate(pairs):
        chosen = first_pair() if place == 0 else 1 - first_pair()
        rows = pl.ds(pl.multiple_of(chosen * count, count), count)
        mixed.append(contract(pair, weight_ref[rows, :]))
    mixed_ref[...] = mixed[0] + mixed[1]


def contract(features, weight):
    return lax.dot_general(
        features, weight, (((0,), (0,)), ((), ())), preferred_element_type=jnp.float32
    )


def join(mine_ref, neighbour_ref):
    mine, neighbour = mine_ref[...].astype(jnp.float32), neighbour_ref[...].astype(jnp.float32)
    even_place = lax.axis_index("win") % 2 == 0
    first = jnp.where(even_place, mine, neighbour)
    second = jnp.where(even_place, neighbour, mine)
    return jnp.concatenate([first, second], axis=0).astype(jnp.bfloat16)


def join_kernel(mine_ref, neighbour_ref, joined_ref):
    joined_ref[...] = join(mine_ref, neighbour_ref)


def partial_kernel(mixed_ref, early_ref, weight_ref, core_ref, summed_ref):
    summed_ref[...] = mixed_ref[...] + contract(early_ref[...], join(weight_ref, core_ref))


def finish_kernel(
    half,
    offset_ref,
    blend_ref,
    modulation_ref,
    embedded_ref,
    mixed_ref,
    late_ref,
    weight_ref,
    final_ref,
    sent_ref,
    center_ref,
    buffer_ref,
    final_norm_ref,
):
    slab_cols, wide = center_ref.shape
    half_pairs = slab_cols // 2
    count = embedded_ref.shape[0] // 4
    couples = count // half_pairs
    final_wide = repeat_pairs(final_ref[...], couples)
    gate, gain = modulation_ref[2:3, :], 1.0 + modulation_ref[3:4, :]
    side_first = pl.multiple_of(half * 2 * count + lax.axis_index("cfg") * count, count)
    lanes = slice(half * 2 * count, (half + 1) * 2 * count)
    other = contract(late_ref[:, lanes], weight_ref[...])
    predicted = []
    block = slab_cols
    for branch in range(2):
        for place in range(count // block):
            rows = slice(branch * count + place * block, branch * count + (place + 1) * block)
            mixed = mixed_ref[lanes.start + rows.start : lanes.start + rows.stop, :] + other[rows]
            embedded = embedded_ref[pl.ds(side_first + place * block, block), :]
            residual = embedded + gate * mixed
            final_norm_ref[rows, :] = (layer_norm(residual) * gain).astype(jnp.bfloat16)
        rows = slice(branch * count, (branch + 1) * count)
        predicted.append(
            lax.dot_general(
                final_norm_ref[rows, :],
                final_wide,
                (((1,), (1,)), ((), ())),
                preferred_element_type=jnp.float32,
            )
        )
    conditional, unconditional = predicted
    guided = unconditional + guidance_scale * (conditional - unconditional)
    lane_couple = lax.broadcasted_iota(jnp.int32, (half_pairs, wide), 1) % (2 * couples) // 2
    pairs = jnp.zeros((half_pairs, wide), jnp.float32)
    for couple in range(couples):
        pairs = pairs + jnp.where(
            lane_couple == couple, guided[couple * half_pairs : (couple + 1) * half_pairs], 0.0
        )
    weight_value = blend_ref[0].astype(jnp.float32)
    is_noise = lax.broadcasted_iota(jnp.int32, (half_pairs, wide), 1) < wide // 2
    even = jnp.where(is_noise, weight_value * pairs, weight_value)
    odd = jnp.where(is_noise, weight_value * pltpu.roll(pairs, wide // 2, 1), weight_value)
    parity = lax.axis_index("win") % 2
    right = 1 - parity if half == 0 else parity
    start_at = slab_cols - offset_ref[0] + right * slab_cols
    buffer_ref[...] = jnp.zeros_like(buffer_ref)
    buffer_ref[pl.ds(start_at, half_pairs, stride=2), :] = even
    buffer_ref[pl.ds(start_at + 1, half_pairs, stride=2), :] = odd
    center_ref[...] = buffer_ref[slab_cols : 2 * slab_cols]
    sent_ref[...] = jnp.where(
        right == 1, buffer_ref[2 * slab_cols : 3 * slab_cols], buffer_ref[:slab_cols]
    )


def blend_kernel(
    plan_ref, center_ref, near_ref, far_center_ref, far_ref, rows_ref, previous_ref, noise_ref
):
    channels, half_rows, slab_cols = noise_ref.shape
    total = (center_ref[...] + near_ref[...]) + (far_center_ref[...] + far_ref[...])
    total = jnp.transpose(total, (1, 0))
    half = total.shape[0] // 2
    noise = total[:half] / total[half:]
    scale = plan_ref[:, :slab_cols]
    previous = (
        scale[0:1] * (rows_ref[...] - scale[1:2] * noise) / scale[2:3] + scale[3:4] * noise
    )
    for channel in range(channels):
        rows = slice(channel * half_rows, (channel + 1) * half_rows)
        noise_ref[channel] = noise[rows]
        previous_ref[channel] = previous[rows]


def on_device(
    latent,
    text_kv,
    modulation,
    qkv_weight,
    out_weight,
    patch_weight,
    final_weight,
    offsets,
    blend_weights,
    step_index,
):
    slab_cols, channels, row_count = latent.shape
    model_width = patch_weight.shape[1]
    half_attn = out_weight.shape[0]
    heads = half_attn // HEAD_DIM
    branches, caption = text_kv.shape[0], text_kv.shape[2]
    col_pairs, row_couples = slab_cols, row_count // 2
    tokens = col_pairs * row_couples
    own_tokens = tokens // 2
    half_rows = row_count // 2
    far = swap_ring(latent, "win", 1)
    near = swap_ring(latent, "win", 0)
    hbm = pl.BlockSpec(memory_space=pltpu.HBM)
    keep = functools.partial(pltpu.with_memory_space_constraint, memory_space=pltpu.HBM)
    weight = jnp.transpose(qkv_weight, (1, 2, 0)).reshape(3 * half_attn, model_width)
    text = jnp.transpose(text_kv, (0, 1, 3, 2)).reshape(branches, 2, heads, HEAD_DIM, caption)
    final = jnp.transpose(final_weight, (1, 0))

    bf16, f32 = jnp.bfloat16, jnp.float32
    shape = jax.ShapeDtypeStruct
    wide = 2 * channels * half_rows
    half_width = model_width // 2
    below, above = half_width // 128 * 128, -(-half_width // 128) * 128
    row_part, col_part, patch_wide, quarter = pl.pallas_call(
        functools.partial(prepare_kernel, row_count),
        out_shape=(
            shape((row_couples, above), f32),
            shape((col_pairs, model_width - below), f32),
            shape((2 * channels * row_count, model_width), bf16),
            shape((half_attn // 4, model_width), bf16),
        ),
        in_specs=[hbm] * 2,
        out_specs=(VM,) * 4,
        scratch_shapes=[pltpu.VMEM(patch_weight.shape, bf16), pltpu.SemaphoreType.DMA((2,))],
        name="prepare",
        compiler_params=pltpu.CompilerParams(vmem_limit_bytes=GRANT),
        cost_estimate=pl.CostEstimate(flops=2*10**9, bytes_accessed=10**6, transcendentals=10**5),
    )(keep(patch_weight), keep(out_weight))
    other_weight = swap(quarter, "cfg")
    projected, normed, modulate, embedded, sent = pl.pallas_call(
        project_kernel,
        out_shape=(
            shape((3 * heads // 2, HEAD_DIM, tokens), bf16),
            shape((tokens, model_width), bf16),
            shape(modulation.shape[1:], f32),
            shape((tokens, model_width), f32),
            shape((half_attn // 2, branches * own_tokens), bf16),
        ),
        in_specs=[SM, SM] + [VM] * 9,
        out_specs=(VM,) * 5,
        scratch_shapes=[pltpu.VMEM((3 * slab_cols, channels * row_count), f32)],
        name="project",
        compiler_params=pltpu.CompilerParams(vmem_limit_bytes=GRANT),
        cost_estimate=pl.CostEstimate(flops=2 * 10**9, bytes_accessed=8 * 10**6, transcendentals=10**6),
    )(
        step_index, offsets, modulation, near, latent, far, row_part, col_part, patch_wide,
        weight, text,
    )
    early = swap(sent, "cfg")
    projected_late, sent = pl.pallas_call(
        second_kernel,
        out_shape=(
            shape((3 * heads // 2, HEAD_DIM, tokens), bf16),
            shape((half_attn // 2, branches * own_tokens), bf16),
        ),
        in_specs=[VM] * 3,
        out_specs=(VM,) * 2,
        name="second",
        compiler_params=pltpu.CompilerParams(vmem_limit_bytes=GRANT),
        cost_estimate=pl.CostEstimate(flops=10**9, bytes_accessed=10**6, transcendentals=10**6),
    )(normed, text, weight)
    late = swap(sent, "cfg")
    cross_weight = swap_across(other_weight, "win", 2)
    core_weight = swap_across(other_weight, "win", 1)
    core_cross_weight = swap_across(cross_weight, "win", 1)
    mixed = pl.pallas_call(
        attend_kernel,
        out_shape=shape((branches * own_tokens, model_width), f32),
        in_specs=[VM] * 4,
        out_specs=VM,
        name="attend",
        compiler_params=pltpu.CompilerParams(vmem_limit_bytes=GRANT),
        cost_estimate=pl.CostEstimate(flops=10**9, bytes_accessed=8 * 10**6, transcendentals=10**6),
    )(projected, projected_late, text, out_weight)
    mixed = pl.pallas_call(
        partial_kernel,
        out_shape=shape(mixed.shape, f32),
        in_specs=[VM] * 4,
        out_specs=VM,
        name="partial",
        compiler_params=pltpu.CompilerParams(vmem_limit_bytes=GRANT),
        cost_estimate=pl.CostEstimate(flops=2 * 10**8, bytes_accessed=10**6, transcendentals=0),
    )(mixed, early, other_weight, core_weight)
    plan_values, rows = pl.pallas_call(
        coefficient_kernel,
        out_shape=(
            shape((8, -(-slab_cols // 128) * 128), f32),
            shape((channels * half_rows, slab_cols), f32),
        ),
        in_specs=[SM, VM],
        out_specs=(VM, VM),
        name="coefficient",
        compiler_params=pltpu.CompilerParams(vmem_limit_bytes=GRANT),
        cost_estimate=pl.CostEstimate(flops=10**5, bytes_accessed=10**5, transcendentals=10**4),
    )(step_index, latent)
    late_rows = pl.pallas_call(
        join_kernel,
        out_shape=shape((half_attn // 2, model_width), bf16),
        in_specs=[VM] * 2,
        out_specs=VM,
        name="join",
        compiler_params=pltpu.CompilerParams(vmem_limit_bytes=GRANT),
    )(cross_weight, core_cross_weight)

    def finish(half):
        return pl.pallas_call(
            functools.partial(finish_kernel, half),
            out_shape=tuple(shape((slab_cols, wide), f32) for _ in range(2)),
            in_specs=[SM, SM] + [VM] * 6,
            out_specs=(VM, VM),
            scratch_shapes=[
                pltpu.VMEM((3 * slab_cols + 8, wide), f32),
                pltpu.VMEM((own_tokens, model_width), bf16),
            ],
            compiler_params=pltpu.CompilerParams(vmem_limit_bytes=GRANT),
            cost_estimate=pl.CostEstimate(
                flops=5 * 10**8, bytes_accessed=2 * 10**6, transcendentals=10**3
            ),
        )(offsets, blend_weights, modulate, embedded, mixed, late, late_rows, final)

    to_far, far_center = finish(1)
    to_near, center = finish(0)
    from_far = swap_ring(to_far, "win", 1)
    from_near = swap_ring(to_near, "win", 0)
    previous, noise = pl.pallas_call(
        blend_kernel,
        out_shape=tuple(shape((channels, half_rows, slab_cols), f32) for _ in range(2)),
        in_specs=[VM] * 6,
        out_specs=(VM, VM),
        name="blend",
        compiler_params=pltpu.CompilerParams(vmem_limit_bytes=GRANT),
    )(plan_values, center, from_near, far_center, from_far, rows)
    return (jnp.transpose(previous, (2, 0, 1)), jnp.transpose(noise, (2, 0, 1)))


def solution(mesh):
    in_specs = (
        P("win", None, None),
        P(None, None, None, "cfg"),
        P(),
        P(None, None, "cfg"),
        P("cfg", None),
        P(),
        P(),
        P("win"),
        P("win"),
        P(),
    )
    out_specs = (P("win", None, "cfg"), P("win", None, "cfg"))
    return jax.shard_map(
        on_device, mesh=mesh, in_specs=in_specs, out_specs=out_specs, check_vma=False
    )
```

```python
import functools
import math

import jax
import jax.numpy as jnp
from jax import lax
from jax.experimental import pallas as pl
from jax.experimental.pallas import tpu as pltpu
from jax.sharding import PartitionSpec as P


HEAD_DIM = 72
STEPS = 20


guidance_scale = 4.5
plan_length = 1000
norm_eps = 1e-06

VM = pl.BlockSpec(memory_space=pltpu.VMEM)
SM = pl.BlockSpec(memory_space=pltpu.SMEM)
GRANT = 24 * 2**20


def swap_ring(array, axis, odd):
    size = lax.axis_size(axis)
    pairs = []
    for left in range(odd, size, 2):
        right = (left + 1) % size
        pairs += [(left, right), (right, left)]
    return lax.ppermute(array, axis, pairs)


def swap(array, axis):
    return lax.ppermute(array, axis, [(0, 1), (1, 0)])


def swap_across(array, axis, step):
    size = lax.axis_size(axis)
    return lax.ppermute(array, axis, [(place, place ^ step) for place in range(size)])


def layer_norm(values):
    average = jnp.mean(values, axis=-1, keepdims=True)
    centered = values - average
    variance = jnp.mean(centered * centered, axis=-1, keepdims=True)
    return centered * lax.rsqrt(variance + norm_eps)


def repeat_pairs(weight, repeats):
    rows, width = weight.shape
    values = weight.astype(jnp.float32)
    even = lax.broadcasted_iota(jnp.int32, (2 * repeats, width), 0) % 2 == 0
    parts = []
    for pair in range(rows // 2):
        parts.append(
            jnp.where(even, values[2 * pair : 2 * pair + 1, :], values[2 * pair + 1 : 2 * pair + 2, :])
        )
    return jnp.concatenate(parts, axis=0).astype(jnp.bfloat16)


def prepare_kernel(
    row_count,
    patch_source,
    out_source,
    row_ref,
    col_ref,
    patch_wide_ref,
    quarter_ref,
    patch_ref,
    semaphores,
):
    patch_copy = pltpu.make_async_copy(patch_source, patch_ref, semaphores.at[0])
    patch_copy.start()
    count = quarter_ref.shape[0]
    first = pl.multiple_of(lax.axis_index("win") % 4 * count, 8)
    copy = pltpu.make_async_copy(out_source.at[pl.ds(first, count)], quarter_ref, semaphores.at[1])
    copy.start()
    model_width = patch_ref.shape[1]
    quarter = model_width // 4

    def table(target_ref, first):
        count, lanes = target_ref.shape
        lane = first + lax.broadcasted_iota(jnp.int32, (count, lanes), 1)
        place = lax.broadcasted_iota(jnp.int32, (count, lanes), 0).astype(jnp.float32)
        frequency = jnp.exp(-math.log(10000.0) * (lane % quarter).astype(jnp.float32) / quarter)
        phase = jnp.where(lane // quarter % 2 == 0, 0.0, 0.5 * math.pi)
        target_ref[...] = jnp.sin(place * frequency + phase)

    table(row_ref, 0)
    table(col_ref, model_width - col_ref.shape[1])
    patch_copy.wait()
    patch_wide_ref[...] = repeat_pairs(patch_ref[...], row_count // 2)
    copy.wait()


def coefficient_kernel(step_ref, latent_ref, plan_ref, rows_ref):
    _, channels, row_count = latent_ref.shape
    moment = step_ref[0]
    index = lax.broadcasted_iota(jnp.int32, (8, 128), 0) * 128 + lax.broadcasted_iota(
        jnp.int32, (8, 128), 1
    )
    train = jnp.minimum(index, plan_length - 1).astype(jnp.float32)
    beta_values = 0.0001 + (0.02 - 0.0001) * train / (plan_length - 1)
    logs = jnp.log(1.0 - beta_values)

    def alpha_bar(last):
        kept = jnp.where((index <= last) & (index < plan_length), logs, 0.0)
        kept = jnp.sum(jnp.sum(kept, axis=0, keepdims=True), axis=1, keepdims=True)
        return jnp.exp(kept)

    alpha_now = alpha_bar(moment)
    alpha_before = alpha_bar(moment - plan_length // STEPS)
    for place, value in enumerate(
        (
            jnp.sqrt(alpha_before),
            jnp.sqrt(1.0 - alpha_now),
            jnp.sqrt(alpha_now),
            jnp.sqrt(1.0 - alpha_before),
        )
    ):
        plan_ref[place : place + 1, :] = jnp.broadcast_to(value, (1, plan_ref.shape[1]))

    half_rows = row_count // 2
    side = lax.axis_index("cfg")
    for channel in range(channels):
        turned = jnp.transpose(latent_ref[:, channel, :], (1, 0))
        rows_ref[channel * half_rows : (channel + 1) * half_rows, :] = jnp.where(
            side == 0, turned[:half_rows], turned[half_rows:]
        )


def first_pair():
    return lax.axis_index("win") % 4 // 2


def token_lanes(side, tokens):
    return [
        pl.multiple_of(half * (tokens // 2) + side * (tokens // 4), tokens // 4)
        for half in range(2)
    ]


def attend(parts, text_ref, first, count, chosen, finished):
    branches = text_ref.shape[0]
    feature = (((0,), (0,)), ((), ()))

    def place_of(head):
        pair = first_pair() if head < 2 else 1 - first_pair()
        return 2 * pair + head % 2

    def score(head):
        queries = jnp.concatenate(
            [parts[head // 2][head % 2, :, pl.ds(start, count // 2)] for start in first], axis=1
        )
        return [
            lax.dot_general(keys, queries, feature, preferred_element_type=jnp.float32)
            for keys in [parts[head // 2][2 + head % 2]]
            + [text_ref[branch, 0, place_of(head)] for branch in range(branches)]
        ]

    def weigh(scores):
        own_highest = jnp.max(scores[0], axis=0, keepdims=True)
        own_exp = jnp.exp2(scores[0] - own_highest)
        own = (own_exp.astype(jnp.bfloat16), jnp.sum(own_exp, axis=0, keepdims=True))
        texts = []
        for text_scores in scores[1:]:
            highest = jnp.maximum(own_highest, jnp.max(text_scores, axis=0, keepdims=True))
            text_exp = jnp.exp2(text_scores - highest)
            lowered = jnp.exp2(own_highest - highest)
            total = lowered * own[1] + jnp.sum(text_exp, axis=0, keepdims=True)
            texts.append((text_exp.astype(jnp.bfloat16), lowered, 1.0 / total))
        return own[0], texts

    def mix(head, own_exp, texts):
        own_mix = jnp.dot(
            parts[head // 2][4 + head % 2], own_exp, preferred_element_type=jnp.float32
        )
        results = []
        for branch, (text_exp, lowered, inverse) in enumerate(texts):
            text_mix = jnp.dot(
                text_ref[branch, 1, place_of(head)], text_exp, preferred_element_type=jnp.float32
            )
            results.append((lowered * own_mix + text_mix) * inverse)
        return jnp.concatenate(
            [result[:, : count // 2] for result in results]
            + [result[:, count // 2 :] for result in results],
            axis=1,
        )

    chosen = list(chosen)
    mixed = []

    def take(place, weights):
        mixed.append(mix(chosen[place], *weights))
        if place % 2:
            finished(place // 2, jnp.concatenate(mixed[-2:], axis=0).astype(jnp.bfloat16))

    ahead = score(chosen[0])
    before = None
    for place, head in enumerate(chosen):
        scores = ahead
        if place + 1 < len(chosen):
            ahead = score(chosen[place + 1])
        weights = weigh(scores)
        if before is not None:
            take(place - 1, before)
        before = weights
    take(len(chosen) - 1, before)


def keep_pair(target_ref, place, pair):
    target_ref[...] = pair


def pair_rows(weight_ref, pair):
    total = weight_ref.shape[0] // 3
    count = 2 * HEAD_DIM
    return jnp.concatenate(
        [
            weight_ref[pl.ds(pl.multiple_of(kind * total + pair * count, 16), count), :]
            for kind in range(3)
        ],
        axis=0,
    )


def project_half(weight_ref, pair, normed, target_ref, lanes):
    projected = lax.dot_general(
        pair_rows(weight_ref, pair), normed, (((1,), (1,)), ((), ())), preferred_element_type=jnp.float32
    )
    for block in range(target_ref.shape[0]):
        part = projected[block * HEAD_DIM : (block + 1) * HEAD_DIM]
        if block < target_ref.shape[0] // 3:
            part = part * (math.log2(math.e) / math.sqrt(HEAD_DIM))
        target_ref[block, :, lanes] = part.astype(jnp.bfloat16)


def project_kernel(
    step_ref,
    offset_ref,
    modulations_ref,
    near_ref,
    own_ref,
    far_ref,
    row_ref,
    col_ref,
    patch_ref,
    weight_ref,
    text_ref,
    proj_ref,
    normed_ref,
    modulation_ref,
    embedded_ref,
    sent_ref,
    extended_ref,
):
    modulation_ref[...] = modulations_ref[step_ref[0] * STEPS // plan_length]
    slab_cols, channels, row_count = own_ref.shape
    col_pairs, row_couples = slab_cols, row_count // 2
    tokens = col_pairs * row_couples
    own_tokens = tokens // 2
    wide = 2 * channels * row_count
    even = lax.axis_index("win") % 2 == 0
    for channel in range(channels):
        near, far = near_ref[:, channel, :], far_ref[:, channel, :]
        values = (jnp.where(even, far, near), own_ref[:, channel, :], jnp.where(even, near, far))
        for place, value in enumerate(values):
            extended_ref[
                place * slab_cols : (place + 1) * slab_cols,
                channel * row_count : (channel + 1) * row_count,
            ] = value
    extended = extended_ref[...].astype(jnp.bfloat16)
    start_at = slab_cols - offset_ref[0]
    chosen = lax.broadcasted_iota(jnp.int32, (2 * col_pairs, 3 * slab_cols), 0)
    column = lax.broadcasted_iota(jnp.int32, (2 * col_pairs, 3 * slab_cols), 1)
    half_pairs = col_pairs // 2
    parity = lax.axis_index("win") % 2
    near_first, far_first = (1 - parity) * half_pairs, parity * half_pairs
    group, within = chosen // half_pairs, chosen % half_pairs
    target = 2 * (within + jnp.where(group < 2, near_first, far_first)) + group % 2
    pick = jnp.where(column == target + start_at, 1.0, 0.0).astype(jnp.bfloat16)
    picked = jnp.dot(pick, extended, preferred_element_type=jnp.float32)
    groups = [picked[place * half_pairs : (place + 1) * half_pairs] for place in range(4)]
    lane_couple = lax.broadcasted_iota(jnp.int32, (half_pairs, wide), 1) % row_count // 2
    spread = []
    for place in range(2):
        pair = jnp.concatenate(groups[2 * place : 2 * place + 2], axis=1)
        spread.append(
            jnp.concatenate(
                [jnp.where(lane_couple == couple, pair, 0.0) for couple in range(row_couples)],
                axis=0,
            ).astype(jnp.bfloat16)
        )
    side = lax.axis_index("cfg")
    chunks = [slice(place * own_tokens, (place + 1) * own_tokens) for place in range(2)]

    model_width = patch_ref.shape[1]
    below, above = model_width - col_ref.shape[1], row_ref.shape[1]
    is_row = below + lax.broadcasted_iota(jnp.int32, (half_pairs, above - below), 1)
    is_row = is_row < model_width // 2

    def position(place, couple):
        line = jnp.broadcast_to(row_ref[couple : couple + 1, :], (half_pairs, above))
        column_first = near_first if place == 0 else far_first
        column = col_ref[pl.ds(pl.multiple_of(column_first, half_pairs), half_pairs), :]
        both = jnp.where(is_row, line[:, below:], column[:, : above - below])
        return jnp.concatenate([line[:, :below], both, column[:, above - below :]], axis=1)

    gain, shift = 1.0 + modulation_ref[1:2, :], modulation_ref[0:1, :]

    def embed(place):
        return jnp.dot(spread[place], patch_ref[...], preferred_element_type=jnp.float32)

    def norm(place, patches):
        for first_couple in range(0, row_couples, 2):
            rows = slice(first_couple * half_pairs, (first_couple + 2) * half_pairs)
            target = slice(place * own_tokens + rows.start, place * own_tokens + rows.stop)
            embedded = patches[rows] + jnp.concatenate(
                [position(place, first_couple + next_) for next_ in range(2)], axis=0
            )
            embedded_ref[target, :] = embedded
            normed = layer_norm(embedded) * gain + shift
            normed_ref[target, :] = normed.astype(jnp.bfloat16)

    early = embed(0)
    later = embed(1)
    norm(0, early)
    project_half(weight_ref, first_pair(), normed_ref[chunks[0], :], proj_ref, chunks[0])
    norm(1, later)
    project_half(weight_ref, first_pair(), normed_ref[chunks[1], :], proj_ref, chunks[1])
    first = token_lanes(1 - side, tokens)
    attend(
        [proj_ref], text_ref, first, own_tokens, range(2), functools.partial(keep_pair, sent_ref)
    )


def keep_halves(near_ref, far_ref, place, pair):
    count = near_ref.shape[1]
    near_ref[...] = pair[:, :count]
    far_ref[...] = pair[:, count:]


def second_kernel(normed_ref, text_ref, weight_ref, proj_ref, near_ref, far_ref):
    own_tokens = normed_ref.shape[0] // 2
    for place in range(2):
        chunk = slice(place * own_tokens, (place + 1) * own_tokens)
        project_half(weight_ref, 1 - first_pair(), normed_ref[chunk, :], proj_ref, chunk)
    first = token_lanes(1 - lax.axis_index("cfg"), 2 * own_tokens)
    attend(
        [None, proj_ref], text_ref, first, own_tokens, range(2, 4),
        functools.partial(keep_halves, near_ref, far_ref),
    )


def attend_kernel(
    early_ref, late_ref, text_ref, weight_ref, final_ref, mixed_ref, final_wide_ref
):
    final_wide_ref[...] = repeat_pairs(
        final_ref[...], final_wide_ref.shape[0] // final_ref.shape[0]
    )
    tokens = early_ref.shape[2]
    own_tokens = tokens // 2
    first = token_lanes(lax.axis_index("cfg"), tokens)
    pairs = []

    def finished(place, pair):
        pairs.append(pair)

    attend([early_ref, late_ref], text_ref, first, own_tokens, range(4), finished)
    count = 2 * HEAD_DIM
    mixed = []
    for place, pair in enumerate(pairs):
        chosen = first_pair() if place == 0 else 1 - first_pair()
        rows = pl.ds(pl.multiple_of(chosen * count, count), count)
        mixed.append(contract(pair, weight_ref[rows, :]))
    mixed_ref[...] = mixed[0] + mixed[1]


def contract(features, weight):
    return lax.dot_general(
        features, weight, (((0,), (0,)), ((), ())), preferred_element_type=jnp.float32
    )


def join(mine_ref, neighbour_ref):
    mine, neighbour = mine_ref[...].astype(jnp.float32), neighbour_ref[...].astype(jnp.float32)
    even_place = lax.axis_index("win") % 2 == 0
    first = jnp.where(even_place, mine, neighbour)
    second = jnp.where(even_place, neighbour, mine)
    return jnp.concatenate([first, second], axis=0).astype(jnp.bfloat16)


def join_kernel(mine_ref, neighbour_ref, joined_ref):
    joined_ref[...] = join(mine_ref, neighbour_ref)


def partial_kernel(
    half, modulation_ref, embedded_ref, mixed_ref, early_ref, weight_ref, core_ref, residual_ref
):
    count = residual_ref.shape[0] // 2
    lanes = slice(half * 2 * count, (half + 1) * 2 * count)
    mixed = contract(early_ref[:, lanes], join(weight_ref, core_ref)) + mixed_ref[lanes, :]
    first = pl.multiple_of(half * 2 * count + lax.axis_index("cfg") * count, count)
    embedded = embedded_ref[pl.ds(first, count), :]
    for branch in range(2):
        rows = slice(branch * count, (branch + 1) * count)
        residual_ref[rows, :] = embedded + modulation_ref[2:3, :] * mixed[rows]


def finish_kernel(
    half,
    offset_ref,
    blend_ref,
    modulation_ref,
    residual_ref,
    late_ref,
    weight_ref,
    final_ref,
    sent_ref,
    center_ref,
    buffer_ref,
    final_norm_ref,
):
    slab_cols, wide = center_ref.shape
    half_pairs = slab_cols // 2
    count = residual_ref.shape[0] // 2
    couples = count // half_pairs
    gate, gain = modulation_ref[2:3, :], 1.0 + modulation_ref[3:4, :]
    other = contract(late_ref[...], weight_ref[...])
    predicted = []
    block = slab_cols
    for branch in range(2):
        for place in range(count // block):
            rows = slice(branch * count + place * block, branch * count + (place + 1) * block)
            residual = residual_ref[rows, :] + gate * other[rows]
            final_norm_ref[rows, :] = (layer_norm(residual) * gain).astype(jnp.bfloat16)
        rows = slice(branch * count, (branch + 1) * count)
        predicted.append(
            lax.dot_general(
                final_norm_ref[rows, :],
                final_ref[...],
                (((1,), (1,)), ((), ())),
                preferred_element_type=jnp.float32,
            )
        )
    conditional, unconditional = predicted
    guided = unconditional + guidance_scale * (conditional - unconditional)
    lane_couple = lax.broadcasted_iota(jnp.int32, (half_pairs, wide), 1) % (2 * couples) // 2
    pairs = jnp.zeros((half_pairs, wide), jnp.float32)
    for couple in range(couples):
        pairs = pairs + jnp.where(
            lane_couple == couple, guided[couple * half_pairs : (couple + 1) * half_pairs], 0.0
        )
    weight_value = blend_ref[0].astype(jnp.float32)
    is_noise = lax.broadcasted_iota(jnp.int32, (half_pairs, wide), 1) < wide // 2
    even = jnp.where(is_noise, weight_value * pairs, weight_value)
    odd = jnp.where(is_noise, weight_value * pltpu.roll(pairs, wide // 2, 1), weight_value)
    parity = lax.axis_index("win") % 2
    right = 1 - parity if half == 0 else parity
    start_at = slab_cols - offset_ref[0] + right * slab_cols
    buffer_ref[...] = jnp.zeros_like(buffer_ref)
    buffer_ref[pl.ds(start_at, half_pairs, stride=2), :] = even
    buffer_ref[pl.ds(start_at + 1, half_pairs, stride=2), :] = odd
    center_ref[...] = buffer_ref[slab_cols : 2 * slab_cols]
    sent_ref[...] = jnp.where(
        right == 1, buffer_ref[2 * slab_cols : 3 * slab_cols], buffer_ref[:slab_cols]
    )


def blend_kernel(
    plan_ref, center_ref, near_ref, far_center_ref, far_ref, rows_ref, previous_ref, noise_ref
):
    channels, half_rows, slab_cols = noise_ref.shape
    total = (center_ref[...] + near_ref[...]) + (far_center_ref[...] + far_ref[...])
    total = jnp.transpose(total, (1, 0))
    half = total.shape[0] // 2
    noise = total[:half] / total[half:]
    scale = plan_ref[:, :slab_cols]
    previous = (
        scale[0:1] * (rows_ref[...] - scale[1:2] * noise) / scale[2:3] + scale[3:4] * noise
    )
    for channel in range(channels):
        rows = slice(channel * half_rows, (channel + 1) * half_rows)
        noise_ref[channel] = noise[rows]
        previous_ref[channel] = previous[rows]


def on_device(
    latent,
    text_kv,
    modulation,
    qkv_weight,
    out_weight,
    patch_weight,
    final_weight,
    offsets,
    blend_weights,
    step_index,
):
    slab_cols, channels, row_count = latent.shape
    model_width = patch_weight.shape[1]
    half_attn = out_weight.shape[0]
    heads = half_attn // HEAD_DIM
    branches, caption = text_kv.shape[0], text_kv.shape[2]
    col_pairs, row_couples = slab_cols, row_count // 2
    tokens = col_pairs * row_couples
    own_tokens = tokens // 2
    half_rows = row_count // 2
    far = swap_ring(latent, "win", 1)
    near = swap_ring(latent, "win", 0)
    hbm = pl.BlockSpec(memory_space=pltpu.HBM)
    keep = functools.partial(pltpu.with_memory_space_constraint, memory_space=pltpu.HBM)
    weight = jnp.transpose(qkv_weight, (1, 2, 0)).reshape(3 * half_attn, model_width)
    text = jnp.transpose(text_kv, (0, 1, 3, 2)).reshape(branches, 2, heads, HEAD_DIM, caption)
    final = jnp.transpose(final_weight, (1, 0))

    bf16, f32 = jnp.bfloat16, jnp.float32
    shape = jax.ShapeDtypeStruct
    wide = 2 * channels * half_rows
    half_width = model_width // 2
    below, above = half_width // 128 * 128, -(-half_width // 128) * 128
    row_part, col_part, patch_wide, quarter = pl.pallas_call(
        functools.partial(prepare_kernel, row_count),
        out_shape=(
            shape((row_couples, above), f32),
            shape((col_pairs, model_width - below), f32),
            shape((2 * channels * row_count, model_width), bf16),
            shape((half_attn // 4, model_width), bf16),
        ),
        in_specs=[hbm] * 2,
        out_specs=(VM,) * 4,
        scratch_shapes=[pltpu.VMEM(patch_weight.shape, bf16), pltpu.SemaphoreType.DMA((2,))],
        name="prepare",
        compiler_params=pltpu.CompilerParams(vmem_limit_bytes=GRANT),
        cost_estimate=pl.CostEstimate(flops=2*10**9, bytes_accessed=10**6, transcendentals=10**5),
    )(keep(patch_weight), keep(out_weight))
    other_weight = swap(quarter, "cfg")
    projected, normed, modulate, embedded, sent = pl.pallas_call(
        project_kernel,
        out_shape=(
            shape((3 * heads // 2, HEAD_DIM, tokens), bf16),
            shape((tokens, model_width), bf16),
            shape(modulation.shape[1:], f32),
            shape((tokens, model_width), f32),
            shape((half_attn // 2, branches * own_tokens), bf16),
        ),
        in_specs=[SM, SM] + [VM] * 9,
        out_specs=(VM,) * 5,
        scratch_shapes=[pltpu.VMEM((3 * slab_cols, channels * row_count), f32)],
        name="project",
        compiler_params=pltpu.CompilerParams(vmem_limit_bytes=GRANT),
        cost_estimate=pl.CostEstimate(flops=2 * 10**9, bytes_accessed=8 * 10**6, transcendentals=10**6),
    )(
        step_index, offsets, modulation, near, latent, far, row_part, col_part, patch_wide,
        weight, text,
    )
    early = swap(sent, "cfg")
    projected_late, sent_near, sent_far = pl.pallas_call(
        second_kernel,
        out_shape=(
            shape((3 * heads // 2, HEAD_DIM, tokens), bf16),
            shape((half_attn // 2, own_tokens), bf16),
            shape((half_attn // 2, own_tokens), bf16),
        ),
        in_specs=[VM] * 3,
        out_specs=(VM,) * 3,
        name="second",
        compiler_params=pltpu.CompilerParams(vmem_limit_bytes=GRANT),
        cost_estimate=pl.CostEstimate(flops=10**9, bytes_accessed=10**6, transcendentals=10**6),
    )(normed, text, weight)
    late_far = swap(sent_far, "cfg")
    late_near = swap(sent_near, "cfg")
    cross_weight = swap_across(other_weight, "win", 2)
    core_weight = swap_across(other_weight, "win", 1)
    core_cross_weight = swap_across(cross_weight, "win", 1)
    mixed, final_wide = pl.pallas_call(
        attend_kernel,
        out_shape=(
            shape((branches * own_tokens, model_width), f32),
            shape((wide, model_width), bf16),
        ),
        in_specs=[VM] * 5,
        out_specs=(VM, VM),
        name="attend",
        compiler_params=pltpu.CompilerParams(vmem_limit_bytes=GRANT),
        cost_estimate=pl.CostEstimate(flops=10**9, bytes_accessed=8 * 10**6, transcendentals=10**6),
    )(projected, projected_late, text, out_weight, final)

    def partial(half):
        return pl.pallas_call(
            functools.partial(partial_kernel, half),
            out_shape=shape((own_tokens, model_width), f32),
            in_specs=[VM] * 6,
            out_specs=VM,
            compiler_params=pltpu.CompilerParams(vmem_limit_bytes=GRANT),
            cost_estimate=pl.CostEstimate(flops=10**8, bytes_accessed=10**6, transcendentals=0),
        )(modulate, embedded, mixed, early, other_weight, core_weight)

    plan_values, rows = pl.pallas_call(
        coefficient_kernel,
        out_shape=(
            shape((8, -(-slab_cols // 128) * 128), f32),
            shape((channels * half_rows, slab_cols), f32),
        ),
        in_specs=[SM, VM],
        out_specs=(VM, VM),
        name="coefficient",
        compiler_params=pltpu.CompilerParams(vmem_limit_bytes=GRANT),
        cost_estimate=pl.CostEstimate(flops=10**5, bytes_accessed=10**5, transcendentals=10**4),
    )(step_index, latent)
    late_rows = pl.pallas_call(
        join_kernel,
        out_shape=shape((half_attn // 2, model_width), bf16),
        in_specs=[VM] * 2,
        out_specs=VM,
        name="join",
        compiler_params=pltpu.CompilerParams(vmem_limit_bytes=GRANT),
    )(cross_weight, core_cross_weight)

    def finish(half, residual, late):
        return pl.pallas_call(
            functools.partial(finish_kernel, half),
            out_shape=tuple(shape((slab_cols, wide), f32) for _ in range(2)),
            in_specs=[SM, SM] + [VM] * 5,
            out_specs=(VM, VM),
            scratch_shapes=[
                pltpu.VMEM((3 * slab_cols + 8, wide), f32),
                pltpu.VMEM((own_tokens, model_width), bf16),
            ],
            compiler_params=pltpu.CompilerParams(vmem_limit_bytes=GRANT),
            cost_estimate=pl.CostEstimate(
                flops=5 * 10**8, bytes_accessed=2 * 10**6, transcendentals=10**3
            ),
        )(offsets, blend_weights, modulate, residual, late, late_rows, final_wide)

    to_far, far_center = finish(1, partial(1), late_far)
    to_near, center = finish(0, partial(0), late_near)
    from_far = swap_ring(to_far, "win", 1)
    from_near = swap_ring(to_near, "win", 0)
    previous, noise = pl.pallas_call(
        blend_kernel,
        out_shape=tuple(shape((channels, half_rows, slab_cols), f32) for _ in range(2)),
        in_specs=[VM] * 6,
        out_specs=(VM, VM),
        name="blend",
        compiler_params=pltpu.CompilerParams(vmem_limit_bytes=GRANT),
    )(plan_values, center, from_near, far_center, from_far, rows)
    return (jnp.transpose(previous, (2, 0, 1)), jnp.transpose(noise, (2, 0, 1)))


def solution(mesh):
    in_specs = (
        P("win", None, None),
        P(None, None, None, "cfg"),
        P(),
        P(None, None, "cfg"),
        P("cfg", None),
        P(),
        P(),
        P("win"),
        P("win"),
        P(),
    )
    out_specs = (P("win", None, "cfg"), P("win", None, "cfg"))
    return jax.shard_map(
        on_device, mesh=mesh, in_specs=in_specs, out_specs=out_specs, check_vma=False
    )
```

```python
import functools
import math

import jax
import jax.numpy as jnp
from jax import lax
from jax.experimental import pallas as pl
from jax.experimental.pallas import tpu as pltpu
from jax.sharding import PartitionSpec as P


HEAD_DIM = 72
STEPS = 20


guidance_scale = 4.5
plan_length = 1000
norm_eps = 1e-06

VM = pl.BlockSpec(memory_space=pltpu.VMEM)
SM = pl.BlockSpec(memory_space=pltpu.SMEM)
GRANT = 24 * 2**20


def swap_ring(array, axis, odd):
    size = lax.axis_size(axis)
    pairs = []
    for left in range(odd, size, 2):
        right = (left + 1) % size
        pairs += [(left, right), (right, left)]
    return lax.ppermute(array, axis, pairs)


def swap(array, axis):
    return lax.ppermute(array, axis, [(0, 1), (1, 0)])


def swap_across(array, axis, even_step, odd_step):
    size = lax.axis_size(axis)
    steps = (even_step, odd_step)
    return lax.ppermute(array, axis, [(place, place ^ steps[place % 2]) for place in range(size)])


def layer_norm(values):
    average = jnp.mean(values, axis=-1, keepdims=True)
    centered = values - average
    variance = jnp.mean(centered * centered, axis=-1, keepdims=True)
    return centered * lax.rsqrt(variance + norm_eps)


def repeat_pairs(weight, repeats):
    rows, width = weight.shape
    values = weight.astype(jnp.float32)
    even = lax.broadcasted_iota(jnp.int32, (2 * repeats, width), 0) % 2 == 0
    parts = []
    for pair in range(rows // 2):
        parts.append(
            jnp.where(even, values[2 * pair : 2 * pair + 1, :], values[2 * pair + 1 : 2 * pair + 2, :])
        )
    return jnp.concatenate(parts, axis=0).astype(jnp.bfloat16)


def prepare_kernel(
    row_count,
    patch_source,
    out_source,
    row_ref,
    col_ref,
    patch_wide_ref,
    quarter_ref,
    patch_ref,
    semaphores,
):
    patch_copy = pltpu.make_async_copy(patch_source, patch_ref, semaphores.at[0])
    patch_copy.start()
    count = quarter_ref.shape[0]
    quarter = 2 * first_pair() + lax.axis_index("win") % 2
    first = pl.multiple_of(quarter * count, 8)
    copy = pltpu.make_async_copy(out_source.at[pl.ds(first, count)], quarter_ref, semaphores.at[1])
    copy.start()
    model_width = patch_ref.shape[1]
    quarter = model_width // 4

    def table(target_ref, first):
        count, lanes = target_ref.shape
        lane = first + lax.broadcasted_iota(jnp.int32, (count, lanes), 1)
        place = lax.broadcasted_iota(jnp.int32, (count, lanes), 0).astype(jnp.float32)
        frequency = jnp.exp(-math.log(10000.0) * (lane % quarter).astype(jnp.float32) / quarter)
        phase = jnp.where(lane // quarter % 2 == 0, 0.0, 0.5 * math.pi)
        target_ref[...] = jnp.sin(place * frequency + phase)

    table(row_ref, 0)
    table(col_ref, model_width - col_ref.shape[1])
    patch_copy.wait()
    patch_wide_ref[...] = repeat_pairs(patch_ref[...], row_count // 2)
    copy.wait()


def coefficient_kernel(step_ref, latent_ref, plan_ref, rows_ref):
    _, channels, row_count = latent_ref.shape
    moment = step_ref[0]
    index = lax.broadcasted_iota(jnp.int32, (8, 128), 0) * 128 + lax.broadcasted_iota(
        jnp.int32, (8, 128), 1
    )
    train = jnp.minimum(index, plan_length - 1).astype(jnp.float32)
    beta_values = 0.0001 + (0.02 - 0.0001) * train / (plan_length - 1)
    logs = jnp.log(1.0 - beta_values)

    def alpha_bar(last):
        kept = jnp.where((index <= last) & (index < plan_length), logs, 0.0)
        kept = jnp.sum(jnp.sum(kept, axis=0, keepdims=True), axis=1, keepdims=True)
        return jnp.exp(kept)

    alpha_now = alpha_bar(moment)
    alpha_before = alpha_bar(moment - plan_length // STEPS)
    for place, value in enumerate(
        (
            jnp.sqrt(alpha_before),
            jnp.sqrt(1.0 - alpha_now),
            jnp.sqrt(alpha_now),
            jnp.sqrt(1.0 - alpha_before),
        )
    ):
        plan_ref[place : place + 1, :] = jnp.broadcast_to(value, (1, plan_ref.shape[1]))

    half_rows = row_count // 2
    side = lax.axis_index("cfg")
    for channel in range(channels):
        turned = jnp.transpose(latent_ref[:, channel, :], (1, 0))
        rows_ref[channel * half_rows : (channel + 1) * half_rows, :] = jnp.where(
            side == 0, turned[:half_rows], turned[half_rows:]
        )


def first_pair():
    place = lax.axis_index("win")
    return (place // 2 + place // 4) % 2


def token_lanes(side, tokens):
    return [
        pl.multiple_of(half * (tokens // 2) + side * (tokens // 4), tokens // 4)
        for half in range(2)
    ]


def attend(parts, text_ref, first, count, chosen, finished):
    width = count // len(first)
    branches = text_ref.shape[0]
    feature = (((0,), (0,)), ((), ()))

    def place_of(head):
        pair = first_pair() if head < 2 else 1 - first_pair()
        return 2 * pair + head % 2

    def score(head):
        queries = jnp.concatenate(
            [parts[head // 2][head % 2, :, pl.ds(start, width)] for start in first], axis=1
        )
        return [
            lax.dot_general(keys, queries, feature, preferred_element_type=jnp.float32)
            for keys in [parts[head // 2][2 + head % 2]]
            + [text_ref[branch, 0, place_of(head)] for branch in range(branches)]
        ]

    def weigh(scores):
        own_highest = jnp.max(scores[0], axis=0, keepdims=True)
        own_exp = jnp.exp2(scores[0] - own_highest)
        own = (own_exp.astype(jnp.bfloat16), jnp.sum(own_exp, axis=0, keepdims=True))
        texts = []
        for text_scores in scores[1:]:
            highest = jnp.maximum(own_highest, jnp.max(text_scores, axis=0, keepdims=True))
            text_exp = jnp.exp2(text_scores - highest)
            lowered = jnp.exp2(own_highest - highest)
            total = lowered * own[1] + jnp.sum(text_exp, axis=0, keepdims=True)
            texts.append((text_exp.astype(jnp.bfloat16), lowered, 1.0 / total))
        return own[0], texts

    def mix(head, own_exp, texts):
        own_mix = jnp.dot(
            parts[head // 2][4 + head % 2], own_exp, preferred_element_type=jnp.float32
        )
        results = []
        for branch, (text_exp, lowered, inverse) in enumerate(texts):
            text_mix = jnp.dot(
                text_ref[branch, 1, place_of(head)], text_exp, preferred_element_type=jnp.float32
            )
            results.append((lowered * own_mix + text_mix) * inverse)
        return jnp.concatenate(
            [
                result[:, place * width : (place + 1) * width]
                for place in range(len(first))
                for result in results
            ],
            axis=1,
        )

    chosen = list(chosen)
    mixed = []

    def take(place, weights):
        mixed.append(mix(chosen[place], *weights))
        if place % 2:
            finished(place // 2, jnp.concatenate(mixed[-2:], axis=0).astype(jnp.bfloat16))

    ahead = score(chosen[0])
    before = None
    for place, head in enumerate(chosen):
        scores = ahead
        if place + 1 < len(chosen):
            ahead = score(chosen[place + 1])
        weights = weigh(scores)
        if before is not None:
            take(place - 1, before)
        before = weights
    take(len(chosen) - 1, before)


def keep_pair(target_ref, place, pair):
    target_ref[...] = pair


def pair_rows(weight_ref, pair):
    total = weight_ref.shape[0] // 3
    count = 2 * HEAD_DIM
    return jnp.concatenate(
        [
            weight_ref[pl.ds(pl.multiple_of(kind * total + pair * count, 16), count), :]
            for kind in range(3)
        ],
        axis=0,
    )


def project_half(weight_ref, pair, normed, target_ref, lanes):
    projected = lax.dot_general(
        pair_rows(weight_ref, pair), normed, (((1,), (1,)), ((), ())), preferred_element_type=jnp.float32
    )
    for block in range(target_ref.shape[0]):
        part = projected[block * HEAD_DIM : (block + 1) * HEAD_DIM]
        if block < target_ref.shape[0] // 3:
            part = part * (math.log2(math.e) / math.sqrt(HEAD_DIM))
        target_ref[block, :, lanes] = part.astype(jnp.bfloat16)


def project_kernel(
    step_ref,
    offset_ref,
    modulations_ref,
    near_ref,
    own_ref,
    far_ref,
    row_ref,
    col_ref,
    patch_ref,
    weight_ref,
    text_ref,
    proj_ref,
    normed_ref,
    modulation_ref,
    embedded_ref,
    sent_ref,
    extended_ref,
):
    modulation_ref[...] = modulations_ref[step_ref[0] * STEPS // plan_length]
    slab_cols, channels, row_count = own_ref.shape
    col_pairs, row_couples = slab_cols, row_count // 2
    tokens = col_pairs * row_couples
    own_tokens = tokens // 2
    wide = 2 * channels * row_count
    even = lax.axis_index("win") % 2 == 0
    for channel in range(channels):
        near, far = near_ref[:, channel, :], far_ref[:, channel, :]
        values = (jnp.where(even, far, near), own_ref[:, channel, :], jnp.where(even, near, far))
        for place, value in enumerate(values):
            extended_ref[
                place * slab_cols : (place + 1) * slab_cols,
                channel * row_count : (channel + 1) * row_count,
            ] = value
    extended = extended_ref[...].astype(jnp.bfloat16)
    start_at = slab_cols - offset_ref[0]
    chosen = lax.broadcasted_iota(jnp.int32, (2 * col_pairs, 3 * slab_cols), 0)
    column = lax.broadcasted_iota(jnp.int32, (2 * col_pairs, 3 * slab_cols), 1)
    half_pairs = col_pairs // 2
    parity = lax.axis_index("win") % 2
    near_first, far_first = (1 - parity) * half_pairs, parity * half_pairs
    group, within = chosen // half_pairs, chosen % half_pairs
    target = 2 * (within + jnp.where(group < 2, near_first, far_first)) + group % 2
    pick = jnp.where(column == target + start_at, 1.0, 0.0).astype(jnp.bfloat16)
    picked = jnp.dot(pick, extended, preferred_element_type=jnp.float32)
    groups = [picked[place * half_pairs : (place + 1) * half_pairs] for place in range(4)]
    lane_couple = lax.broadcasted_iota(jnp.int32, (half_pairs, wide), 1) % row_count // 2
    spread = []
    for place in range(2):
        pair = jnp.concatenate(groups[2 * place : 2 * place + 2], axis=1)
        spread.append(
            jnp.concatenate(
                [jnp.where(lane_couple == couple, pair, 0.0) for couple in range(row_couples)],
                axis=0,
            ).astype(jnp.bfloat16)
        )
    side = lax.axis_index("cfg")
    chunks = [slice(place * own_tokens, (place + 1) * own_tokens) for place in range(2)]

    model_width = patch_ref.shape[1]
    below, above = model_width - col_ref.shape[1], row_ref.shape[1]
    is_row = below + lax.broadcasted_iota(jnp.int32, (half_pairs, above - below), 1)
    is_row = is_row < model_width // 2

    def position(place, couple):
        line = jnp.broadcast_to(row_ref[couple : couple + 1, :], (half_pairs, above))
        column_first = near_first if place == 0 else far_first
        column = col_ref[pl.ds(pl.multiple_of(column_first, half_pairs), half_pairs), :]
        both = jnp.where(is_row, line[:, below:], column[:, : above - below])
        return jnp.concatenate([line[:, :below], both, column[:, above - below :]], axis=1)

    gain, shift = 1.0 + modulation_ref[1:2, :], modulation_ref[0:1, :]

    def embed(place):
        return jnp.dot(spread[place], patch_ref[...], preferred_element_type=jnp.float32)

    def norm(place, patches):
        for first_couple in range(0, row_couples, 2):
            rows = slice(first_couple * half_pairs, (first_couple + 2) * half_pairs)
            target = slice(place * own_tokens + rows.start, place * own_tokens + rows.stop)
            embedded = patches[rows] + jnp.concatenate(
                [position(place, first_couple + next_) for next_ in range(2)], axis=0
            )
            embedded_ref[target, :] = embedded
            normed = layer_norm(embedded) * gain + shift
            normed_ref[target, :] = normed.astype(jnp.bfloat16)

    early = embed(0)
    later = embed(1)
    norm(0, early)
    project_half(weight_ref, first_pair(), normed_ref[chunks[0], :], proj_ref, chunks[0])
    norm(1, later)
    project_half(weight_ref, first_pair(), normed_ref[chunks[1], :], proj_ref, chunks[1])
    first = token_lanes(1 - side, tokens)
    attend(
        [proj_ref], text_ref, first, own_tokens, range(2), functools.partial(keep_pair, sent_ref)
    )


def keep_halves(near_ref, far_ref, place, pair):
    count = near_ref.shape[1]
    near_ref[...] = pair[:, :count]
    far_ref[...] = pair[:, count:]


def second_kernel(normed_ref, text_ref, weight_ref, proj_ref, near_ref, far_ref):
    own_tokens = normed_ref.shape[0] // 2
    for place in range(2):
        chunk = slice(place * own_tokens, (place + 1) * own_tokens)
        project_half(weight_ref, 1 - first_pair(), normed_ref[chunk, :], proj_ref, chunk)
    first = token_lanes(1 - lax.axis_index("cfg"), 2 * own_tokens)
    attend(
        [None, proj_ref], text_ref, first, own_tokens, range(2, 4),
        functools.partial(keep_halves, near_ref, far_ref),
    )


def attend_kernel(half, early_ref, late_ref, text_ref, weight_ref, final_ref, *outputs):
    mixed_ref = outputs[0]
    if half == 1:
        final_wide_ref = outputs[1]
        final_wide_ref[...] = repeat_pairs(
            final_ref[...], final_wide_ref.shape[0] // final_ref.shape[0]
        )
    tokens = early_ref.shape[2]
    own_tokens = tokens // 4
    first = token_lanes(lax.axis_index("cfg"), tokens)[half : half + 1]
    pairs = []

    def finished(place, pair):
        pairs.append(pair)

    attend([early_ref, late_ref], text_ref, first, own_tokens, range(4), finished)
    count = 2 * HEAD_DIM
    mixed = []
    for place, pair in enumerate(pairs):
        chosen = first_pair() if place == 0 else 1 - first_pair()
        rows = pl.ds(pl.multiple_of(chosen * count, count), count)
        mixed.append(contract(pair, weight_ref[rows, :]))
    mixed_ref[...] = mixed[0] + mixed[1]


def contract(features, weight):
    return lax.dot_general(
        features, weight, (((0,), (0,)), ((), ())), preferred_element_type=jnp.float32
    )


def join(mine_ref, neighbour_ref):
    mine, neighbour = mine_ref[...].astype(jnp.float32), neighbour_ref[...].astype(jnp.float32)
    even_place = lax.axis_index("win") % 2 == 0
    first = jnp.where(even_place, mine, neighbour)
    second = jnp.where(even_place, neighbour, mine)
    return jnp.concatenate([first, second], axis=0).astype(jnp.bfloat16)


def join_kernel(mine_ref, neighbour_ref, joined_ref):
    joined_ref[...] = join(mine_ref, neighbour_ref)


def partial_kernel(
    half, modulation_ref, embedded_ref, mixed_ref, early_ref, weight_ref, core_ref, residual_ref
):
    count = residual_ref.shape[0] // 2
    lanes = slice(half * 2 * count, (half + 1) * 2 * count)
    mixed = contract(early_ref[:, lanes], join(weight_ref, core_ref)) + mixed_ref[...]
    first = pl.multiple_of(half * 2 * count + lax.axis_index("cfg") * count, count)
    embedded = embedded_ref[pl.ds(first, count), :]
    for branch in range(2):
        rows = slice(branch * count, (branch + 1) * count)
        residual_ref[rows, :] = embedded + modulation_ref[2:3, :] * mixed[rows]


def finish_kernel(
    half,
    offset_ref,
    blend_ref,
    modulation_ref,
    residual_ref,
    late_ref,
    weight_ref,
    final_ref,
    sent_ref,
    center_ref,
    buffer_ref,
    final_norm_ref,
):
    slab_cols, wide = center_ref.shape
    half_pairs = slab_cols // 2
    count = residual_ref.shape[0] // 2
    couples = count // half_pairs
    gate, gain = modulation_ref[2:3, :], 1.0 + modulation_ref[3:4, :]
    other = contract(late_ref[...], weight_ref[...])
    predicted = []
    block = slab_cols
    for branch in range(2):
        for place in range(count // block):
            rows = slice(branch * count + place * block, branch * count + (place + 1) * block)
            residual = residual_ref[rows, :] + gate * other[rows]
            final_norm_ref[rows, :] = (layer_norm(residual) * gain).astype(jnp.bfloat16)
        rows = slice(branch * count, (branch + 1) * count)
        predicted.append(
            lax.dot_general(
                final_norm_ref[rows, :],
                final_ref[...],
                (((1,), (1,)), ((), ())),
                preferred_element_type=jnp.float32,
            )
        )
    conditional, unconditional = predicted
    guided = unconditional + guidance_scale * (conditional - unconditional)
    lane_couple = lax.broadcasted_iota(jnp.int32, (half_pairs, wide), 1) % (2 * couples) // 2
    pairs = jnp.zeros((half_pairs, wide), jnp.float32)
    for couple in range(couples):
        pairs = pairs + jnp.where(
            lane_couple == couple, guided[couple * half_pairs : (couple + 1) * half_pairs], 0.0
        )
    weight_value = blend_ref[0].astype(jnp.float32)
    is_noise = lax.broadcasted_iota(jnp.int32, (half_pairs, wide), 1) < wide // 2
    even = jnp.where(is_noise, weight_value * pairs, weight_value)
    odd = jnp.where(is_noise, weight_value * pltpu.roll(pairs, wide // 2, 1), weight_value)
    parity = lax.axis_index("win") % 2
    right = 1 - parity if half == 0 else parity
    start_at = slab_cols - offset_ref[0] + right * slab_cols
    buffer_ref[...] = jnp.zeros_like(buffer_ref)
    buffer_ref[pl.ds(start_at, half_pairs, stride=2), :] = even
    buffer_ref[pl.ds(start_at + 1, half_pairs, stride=2), :] = odd
    center_ref[...] = buffer_ref[slab_cols : 2 * slab_cols]
    sent_ref[...] = jnp.where(
        right == 1, buffer_ref[2 * slab_cols : 3 * slab_cols], buffer_ref[:slab_cols]
    )


def blend_kernel(
    plan_ref, center_ref, near_ref, far_center_ref, far_ref, rows_ref, previous_ref, noise_ref
):
    channels, half_rows, slab_cols = noise_ref.shape
    total = (center_ref[...] + near_ref[...]) + (far_center_ref[...] + far_ref[...])
    total = jnp.transpose(total, (1, 0))
    half = total.shape[0] // 2
    noise = total[:half] / total[half:]
    scale = plan_ref[:, :slab_cols]
    previous = (
        scale[0:1] * (rows_ref[...] - scale[1:2] * noise) / scale[2:3] + scale[3:4] * noise
    )
    for channel in range(channels):
        rows = slice(channel * half_rows, (channel + 1) * half_rows)
        noise_ref[channel] = noise[rows]
        previous_ref[channel] = previous[rows]


def on_device(
    latent,
    text_kv,
    modulation,
    qkv_weight,
    out_weight,
    patch_weight,
    final_weight,
    offsets,
    blend_weights,
    step_index,
):
    slab_cols, channels, row_count = latent.shape
    model_width = patch_weight.shape[1]
    half_attn = out_weight.shape[0]
    heads = half_attn // HEAD_DIM
    branches, caption = text_kv.shape[0], text_kv.shape[2]
    col_pairs, row_couples = slab_cols, row_count // 2
    tokens = col_pairs * row_couples
    own_tokens = tokens // 2
    half_rows = row_count // 2
    far = swap_ring(latent, "win", 1)
    near = swap_ring(latent, "win", 0)
    hbm = pl.BlockSpec(memory_space=pltpu.HBM)
    keep = functools.partial(pltpu.with_memory_space_constraint, memory_space=pltpu.HBM)
    weight = jnp.transpose(qkv_weight, (1, 2, 0)).reshape(3 * half_attn, model_width)
    text = jnp.transpose(text_kv, (0, 1, 3, 2)).reshape(branches, 2, heads, HEAD_DIM, caption)
    final = jnp.transpose(final_weight, (1, 0))

    bf16, f32 = jnp.bfloat16, jnp.float32
    shape = jax.ShapeDtypeStruct
    wide = 2 * channels * half_rows
    half_width = model_width // 2
    below, above = half_width // 128 * 128, -(-half_width // 128) * 128
    row_part, col_part, patch_wide, quarter = pl.pallas_call(
        functools.partial(prepare_kernel, row_count),
        out_shape=(
            shape((row_couples, above), f32),
            shape((col_pairs, model_width - below), f32),
            shape((2 * channels * row_count, model_width), bf16),
            shape((half_attn // 4, model_width), bf16),
        ),
        in_specs=[hbm] * 2,
        out_specs=(VM,) * 4,
        scratch_shapes=[pltpu.VMEM(patch_weight.shape, bf16), pltpu.SemaphoreType.DMA((2,))],
        name="prepare",
        compiler_params=pltpu.CompilerParams(vmem_limit_bytes=GRANT),
        cost_estimate=pl.CostEstimate(flops=2*10**9, bytes_accessed=10**6, transcendentals=10**5),
    )(keep(patch_weight), keep(out_weight))
    other_weight = swap(quarter, "cfg")
    projected, normed, modulate, embedded, sent = pl.pallas_call(
        project_kernel,
        out_shape=(
            shape((3 * heads // 2, HEAD_DIM, tokens), bf16),
            shape((tokens, model_width), bf16),
            shape(modulation.shape[1:], f32),
            shape((tokens, model_width), f32),
            shape((half_attn // 2, branches * own_tokens), bf16),
        ),
        in_specs=[SM, SM] + [VM] * 9,
        out_specs=(VM,) * 5,
        scratch_shapes=[pltpu.VMEM((3 * slab_cols, channels * row_count), f32)],
        name="project",
        compiler_params=pltpu.CompilerParams(vmem_limit_bytes=GRANT),
        cost_estimate=pl.CostEstimate(flops=2 * 10**9, bytes_accessed=8 * 10**6, transcendentals=10**6),
    )(
        step_index, offsets, modulation, near, latent, far, row_part, col_part, patch_wide,
        weight, text,
    )
    early = swap(sent, "cfg")
    projected_late, sent_near, sent_far = pl.pallas_call(
        second_kernel,
        out_shape=(
            shape((3 * heads // 2, HEAD_DIM, tokens), bf16),
            shape((half_attn // 2, own_tokens), bf16),
            shape((half_attn // 2, own_tokens), bf16),
        ),
        in_specs=[VM] * 3,
        out_specs=(VM,) * 3,
        name="second",
        compiler_params=pltpu.CompilerParams(vmem_limit_bytes=GRANT),
        cost_estimate=pl.CostEstimate(flops=10**9, bytes_accessed=10**6, transcendentals=10**6),
    )(normed, text, weight)
    late_far = swap(sent_far, "cfg")
    late_near = swap(sent_near, "cfg")
    cross_weight = swap_across(other_weight, "win", 2, 4)
    core_weight = swap_across(other_weight, "win", 1, 1)
    core_cross_weight = swap_across(cross_weight, "win", 1, 1)

    def attend_own(half):
        return pl.pallas_call(
            functools.partial(attend_kernel, half),
            out_shape=(shape((own_tokens, model_width), f32), shape((wide, model_width), bf16))[
                : half + 1
            ],
            in_specs=[VM] * 5,
            out_specs=(VM, VM)[: half + 1],
            compiler_params=pltpu.CompilerParams(vmem_limit_bytes=GRANT),
            cost_estimate=pl.CostEstimate(
                flops=5 * 10**8, bytes_accessed=4 * 10**6, transcendentals=5 * 10**5
            ),
        )(projected, projected_late, text, out_weight, final)

    mixed_far, final_wide = attend_own(1)
    (mixed_near,) = attend_own(0)

    def partial(half, mixed):
        return pl.pallas_call(
            functools.partial(partial_kernel, half),
            out_shape=shape((own_tokens, model_width), f32),
            in_specs=[VM] * 6,
            out_specs=VM,
            compiler_params=pltpu.CompilerParams(vmem_limit_bytes=GRANT),
            cost_estimate=pl.CostEstimate(flops=10**8, bytes_accessed=10**6, transcendentals=0),
        )(modulate, embedded, mixed, early, other_weight, core_weight)

    plan_values, rows = pl.pallas_call(
        coefficient_kernel,
        out_shape=(
            shape((8, -(-slab_cols // 128) * 128), f32),
            shape((channels * half_rows, slab_cols), f32),
        ),
        in_specs=[SM, VM],
        out_specs=(VM, VM),
        name="coefficient",
        compiler_params=pltpu.CompilerParams(vmem_limit_bytes=GRANT),
        cost_estimate=pl.CostEstimate(flops=10**5, bytes_accessed=10**5, transcendentals=10**4),
    )(step_index, latent)
    late_rows = pl.pallas_call(
        join_kernel,
        out_shape=shape((half_attn // 2, model_width), bf16),
        in_specs=[VM] * 2,
        out_specs=VM,
        name="join",
        compiler_params=pltpu.CompilerParams(vmem_limit_bytes=GRANT),
    )(cross_weight, core_cross_weight)

    def finish(half, residual, late):
        return pl.pallas_call(
            functools.partial(finish_kernel, half),
            out_shape=tuple(shape((slab_cols, wide), f32) for _ in range(2)),
            in_specs=[SM, SM] + [VM] * 5,
            out_specs=(VM, VM),
            scratch_shapes=[
                pltpu.VMEM((3 * slab_cols + 8, wide), f32),
                pltpu.VMEM((own_tokens, model_width), bf16),
            ],
            compiler_params=pltpu.CompilerParams(vmem_limit_bytes=GRANT),
            cost_estimate=pl.CostEstimate(
                flops=5 * 10**8, bytes_accessed=2 * 10**6, transcendentals=10**3
            ),
        )(offsets, blend_weights, modulate, residual, late, late_rows, final_wide)

    to_far, far_center = finish(1, partial(1, mixed_far), late_far)
    to_near, center = finish(0, partial(0, mixed_near), late_near)
    from_far = swap_ring(to_far, "win", 1)
    from_near = swap_ring(to_near, "win", 0)
    previous, noise = pl.pallas_call(
        blend_kernel,
        out_shape=tuple(shape((channels, half_rows, slab_cols), f32) for _ in range(2)),
        in_specs=[VM] * 6,
        out_specs=(VM, VM),
        name="blend",
        compiler_params=pltpu.CompilerParams(vmem_limit_bytes=GRANT),
    )(plan_values, center, from_near, far_center, from_far, rows)
    return (jnp.transpose(previous, (2, 0, 1)), jnp.transpose(noise, (2, 0, 1)))


def solution(mesh):
    in_specs = (
        P("win", None, None),
        P(None, None, None, "cfg"),
        P(),
        P(None, None, "cfg"),
        P("cfg", None),
        P(),
        P(),
        P("win"),
        P("win"),
        P(),
    )
    out_specs = (P("win", None, "cfg"), P("win", None, "cfg"))
    return jax.shard_map(
        on_device, mesh=mesh, in_specs=in_specs, out_specs=out_specs, check_vma=False
    )
```

```python
import functools
import math

import jax
import jax.numpy as jnp
from jax import lax
from jax.experimental import pallas as pl
from jax.experimental.pallas import tpu as pltpu
from jax.sharding import PartitionSpec as P


HEAD_DIM = 72
STEPS = 20


guidance_scale = 4.5
plan_length = 1000
norm_eps = 1e-06

VM = pl.BlockSpec(memory_space=pltpu.VMEM)
SM = pl.BlockSpec(memory_space=pltpu.SMEM)
GRANT = 24 * 2**20


def swap_ring(array, axis, odd):
    size = lax.axis_size(axis)
    pairs = []
    for left in range(odd, size, 2):
        right = (left + 1) % size
        pairs += [(left, right), (right, left)]
    return lax.ppermute(array, axis, pairs)


def swap(array, axis):
    return lax.ppermute(array, axis, [(0, 1), (1, 0)])


def swap_across(array, axis, even_step, odd_step):
    size = lax.axis_size(axis)
    steps = (even_step, odd_step)
    return lax.ppermute(array, axis, [(place, place ^ steps[place % 2]) for place in range(size)])


def layer_norm(values):
    average = jnp.mean(values, axis=-1, keepdims=True)
    centered = values - average
    variance = jnp.mean(centered * centered, axis=-1, keepdims=True)
    return centered * lax.rsqrt(variance + norm_eps)


def repeat_pairs(weight, repeats):
    rows, width = weight.shape
    values = weight.astype(jnp.float32)
    even = lax.broadcasted_iota(jnp.int32, (2 * repeats, width), 0) % 2 == 0
    parts = []
    for pair in range(rows // 2):
        parts.append(
            jnp.where(even, values[2 * pair : 2 * pair + 1, :], values[2 * pair + 1 : 2 * pair + 2, :])
        )
    return jnp.concatenate(parts, axis=0).astype(jnp.bfloat16)


def prepare_kernel(
    row_count,
    patch_source,
    out_source,
    row_ref,
    col_ref,
    patch_wide_ref,
    quarter_ref,
    patch_ref,
    semaphores,
):
    patch_copy = pltpu.make_async_copy(patch_source, patch_ref, semaphores.at[0])
    patch_copy.start()
    count = quarter_ref.shape[0]
    quarter = 2 * first_pair() + lax.axis_index("win") % 2
    first = pl.multiple_of(quarter * count, 8)
    copy = pltpu.make_async_copy(out_source.at[pl.ds(first, count)], quarter_ref, semaphores.at[1])
    copy.start()
    model_width = patch_ref.shape[1]
    quarter = model_width // 4

    def table(target_ref, first):
        count, lanes = target_ref.shape
        lane = first + lax.broadcasted_iota(jnp.int32, (count, lanes), 1)
        place = lax.broadcasted_iota(jnp.int32, (count, lanes), 0).astype(jnp.float32)
        frequency = jnp.exp(-math.log(10000.0) * (lane % quarter).astype(jnp.float32) / quarter)
        phase = jnp.where(lane // quarter % 2 == 0, 0.0, 0.5 * math.pi)
        target_ref[...] = jnp.sin(place * frequency + phase)

    table(row_ref, 0)
    table(col_ref, model_width - col_ref.shape[1])
    patch_copy.wait()
    patch_wide_ref[...] = repeat_pairs(patch_ref[...], row_count // 2)
    copy.wait()


def coefficient_kernel(step_ref, latent_ref, plan_ref, rows_ref):
    _, channels, row_count = latent_ref.shape
    moment = step_ref[0]
    index = lax.broadcasted_iota(jnp.int32, (8, 128), 0) * 128 + lax.broadcasted_iota(
        jnp.int32, (8, 128), 1
    )
    train = jnp.minimum(index, plan_length - 1).astype(jnp.float32)
    beta_values = 0.0001 + (0.02 - 0.0001) * train / (plan_length - 1)
    logs = jnp.log(1.0 - beta_values)

    def alpha_bar(last):
        kept = jnp.where((index <= last) & (index < plan_length), logs, 0.0)
        kept = jnp.sum(jnp.sum(kept, axis=0, keepdims=True), axis=1, keepdims=True)
        return jnp.exp(kept)

    alpha_now = alpha_bar(moment)
    alpha_before = alpha_bar(moment - plan_length // STEPS)
    for place, value in enumerate(
        (
            jnp.sqrt(alpha_before),
            jnp.sqrt(1.0 - alpha_now),
            jnp.sqrt(alpha_now),
            jnp.sqrt(1.0 - alpha_before),
        )
    ):
        plan_ref[place : place + 1, :] = jnp.broadcast_to(value, (1, plan_ref.shape[1]))

    half_rows = row_count // 2
    side = lax.axis_index("cfg")
    for channel in range(channels):
        turned = jnp.transpose(latent_ref[:, channel, :], (1, 0))
        rows_ref[channel * half_rows : (channel + 1) * half_rows, :] = jnp.where(
            side == 0, turned[:half_rows], turned[half_rows:]
        )


def first_pair():
    place = lax.axis_index("win")
    return (place // 2 + place // 4) % 2


def token_lanes(side, tokens):
    return [
        pl.multiple_of(half * (tokens // 2) + side * (tokens // 4), tokens // 4)
        for half in range(2)
    ]


def attend(parts, text_ref, first, count, chosen, finished):
    width = count // len(first)
    branches = text_ref.shape[0]
    feature = (((0,), (0,)), ((), ()))

    def place_of(head):
        pair = first_pair() if head < 2 else 1 - first_pair()
        return 2 * pair + head % 2

    def score(head):
        queries = jnp.concatenate(
            [parts[head // 2][head % 2, :, pl.ds(start, width)] for start in first], axis=1
        )
        return [
            lax.dot_general(keys, queries, feature, preferred_element_type=jnp.float32)
            for keys in [parts[head // 2][2 + head % 2]]
            + [text_ref[branch, 0, place_of(head)] for branch in range(branches)]
        ]

    def weigh(scores):
        own_highest = jnp.max(scores[0], axis=0, keepdims=True)
        own_exp = jnp.exp2(scores[0] - own_highest)
        own = (own_exp.astype(jnp.bfloat16), jnp.sum(own_exp, axis=0, keepdims=True))
        texts = []
        for text_scores in scores[1:]:
            highest = jnp.maximum(own_highest, jnp.max(text_scores, axis=0, keepdims=True))
            text_exp = jnp.exp2(text_scores - highest)
            lowered = jnp.exp2(own_highest - highest)
            total = lowered * own[1] + jnp.sum(text_exp, axis=0, keepdims=True)
            texts.append((text_exp.astype(jnp.bfloat16), lowered, 1.0 / total))
        return own[0], texts

    def mix(head, own_exp, texts):
        own_mix = jnp.dot(
            parts[head // 2][4 + head % 2], own_exp, preferred_element_type=jnp.float32
        )
        results = []
        for branch, (text_exp, lowered, inverse) in enumerate(texts):
            text_mix = jnp.dot(
                text_ref[branch, 1, place_of(head)], text_exp, preferred_element_type=jnp.float32
            )
            results.append((lowered * own_mix + text_mix) * inverse)
        return jnp.concatenate(
            [
                result[:, place * width : (place + 1) * width]
                for place in range(len(first))
                for result in results
            ],
            axis=1,
        )

    chosen = list(chosen)
    mixed = []

    def take(place, weights):
        mixed.append(mix(chosen[place], *weights))
        if place % 2:
            finished(place // 2, jnp.concatenate(mixed[-2:], axis=0).astype(jnp.bfloat16))

    ahead = score(chosen[0])
    before = None
    for place, head in enumerate(chosen):
        scores = ahead
        if place + 1 < len(chosen):
            ahead = score(chosen[place + 1])
        weights = weigh(scores)
        if before is not None:
            take(place - 1, before)
        before = weights
    take(len(chosen) - 1, before)


def keep_pair(target_ref, place, pair):
    target_ref[...] = pair


def pair_rows(weight_ref, pair):
    total = weight_ref.shape[0] // 3
    count = 2 * HEAD_DIM
    return jnp.concatenate(
        [
            weight_ref[pl.ds(pl.multiple_of(kind * total + pair * count, 16), count), :]
            for kind in range(3)
        ],
        axis=0,
    )


def project_half(weight_ref, pair, normed, target_ref, lanes):
    projected = lax.dot_general(
        pair_rows(weight_ref, pair), normed, (((1,), (1,)), ((), ())), preferred_element_type=jnp.float32
    )
    for block in range(target_ref.shape[0]):
        part = projected[block * HEAD_DIM : (block + 1) * HEAD_DIM]
        if block < target_ref.shape[0] // 3:
            part = part * (math.log2(math.e) / math.sqrt(HEAD_DIM))
        target_ref[block, :, lanes] = part.astype(jnp.bfloat16)


def project_kernel(
    step_ref,
    offset_ref,
    modulations_ref,
    near_ref,
    own_ref,
    far_ref,
    row_ref,
    col_ref,
    patch_ref,
    weight_ref,
    text_ref,
    proj_ref,
    normed_ref,
    modulation_ref,
    embedded_ref,
    sent_ref,
    extended_ref,
):
    modulation_ref[...] = modulations_ref[step_ref[0] * STEPS // plan_length]
    slab_cols, channels, row_count = own_ref.shape
    col_pairs, row_couples = slab_cols, row_count // 2
    tokens = col_pairs * row_couples
    own_tokens = tokens // 2
    wide = 2 * channels * row_count
    even = lax.axis_index("win") % 2 == 0
    for channel in range(channels):
        near, far = near_ref[:, channel, :], far_ref[:, channel, :]
        values = (jnp.where(even, far, near), own_ref[:, channel, :], jnp.where(even, near, far))
        for place, value in enumerate(values):
            extended_ref[
                place * slab_cols : (place + 1) * slab_cols,
                channel * row_count : (channel + 1) * row_count,
            ] = value
    extended = extended_ref[...].astype(jnp.bfloat16)
    start_at = slab_cols - offset_ref[0]
    chosen = lax.broadcasted_iota(jnp.int32, (2 * col_pairs, 3 * slab_cols), 0)
    column = lax.broadcasted_iota(jnp.int32, (2 * col_pairs, 3 * slab_cols), 1)
    half_pairs = col_pairs // 2
    parity = lax.axis_index("win") % 2
    near_first, far_first = (1 - parity) * half_pairs, parity * half_pairs
    group, within = chosen // half_pairs, chosen % half_pairs
    target = 2 * (within + jnp.where(group < 2, near_first, far_first)) + group % 2
    pick = jnp.where(column == target + start_at, 1.0, 0.0).astype(jnp.bfloat16)
    picked = jnp.dot(pick, extended, preferred_element_type=jnp.float32)
    groups = [picked[place * half_pairs : (place + 1) * half_pairs] for place in range(4)]
    lane_couple = lax.broadcasted_iota(jnp.int32, (half_pairs, wide), 1) % row_count // 2
    spread = []
    for place in range(2):
        pair = jnp.concatenate(groups[2 * place : 2 * place + 2], axis=1)
        spread.append(
            jnp.concatenate(
                [jnp.where(lane_couple == couple, pair, 0.0) for couple in range(row_couples)],
                axis=0,
            ).astype(jnp.bfloat16)
        )
    side = lax.axis_index("cfg")
    chunks = [slice(place * own_tokens, (place + 1) * own_tokens) for place in range(2)]

    model_width = patch_ref.shape[1]
    below, above = model_width - col_ref.shape[1], row_ref.shape[1]
    is_row = below + lax.broadcasted_iota(jnp.int32, (half_pairs, above - below), 1)
    is_row = is_row < model_width // 2

    def position(place, couple):
        line = jnp.broadcast_to(row_ref[couple : couple + 1, :], (half_pairs, above))
        column_first = near_first if place == 0 else far_first
        column = col_ref[pl.ds(pl.multiple_of(column_first, half_pairs), half_pairs), :]
        both = jnp.where(is_row, line[:, below:], column[:, : above - below])
        return jnp.concatenate([line[:, :below], both, column[:, above - below :]], axis=1)

    gain, shift = 1.0 + modulation_ref[1:2, :], modulation_ref[0:1, :]

    def embed(place):
        return jnp.dot(spread[place], patch_ref[...], preferred_element_type=jnp.float32)

    def norm(place, patches):
        for first_couple in range(0, row_couples, 2):
            rows = slice(first_couple * half_pairs, (first_couple + 2) * half_pairs)
            target = slice(place * own_tokens + rows.start, place * own_tokens + rows.stop)
            embedded = patches[rows] + jnp.concatenate(
                [position(place, first_couple + next_) for next_ in range(2)], axis=0
            )
            embedded_ref[target, :] = embedded
            normed = layer_norm(embedded) * gain + shift
            normed_ref[target, :] = normed.astype(jnp.bfloat16)

    early = embed(0)
    later = embed(1)
    norm(0, early)
    project_half(weight_ref, first_pair(), normed_ref[chunks[0], :], proj_ref, chunks[0])
    norm(1, later)
    project_half(weight_ref, first_pair(), normed_ref[chunks[1], :], proj_ref, chunks[1])
    first = token_lanes(1 - side, tokens)
    attend(
        [proj_ref], text_ref, first, own_tokens, range(2), functools.partial(keep_pair, sent_ref)
    )


def keep_halves(near_ref, far_ref, place, pair):
    count = near_ref.shape[1]
    near_ref[...] = pair[:, :count]
    far_ref[...] = pair[:, count:]


def second_kernel(normed_ref, text_ref, weight_ref, proj_ref, near_ref, far_ref):
    own_tokens = normed_ref.shape[0] // 2
    for place in range(2):
        chunk = slice(place * own_tokens, (place + 1) * own_tokens)
        project_half(weight_ref, 1 - first_pair(), normed_ref[chunk, :], proj_ref, chunk)
    first = token_lanes(1 - lax.axis_index("cfg"), 2 * own_tokens)
    attend(
        [None, proj_ref], text_ref, first, own_tokens, range(2, 4),
        functools.partial(keep_halves, near_ref, far_ref),
    )


def attend_kernel(half, early_ref, late_ref, text_ref, weight_ref, final_ref, *outputs):
    mixed_ref = outputs[0]
    if half == 1:
        final_wide_ref = outputs[1]
        final_wide_ref[...] = repeat_pairs(
            final_ref[...], final_wide_ref.shape[0] // final_ref.shape[0]
        )
    tokens = early_ref.shape[2]
    own_tokens = tokens // 4
    first = token_lanes(lax.axis_index("cfg"), tokens)[half : half + 1]
    pairs = []

    def finished(place, pair):
        pairs.append(pair)

    attend([early_ref, late_ref], text_ref, first, own_tokens, range(4), finished)
    count = 2 * HEAD_DIM
    mixed = []
    for place, pair in enumerate(pairs):
        chosen = first_pair() if place == 0 else 1 - first_pair()
        rows = pl.ds(pl.multiple_of(chosen * count, count), count)
        mixed.append(contract(pair, weight_ref[rows, :]))
    mixed_ref[...] = mixed[0] + mixed[1]


def contract(features, weight):
    return lax.dot_general(
        features, weight, (((0,), (0,)), ((), ())), preferred_element_type=jnp.float32
    )


def join(mine_ref, neighbour_ref):
    mine, neighbour = mine_ref[...].astype(jnp.float32), neighbour_ref[...].astype(jnp.float32)
    even_place = lax.axis_index("win") % 2 == 0
    first = jnp.where(even_place, mine, neighbour)
    second = jnp.where(even_place, neighbour, mine)
    return jnp.concatenate([first, second], axis=0).astype(jnp.bfloat16)


def join_kernel(mine_ref, neighbour_ref, joined_ref):
    joined_ref[...] = join(mine_ref, neighbour_ref)


def partial_kernel(
    half, modulation_ref, embedded_ref, mixed_ref, early_ref, weight_ref, core_ref, residual_ref
):
    count = residual_ref.shape[0] // 2
    lanes = slice(half * 2 * count, (half + 1) * 2 * count)
    mixed = contract(early_ref[:, lanes], join(weight_ref, core_ref)) + mixed_ref[...]
    first = pl.multiple_of(half * 2 * count + lax.axis_index("cfg") * count, count)
    embedded = embedded_ref[pl.ds(first, count), :]
    for branch in range(2):
        rows = slice(branch * count, (branch + 1) * count)
        residual_ref[rows, :] = embedded + modulation_ref[2:3, :] * mixed[rows]


def finish_kernel(
    half,
    offset_ref,
    blend_ref,
    modulation_ref,
    residual_ref,
    late_ref,
    weight_ref,
    final_ref,
    sent_ref,
    center_ref,
    buffer_ref,
    final_norm_ref,
):
    slab_cols, wide = center_ref.shape
    half_pairs = slab_cols // 2
    count = residual_ref.shape[0] // 2
    couples = count // half_pairs
    gate, gain = modulation_ref[2:3, :], 1.0 + modulation_ref[3:4, :]
    other = contract(late_ref[...], weight_ref[...])
    predicted = []
    block = slab_cols
    for branch in range(2):
        for place in range(count // block):
            rows = slice(branch * count + place * block, branch * count + (place + 1) * block)
            residual = residual_ref[rows, :] + gate * other[rows]
            final_norm_ref[rows, :] = (layer_norm(residual) * gain).astype(jnp.bfloat16)
        rows = slice(branch * count, (branch + 1) * count)
        predicted.append(
            lax.dot_general(
                final_norm_ref[rows, :],
                final_ref[...],
                (((1,), (1,)), ((), ())),
                preferred_element_type=jnp.float32,
            )
        )
    conditional, unconditional = predicted
    guided = unconditional + guidance_scale * (conditional - unconditional)
    lane_couple = lax.broadcasted_iota(jnp.int32, (half_pairs, wide), 1) % (2 * couples) // 2
    pairs = jnp.zeros((half_pairs, wide), jnp.float32)
    for couple in range(couples):
        pairs = pairs + jnp.where(
            lane_couple == couple, guided[couple * half_pairs : (couple + 1) * half_pairs], 0.0
        )
    weight_value = blend_ref[0].astype(jnp.float32)
    is_noise = lax.broadcasted_iota(jnp.int32, (half_pairs, wide), 1) < wide // 2
    even = jnp.where(is_noise, weight_value * pairs, weight_value)
    odd = jnp.where(is_noise, weight_value * pltpu.roll(pairs, wide // 2, 1), weight_value)
    parity = lax.axis_index("win") % 2
    right = 1 - parity if half == 0 else parity
    start_at = slab_cols - offset_ref[0] + right * slab_cols
    buffer_ref[...] = jnp.zeros_like(buffer_ref)
    buffer_ref[pl.ds(start_at, half_pairs, stride=2), :] = even
    buffer_ref[pl.ds(start_at + 1, half_pairs, stride=2), :] = odd
    center_ref[...] = buffer_ref[slab_cols : 2 * slab_cols]
    sent_ref[...] = jnp.where(
        right == 1, buffer_ref[2 * slab_cols : 3 * slab_cols], buffer_ref[:slab_cols]
    )


def near_kernel(
    offset_ref,
    blend_ref,
    modulation_ref,
    embedded_ref,
    first_ref,
    second_ref,
    text_ref,
    own_weight_ref,
    early_ref,
    weight_ref,
    core_ref,
    late_ref,
    late_weight_ref,
    final_ref,
    sent_ref,
    center_ref,
    mixed_ref,
    residual_ref,
    buffer_ref,
    final_norm_ref,
):
    attend_kernel(0, first_ref, second_ref, text_ref, own_weight_ref, None, mixed_ref)
    partial_kernel(
        0, modulation_ref, embedded_ref, mixed_ref, early_ref, weight_ref, core_ref, residual_ref
    )
    finish_kernel(
        0, offset_ref, blend_ref, modulation_ref, residual_ref, late_ref, late_weight_ref,
        final_ref, sent_ref, center_ref, buffer_ref, final_norm_ref,
    )


def blend_kernel(
    plan_ref, center_ref, near_ref, far_center_ref, far_ref, rows_ref, previous_ref, noise_ref
):
    channels, half_rows, slab_cols = noise_ref.shape
    total = (center_ref[...] + near_ref[...]) + (far_center_ref[...] + far_ref[...])
    total = jnp.transpose(total, (1, 0))
    half = total.shape[0] // 2
    noise = total[:half] / total[half:]
    scale = plan_ref[:, :slab_cols]
    previous = (
        scale[0:1] * (rows_ref[...] - scale[1:2] * noise) / scale[2:3] + scale[3:4] * noise
    )
    for channel in range(channels):
        rows = slice(channel * half_rows, (channel + 1) * half_rows)
        noise_ref[channel] = noise[rows]
        previous_ref[channel] = previous[rows]


def on_device(
    latent,
    text_kv,
    modulation,
    qkv_weight,
    out_weight,
    patch_weight,
    final_weight,
    offsets,
    blend_weights,
    step_index,
):
    slab_cols, channels, row_count = latent.shape
    model_width = patch_weight.shape[1]
    half_attn = out_weight.shape[0]
    heads = half_attn // HEAD_DIM
    branches, caption = text_kv.shape[0], text_kv.shape[2]
    col_pairs, row_couples = slab_cols, row_count // 2
    tokens = col_pairs * row_couples
    own_tokens = tokens // 2
    half_rows = row_count // 2
    far = swap_ring(latent, "win", 1)
    near = swap_ring(latent, "win", 0)
    hbm = pl.BlockSpec(memory_space=pltpu.HBM)
    keep = functools.partial(pltpu.with_memory_space_constraint, memory_space=pltpu.HBM)
    weight = jnp.transpose(qkv_weight, (1, 2, 0)).reshape(3 * half_attn, model_width)
    text = jnp.transpose(text_kv, (0, 1, 3, 2)).reshape(branches, 2, heads, HEAD_DIM, caption)
    final = jnp.transpose(final_weight, (1, 0))

    bf16, f32 = jnp.bfloat16, jnp.float32
    shape = jax.ShapeDtypeStruct
    wide = 2 * channels * half_rows
    half_width = model_width // 2
    below, above = half_width // 128 * 128, -(-half_width // 128) * 128
    row_part, col_part, patch_wide, quarter = pl.pallas_call(
        functools.partial(prepare_kernel, row_count),
        out_shape=(
            shape((row_couples, above), f32),
            shape((col_pairs, model_width - below), f32),
            shape((2 * channels * row_count, model_width), bf16),
            shape((half_attn // 4, model_width), bf16),
        ),
        in_specs=[hbm] * 2,
        out_specs=(VM,) * 4,
        scratch_shapes=[pltpu.VMEM(patch_weight.shape, bf16), pltpu.SemaphoreType.DMA((2,))],
        name="prepare",
        compiler_params=pltpu.CompilerParams(vmem_limit_bytes=GRANT),
        cost_estimate=pl.CostEstimate(flops=2*10**9, bytes_accessed=10**6, transcendentals=10**5),
    )(keep(patch_weight), keep(out_weight))
    other_weight = swap(quarter, "cfg")
    projected, normed, modulate, embedded, sent = pl.pallas_call(
        project_kernel,
        out_shape=(
            shape((3 * heads // 2, HEAD_DIM, tokens), bf16),
            shape((tokens, model_width), bf16),
            shape(modulation.shape[1:], f32),
            shape((tokens, model_width), f32),
            shape((half_attn // 2, branches * own_tokens), bf16),
        ),
        in_specs=[SM, SM] + [VM] * 9,
        out_specs=(VM,) * 5,
        scratch_shapes=[pltpu.VMEM((3 * slab_cols, channels * row_count), f32)],
        name="project",
        compiler_params=pltpu.CompilerParams(vmem_limit_bytes=GRANT),
        cost_estimate=pl.CostEstimate(flops=2 * 10**9, bytes_accessed=8 * 10**6, transcendentals=10**6),
    )(
        step_index, offsets, modulation, near, latent, far, row_part, col_part, patch_wide,
        weight, text,
    )
    early = swap(sent, "cfg")
    projected_late, sent_near, sent_far = pl.pallas_call(
        second_kernel,
        out_shape=(
            shape((3 * heads // 2, HEAD_DIM, tokens), bf16),
            shape((half_attn // 2, own_tokens), bf16),
            shape((half_attn // 2, own_tokens), bf16),
        ),
        in_specs=[VM] * 3,
        out_specs=(VM,) * 3,
        name="second",
        compiler_params=pltpu.CompilerParams(vmem_limit_bytes=GRANT),
        cost_estimate=pl.CostEstimate(flops=10**9, bytes_accessed=10**6, transcendentals=10**6),
    )(normed, text, weight)
    late_far = swap(sent_far, "cfg")
    late_near = swap(sent_near, "cfg")
    cross_weight = swap_across(other_weight, "win", 2, 4)
    core_weight = swap_across(other_weight, "win", 1, 1)
    core_cross_weight = swap_across(cross_weight, "win", 1, 1)

    def attend_own(half):
        return pl.pallas_call(
            functools.partial(attend_kernel, half),
            out_shape=(shape((own_tokens, model_width), f32), shape((wide, model_width), bf16))[
                : half + 1
            ],
            in_specs=[VM] * 5,
            out_specs=(VM, VM)[: half + 1],
            compiler_params=pltpu.CompilerParams(vmem_limit_bytes=GRANT),
            cost_estimate=pl.CostEstimate(
                flops=5 * 10**8, bytes_accessed=4 * 10**6, transcendentals=5 * 10**5
            ),
        )(projected, projected_late, text, out_weight, final)

    mixed_far, final_wide = attend_own(1)

    def partial(half, mixed):
        return pl.pallas_call(
            functools.partial(partial_kernel, half),
            out_shape=shape((own_tokens, model_width), f32),
            in_specs=[VM] * 6,
            out_specs=VM,
            compiler_params=pltpu.CompilerParams(vmem_limit_bytes=GRANT),
            cost_estimate=pl.CostEstimate(flops=10**8, bytes_accessed=10**6, transcendentals=0),
        )(modulate, embedded, mixed, early, other_weight, core_weight)

    plan_values, rows = pl.pallas_call(
        coefficient_kernel,
        out_shape=(
            shape((8, -(-slab_cols // 128) * 128), f32),
            shape((channels * half_rows, slab_cols), f32),
        ),
        in_specs=[SM, VM],
        out_specs=(VM, VM),
        name="coefficient",
        compiler_params=pltpu.CompilerParams(vmem_limit_bytes=GRANT),
        cost_estimate=pl.CostEstimate(flops=10**5, bytes_accessed=10**5, transcendentals=10**4),
    )(step_index, latent)
    late_rows = pl.pallas_call(
        join_kernel,
        out_shape=shape((half_attn // 2, model_width), bf16),
        in_specs=[VM] * 2,
        out_specs=VM,
        name="join",
        compiler_params=pltpu.CompilerParams(vmem_limit_bytes=GRANT),
    )(cross_weight, core_cross_weight)

    def finish(half, residual, late):
        return pl.pallas_call(
            functools.partial(finish_kernel, half),
            out_shape=tuple(shape((slab_cols, wide), f32) for _ in range(2)),
            in_specs=[SM, SM] + [VM] * 5,
            out_specs=(VM, VM),
            scratch_shapes=[
                pltpu.VMEM((3 * slab_cols + 8, wide), f32),
                pltpu.VMEM((own_tokens, model_width), bf16),
            ],
            compiler_params=pltpu.CompilerParams(vmem_limit_bytes=GRANT),
            cost_estimate=pl.CostEstimate(
                flops=5 * 10**8, bytes_accessed=2 * 10**6, transcendentals=10**3
            ),
        )(offsets, blend_weights, modulate, residual, late, late_rows, final_wide)

    to_far, far_center = finish(1, partial(1, mixed_far), late_far)
    to_near, center = pl.pallas_call(
        near_kernel,
        out_shape=tuple(shape((slab_cols, wide), f32) for _ in range(2)),
        in_specs=[SM, SM] + [VM] * 12,
        out_specs=(VM, VM),
        scratch_shapes=[
            pltpu.VMEM((own_tokens, model_width), f32),
            pltpu.VMEM((own_tokens, model_width), f32),
            pltpu.VMEM((3 * slab_cols + 8, wide), f32),
            pltpu.VMEM((own_tokens, model_width), bf16),
        ],
        name="near",
        compiler_params=pltpu.CompilerParams(vmem_limit_bytes=GRANT),
        cost_estimate=pl.CostEstimate(
            flops=10**9, bytes_accessed=6 * 10**6, transcendentals=5 * 10**5
        ),
    )(
        offsets, blend_weights, modulate, embedded, projected, projected_late, text, out_weight,
        early, other_weight, core_weight, late_near, late_rows, final_wide,
    )
    from_far = swap_ring(to_far, "win", 1)
    from_near = swap_ring(to_near, "win", 0)
    previous, noise = pl.pallas_call(
        blend_kernel,
        out_shape=tuple(shape((channels, half_rows, slab_cols), f32) for _ in range(2)),
        in_specs=[VM] * 6,
        out_specs=(VM, VM),
        name="blend",
        compiler_params=pltpu.CompilerParams(vmem_limit_bytes=GRANT),
    )(plan_values, center, from_near, far_center, from_far, rows)
    return (jnp.transpose(previous, (2, 0, 1)), jnp.transpose(noise, (2, 0, 1)))


def solution(mesh):
    in_specs = (
        P("win", None, None),
        P(None, None, None, "cfg"),
        P(),
        P(None, None, "cfg"),
        P("cfg", None),
        P(),
        P(),
        P("win"),
        P("win"),
        P(),
    )
    out_specs = (P("win", None, "cfg"), P("win", None, "cfg"))
    return jax.shard_map(
        on_device, mesh=mesh, in_specs=in_specs, out_specs=out_specs, check_vma=False
    )
```

```python
import functools
import math

import jax
import jax.numpy as jnp
from jax import lax
from jax.experimental import pallas as pl
from jax.experimental.pallas import tpu as pltpu
from jax.sharding import PartitionSpec as P


HEAD_DIM = 72
STEPS = 20


guidance_scale = 4.5
plan_length = 1000
norm_eps = 1e-06

VM = pl.BlockSpec(memory_space=pltpu.VMEM)
SM = pl.BlockSpec(memory_space=pltpu.SMEM)
GRANT = 24 * 2**20


def swap_ring(array, axis, odd):
    size = lax.axis_size(axis)
    pairs = []
    for left in range(odd, size, 2):
        right = (left + 1) % size
        pairs += [(left, right), (right, left)]
    return lax.ppermute(array, axis, pairs)


def swap(array, axis):
    return lax.ppermute(array, axis, [(0, 1), (1, 0)])


def swap_across(array, axis, even_step, odd_step):
    size = lax.axis_size(axis)
    steps = (even_step, odd_step)
    return lax.ppermute(array, axis, [(place, place ^ steps[place % 2]) for place in range(size)])


def layer_norm(values):
    average = jnp.mean(values, axis=-1, keepdims=True)
    centered = values - average
    variance = jnp.mean(centered * centered, axis=-1, keepdims=True)
    return centered * lax.rsqrt(variance + norm_eps)


def repeat_pairs(weight, repeats):
    rows, width = weight.shape
    values = weight.astype(jnp.float32)
    even = lax.broadcasted_iota(jnp.int32, (2 * repeats, width), 0) % 2 == 0
    parts = []
    for pair in range(rows // 2):
        parts.append(
            jnp.where(even, values[2 * pair : 2 * pair + 1, :], values[2 * pair + 1 : 2 * pair + 2, :])
        )
    return jnp.concatenate(parts, axis=0).astype(jnp.bfloat16)


def prepare_kernel(
    row_count,
    patch_source,
    out_source,
    row_ref,
    col_ref,
    patch_wide_ref,
    quarter_ref,
    patch_ref,
    semaphores,
):
    patch_copy = pltpu.make_async_copy(patch_source, patch_ref, semaphores.at[0])
    patch_copy.start()
    count = quarter_ref.shape[0]
    quarter = 2 * first_pair() + lax.axis_index("win") % 2
    first = pl.multiple_of(quarter * count, 8)
    copy = pltpu.make_async_copy(out_source.at[pl.ds(first, count)], quarter_ref, semaphores.at[1])
    copy.start()
    model_width = patch_ref.shape[1]
    quarter = model_width // 4

    def table(target_ref, first):
        count, lanes = target_ref.shape
        lane = first + lax.broadcasted_iota(jnp.int32, (count, lanes), 1)
        place = lax.broadcasted_iota(jnp.int32, (count, lanes), 0).astype(jnp.float32)
        frequency = jnp.exp(-math.log(10000.0) * (lane % quarter).astype(jnp.float32) / quarter)
        phase = jnp.where(lane // quarter % 2 == 0, 0.0, 0.5 * math.pi)
        target_ref[...] = jnp.sin(place * frequency + phase)

    table(row_ref, 0)
    table(col_ref, model_width - col_ref.shape[1])
    patch_copy.wait()
    patch_wide_ref[...] = repeat_pairs(patch_ref[...], row_count // 2)
    copy.wait()


def coefficient_kernel(step_ref, latent_ref, plan_ref, rows_ref):
    _, channels, row_count = latent_ref.shape
    moment = step_ref[0]
    index = lax.broadcasted_iota(jnp.int32, (8, 128), 0) * 128 + lax.broadcasted_iota(
        jnp.int32, (8, 128), 1
    )
    train = jnp.minimum(index, plan_length - 1).astype(jnp.float32)
    beta_values = 0.0001 + (0.02 - 0.0001) * train / (plan_length - 1)
    logs = jnp.log(1.0 - beta_values)

    def alpha_bar(last):
        kept = jnp.where((index <= last) & (index < plan_length), logs, 0.0)
        kept = jnp.sum(jnp.sum(kept, axis=0, keepdims=True), axis=1, keepdims=True)
        return jnp.exp(kept)

    alpha_now = alpha_bar(moment)
    alpha_before = alpha_bar(moment - plan_length // STEPS)
    for place, value in enumerate(
        (
            jnp.sqrt(alpha_before),
            jnp.sqrt(1.0 - alpha_now),
            jnp.sqrt(alpha_now),
            jnp.sqrt(1.0 - alpha_before),
        )
    ):
        plan_ref[place : place + 1, :] = jnp.broadcast_to(value, (1, plan_ref.shape[1]))

    half_rows = row_count // 2
    side = lax.axis_index("cfg")
    for channel in range(channels):
        turned = jnp.transpose(latent_ref[:, channel, :], (1, 0))
        rows_ref[channel * half_rows : (channel + 1) * half_rows, :] = jnp.where(
            side == 0, turned[:half_rows], turned[half_rows:]
        )


def first_pair():
    place = lax.axis_index("win")
    return (place // 2 + place // 4) % 2


def token_lanes(side, tokens):
    return [
        pl.multiple_of(half * (tokens // 2) + side * (tokens // 4), tokens // 4)
        for half in range(2)
    ]


def attend(parts, text_ref, first, count, chosen, finished):
    width = count // len(first)
    branches = text_ref.shape[0]
    feature = (((0,), (0,)), ((), ()))

    def place_of(head):
        pair = first_pair() if head < 2 else 1 - first_pair()
        return 2 * pair + head % 2

    def score(head):
        queries = jnp.concatenate(
            [parts[head // 2][head % 2, :, pl.ds(start, width)] for start in first], axis=1
        )
        return [
            lax.dot_general(keys, queries, feature, preferred_element_type=jnp.float32)
            for keys in [parts[head // 2][2 + head % 2]]
            + [text_ref[branch, 0, place_of(head)] for branch in range(branches)]
        ]

    def weigh(scores):
        own_highest = jnp.max(scores[0], axis=0, keepdims=True)
        own_exp = jnp.exp2(scores[0] - own_highest)
        own = (own_exp.astype(jnp.bfloat16), jnp.sum(own_exp, axis=0, keepdims=True))
        texts = []
        for text_scores in scores[1:]:
            highest = jnp.maximum(own_highest, jnp.max(text_scores, axis=0, keepdims=True))
            text_exp = jnp.exp2(text_scores - highest)
            lowered = jnp.exp2(own_highest - highest)
            total = lowered * own[1] + jnp.sum(text_exp, axis=0, keepdims=True)
            texts.append((text_exp.astype(jnp.bfloat16), lowered, 1.0 / total))
        return own[0], texts

    def mix(head, own_exp, texts):
        own_mix = jnp.dot(
            parts[head // 2][4 + head % 2], own_exp, preferred_element_type=jnp.float32
        )
        results = []
        for branch, (text_exp, lowered, inverse) in enumerate(texts):
            text_mix = jnp.dot(
                text_ref[branch, 1, place_of(head)], text_exp, preferred_element_type=jnp.float32
            )
            results.append((lowered * own_mix + text_mix) * inverse)
        return jnp.concatenate(
            [
                result[:, place * width : (place + 1) * width]
                for place in range(len(first))
                for result in results
            ],
            axis=1,
        )

    chosen = list(chosen)
    mixed = []

    def take(place, weights):
        mixed.append(mix(chosen[place], *weights))
        if place % 2:
            finished(place // 2, jnp.concatenate(mixed[-2:], axis=0).astype(jnp.bfloat16))

    ahead = score(chosen[0])
    before = None
    for place, head in enumerate(chosen):
        scores = ahead
        if place + 1 < len(chosen):
            ahead = score(chosen[place + 1])
        weights = weigh(scores)
        if before is not None:
            take(place - 1, before)
        before = weights
    take(len(chosen) - 1, before)


def keep_pair(target_ref, place, pair):
    target_ref[...] = pair


def pair_rows(weight_ref, pair):
    total = weight_ref.shape[0] // 3
    count = 2 * HEAD_DIM
    return jnp.concatenate(
        [
            weight_ref[pl.ds(pl.multiple_of(kind * total + pair * count, 16), count), :]
            for kind in range(3)
        ],
        axis=0,
    )


def project_half(weight_ref, pair, normed, target_ref, lanes):
    projected = lax.dot_general(
        pair_rows(weight_ref, pair), normed, (((1,), (1,)), ((), ())), preferred_element_type=jnp.float32
    )
    for block in range(target_ref.shape[0]):
        part = projected[block * HEAD_DIM : (block + 1) * HEAD_DIM]
        if block < target_ref.shape[0] // 3:
            part = part * (math.log2(math.e) / math.sqrt(HEAD_DIM))
        target_ref[block, :, lanes] = part.astype(jnp.bfloat16)


def project_kernel(
    step_ref,
    offset_ref,
    modulations_ref,
    near_ref,
    own_ref,
    far_ref,
    row_ref,
    col_ref,
    patch_ref,
    weight_ref,
    text_ref,
    proj_ref,
    normed_ref,
    modulation_ref,
    embedded_ref,
    sent_ref,
    extended_ref,
):
    modulation_ref[...] = modulations_ref[step_ref[0] * STEPS // plan_length]
    slab_cols, channels, row_count = own_ref.shape
    col_pairs, row_couples = slab_cols, row_count // 2
    tokens = col_pairs * row_couples
    own_tokens = tokens // 2
    wide = 2 * channels * row_count
    even = lax.axis_index("win") % 2 == 0
    for channel in range(channels):
        near, far = near_ref[:, channel, :], far_ref[:, channel, :]
        values = (jnp.where(even, far, near), own_ref[:, channel, :], jnp.where(even, near, far))
        for place, value in enumerate(values):
            extended_ref[
                place * slab_cols : (place + 1) * slab_cols,
                channel * row_count : (channel + 1) * row_count,
            ] = value
    extended = extended_ref[...].astype(jnp.bfloat16)
    start_at = slab_cols - offset_ref[0]
    chosen = lax.broadcasted_iota(jnp.int32, (2 * col_pairs, 3 * slab_cols), 0)
    column = lax.broadcasted_iota(jnp.int32, (2 * col_pairs, 3 * slab_cols), 1)
    half_pairs = col_pairs // 2
    parity = lax.axis_index("win") % 2
    near_first, far_first = (1 - parity) * half_pairs, parity * half_pairs
    group, within = chosen // half_pairs, chosen % half_pairs
    target = 2 * (within + jnp.where(group < 2, near_first, far_first)) + group % 2
    pick = jnp.where(column == target + start_at, 1.0, 0.0).astype(jnp.bfloat16)
    picked = jnp.dot(pick, extended, preferred_element_type=jnp.float32)
    groups = [picked[place * half_pairs : (place + 1) * half_pairs] for place in range(4)]
    lane_couple = lax.broadcasted_iota(jnp.int32, (half_pairs, wide), 1) % row_count // 2
    spread = []
    for place in range(2):
        pair = jnp.concatenate(groups[2 * place : 2 * place + 2], axis=1)
        spread.append(
            jnp.concatenate(
                [jnp.where(lane_couple == couple, pair, 0.0) for couple in range(row_couples)],
                axis=0,
            ).astype(jnp.bfloat16)
        )
    side = lax.axis_index("cfg")
    chunks = [slice(place * own_tokens, (place + 1) * own_tokens) for place in range(2)]

    model_width = patch_ref.shape[1]
    below, above = model_width - col_ref.shape[1], row_ref.shape[1]
    is_row = below + lax.broadcasted_iota(jnp.int32, (half_pairs, above - below), 1)
    is_row = is_row < model_width // 2

    def position(place, couple):
        line = jnp.broadcast_to(row_ref[couple : couple + 1, :], (half_pairs, above))
        column_first = near_first if place == 0 else far_first
        column = col_ref[pl.ds(pl.multiple_of(column_first, half_pairs), half_pairs), :]
        both = jnp.where(is_row, line[:, below:], column[:, : above - below])
        return jnp.concatenate([line[:, :below], both, column[:, above - below :]], axis=1)

    gain, shift = 1.0 + modulation_ref[1:2, :], modulation_ref[0:1, :]

    def embed(place):
        return jnp.dot(spread[place], patch_ref[...], preferred_element_type=jnp.float32)

    def norm(place, patches):
        for first_couple in range(0, row_couples, 2):
            rows = slice(first_couple * half_pairs, (first_couple + 2) * half_pairs)
            target = slice(place * own_tokens + rows.start, place * own_tokens + rows.stop)
            embedded = patches[rows] + jnp.concatenate(
                [position(place, first_couple + next_) for next_ in range(2)], axis=0
            )
            embedded_ref[target, :] = embedded
            normed = layer_norm(embedded) * gain + shift
            normed_ref[target, :] = normed.astype(jnp.bfloat16)

    early = embed(0)
    later = embed(1)
    norm(0, early)
    project_half(weight_ref, first_pair(), normed_ref[chunks[0], :], proj_ref, chunks[0])
    norm(1, later)
    project_half(weight_ref, first_pair(), normed_ref[chunks[1], :], proj_ref, chunks[1])
    first = token_lanes(1 - side, tokens)
    attend(
        [proj_ref], text_ref, first, own_tokens, range(2), functools.partial(keep_pair, sent_ref)
    )


def keep_halves(near_ref, far_ref, place, pair):
    count = near_ref.shape[1]
    near_ref[...] = pair[:, :count]
    far_ref[...] = pair[:, count:]


def second_kernel(normed_ref, text_ref, weight_ref, proj_ref, near_ref, far_ref):
    own_tokens = normed_ref.shape[0] // 2
    for place in range(2):
        chunk = slice(place * own_tokens, (place + 1) * own_tokens)
        project_half(weight_ref, 1 - first_pair(), normed_ref[chunk, :], proj_ref, chunk)
    first = token_lanes(1 - lax.axis_index("cfg"), 2 * own_tokens)
    attend(
        [None, proj_ref], text_ref, first, own_tokens, range(2, 4),
        functools.partial(keep_halves, near_ref, far_ref),
    )


def attend_kernel(half, early_ref, late_ref, text_ref, weight_ref, final_ref, *outputs):
    mixed_ref = outputs[0]
    if half == 1:
        final_wide_ref = outputs[1]
        final_wide_ref[...] = repeat_pairs(
            final_ref[...], final_wide_ref.shape[0] // final_ref.shape[0]
        )
    tokens = early_ref.shape[2]
    own_tokens = tokens // 4
    first = token_lanes(lax.axis_index("cfg"), tokens)[half : half + 1]
    pairs = []

    def finished(place, pair):
        pairs.append(pair)

    attend([early_ref, late_ref], text_ref, first, own_tokens, range(4), finished)
    count = 2 * HEAD_DIM
    mixed = []
    for place, pair in enumerate(pairs):
        chosen = first_pair() if place == 0 else 1 - first_pair()
        rows = pl.ds(pl.multiple_of(chosen * count, count), count)
        mixed.append(contract(pair, weight_ref[rows, :]))
    mixed_ref[...] = mixed[0] + mixed[1]


def contract(features, weight):
    return lax.dot_general(
        features, weight, (((0,), (0,)), ((), ())), preferred_element_type=jnp.float32
    )


def join(mine_ref, neighbour_ref):
    mine, neighbour = mine_ref[...].astype(jnp.float32), neighbour_ref[...].astype(jnp.float32)
    even_place = lax.axis_index("win") % 2 == 0
    first = jnp.where(even_place, mine, neighbour)
    second = jnp.where(even_place, neighbour, mine)
    return jnp.concatenate([first, second], axis=0).astype(jnp.bfloat16)


def partial_kernel(
    half, modulation_ref, embedded_ref, mixed_ref, early_ref, weight_ref, core_ref, residual_ref
):
    count = residual_ref.shape[0] // 2
    lanes = slice(half * 2 * count, (half + 1) * 2 * count)
    mixed = contract(early_ref[:, lanes], join(weight_ref, core_ref)) + mixed_ref[...]
    first = pl.multiple_of(half * 2 * count + lax.axis_index("cfg") * count, count)
    embedded = embedded_ref[pl.ds(first, count), :]
    for branch in range(2):
        rows = slice(branch * count, (branch + 1) * count)
        residual_ref[rows, :] = embedded + modulation_ref[2:3, :] * mixed[rows]


def finish_kernel(
    half,
    offset_ref,
    blend_ref,
    modulation_ref,
    residual_ref,
    late_ref,
    cross_ref,
    core_cross_ref,
    final_ref,
    sent_ref,
    center_ref,
    buffer_ref,
    final_norm_ref,
):
    slab_cols, wide = center_ref.shape
    half_pairs = slab_cols // 2
    count = residual_ref.shape[0] // 2
    couples = count // half_pairs
    gate, gain = modulation_ref[2:3, :], 1.0 + modulation_ref[3:4, :]
    other = contract(late_ref[...], join(cross_ref, core_cross_ref))
    predicted = []
    block = slab_cols
    for branch in range(2):
        for place in range(count // block):
            rows = slice(branch * count + place * block, branch * count + (place + 1) * block)
            residual = residual_ref[rows, :] + gate * other[rows]
            final_norm_ref[rows, :] = (layer_norm(residual) * gain).astype(jnp.bfloat16)
        rows = slice(branch * count, (branch + 1) * count)
        predicted.append(
            lax.dot_general(
                final_norm_ref[rows, :],
                final_ref[...],
                (((1,), (1,)), ((), ())),
                preferred_element_type=jnp.float32,
            )
        )
    conditional, unconditional = predicted
    guided = unconditional + guidance_scale * (conditional - unconditional)
    lane_couple = lax.broadcasted_iota(jnp.int32, (half_pairs, wide), 1) % (2 * couples) // 2
    pairs = jnp.zeros((half_pairs, wide), jnp.float32)
    for couple in range(couples):
        pairs = pairs + jnp.where(
            lane_couple == couple, guided[couple * half_pairs : (couple + 1) * half_pairs], 0.0
        )
    weight_value = blend_ref[0].astype(jnp.float32)
    is_noise = lax.broadcasted_iota(jnp.int32, (half_pairs, wide), 1) < wide // 2
    even = jnp.where(is_noise, weight_value * pairs, weight_value)
    odd = jnp.where(is_noise, weight_value * pltpu.roll(pairs, wide // 2, 1), weight_value)
    parity = lax.axis_index("win") % 2
    right = 1 - parity if half == 0 else parity
    start_at = slab_cols - offset_ref[0] + right * slab_cols
    buffer_ref[...] = jnp.zeros_like(buffer_ref)
    buffer_ref[pl.ds(start_at, half_pairs, stride=2), :] = even
    buffer_ref[pl.ds(start_at + 1, half_pairs, stride=2), :] = odd
    center_ref[...] = buffer_ref[slab_cols : 2 * slab_cols]
    sent_ref[...] = jnp.where(
        right == 1, buffer_ref[2 * slab_cols : 3 * slab_cols], buffer_ref[:slab_cols]
    )


def near_kernel(
    offset_ref,
    blend_ref,
    modulation_ref,
    embedded_ref,
    first_ref,
    second_ref,
    text_ref,
    own_weight_ref,
    early_ref,
    weight_ref,
    core_ref,
    late_ref,
    cross_ref,
    core_cross_ref,
    final_ref,
    sent_ref,
    center_ref,
    mixed_ref,
    residual_ref,
    buffer_ref,
    final_norm_ref,
):
    attend_kernel(0, first_ref, second_ref, text_ref, own_weight_ref, None, mixed_ref)
    partial_kernel(
        0, modulation_ref, embedded_ref, mixed_ref, early_ref, weight_ref, core_ref, residual_ref
    )
    finish_kernel(
        0, offset_ref, blend_ref, modulation_ref, residual_ref, late_ref, cross_ref,
        core_cross_ref, final_ref, sent_ref, center_ref, buffer_ref, final_norm_ref,
    )


def blend_kernel(
    plan_ref, center_ref, near_ref, far_center_ref, far_ref, rows_ref, previous_ref, noise_ref
):
    channels, half_rows, slab_cols = noise_ref.shape
    total = (center_ref[...] + near_ref[...]) + (far_center_ref[...] + far_ref[...])
    total = jnp.transpose(total, (1, 0))
    half = total.shape[0] // 2
    noise = total[:half] / total[half:]
    scale = plan_ref[:, :slab_cols]
    previous = (
        scale[0:1] * (rows_ref[...] - scale[1:2] * noise) / scale[2:3] + scale[3:4] * noise
    )
    for channel in range(channels):
        rows = slice(channel * half_rows, (channel + 1) * half_rows)
        noise_ref[channel] = noise[rows]
        previous_ref[channel] = previous[rows]


def on_device(
    latent,
    text_kv,
    modulation,
    qkv_weight,
    out_weight,
    patch_weight,
    final_weight,
    offsets,
    blend_weights,
    step_index,
):
    slab_cols, channels, row_count = latent.shape
    model_width = patch_weight.shape[1]
    half_attn = out_weight.shape[0]
    heads = half_attn // HEAD_DIM
    branches, caption = text_kv.shape[0], text_kv.shape[2]
    col_pairs, row_couples = slab_cols, row_count // 2
    tokens = col_pairs * row_couples
    own_tokens = tokens // 2
    half_rows = row_count // 2
    far = swap_ring(latent, "win", 1)
    near = swap_ring(latent, "win", 0)
    hbm = pl.BlockSpec(memory_space=pltpu.HBM)
    keep = functools.partial(pltpu.with_memory_space_constraint, memory_space=pltpu.HBM)
    weight = jnp.transpose(qkv_weight, (1, 2, 0)).reshape(3 * half_attn, model_width)
    text = jnp.transpose(text_kv, (0, 1, 3, 2)).reshape(branches, 2, heads, HEAD_DIM, caption)
    final = jnp.transpose(final_weight, (1, 0))

    bf16, f32 = jnp.bfloat16, jnp.float32
    shape = jax.ShapeDtypeStruct
    wide = 2 * channels * half_rows
    half_width = model_width // 2
    below, above = half_width // 128 * 128, -(-half_width // 128) * 128
    row_part, col_part, patch_wide, quarter = pl.pallas_call(
        functools.partial(prepare_kernel, row_count),
        out_shape=(
            shape((row_couples, above), f32),
            shape((col_pairs, model_width - below), f32),
            shape((2 * channels * row_count, model_width), bf16),
            shape((half_attn // 4, model_width), bf16),
        ),
        in_specs=[hbm] * 2,
        out_specs=(VM,) * 4,
        scratch_shapes=[pltpu.VMEM(patch_weight.shape, bf16), pltpu.SemaphoreType.DMA((2,))],
        name="prepare",
        compiler_params=pltpu.CompilerParams(vmem_limit_bytes=GRANT),
        cost_estimate=pl.CostEstimate(flops=2*10**9, bytes_accessed=10**6, transcendentals=10**5),
    )(keep(patch_weight), keep(out_weight))
    other_weight = swap(quarter, "cfg")
    projected, normed, modulate, embedded, sent = pl.pallas_call(
        project_kernel,
        out_shape=(
            shape((3 * heads // 2, HEAD_DIM, tokens), bf16),
            shape((tokens, model_width), bf16),
            shape(modulation.shape[1:], f32),
            shape((tokens, model_width), f32),
            shape((half_attn // 2, branches * own_tokens), bf16),
        ),
        in_specs=[SM, SM] + [VM] * 9,
        out_specs=(VM,) * 5,
        scratch_shapes=[pltpu.VMEM((3 * slab_cols, channels * row_count), f32)],
        name="project",
        compiler_params=pltpu.CompilerParams(vmem_limit_bytes=GRANT),
        cost_estimate=pl.CostEstimate(flops=2 * 10**9, bytes_accessed=8 * 10**6, transcendentals=10**6),
    )(
        step_index, offsets, modulation, near, latent, far, row_part, col_part, patch_wide,
        weight, text,
    )
    early = swap(sent, "cfg")
    projected_late, sent_near, sent_far = pl.pallas_call(
        second_kernel,
        out_shape=(
            shape((3 * heads // 2, HEAD_DIM, tokens), bf16),
            shape((half_attn // 2, own_tokens), bf16),
            shape((half_attn // 2, own_tokens), bf16),
        ),
        in_specs=[VM] * 3,
        out_specs=(VM,) * 3,
        name="second",
        compiler_params=pltpu.CompilerParams(vmem_limit_bytes=GRANT),
        cost_estimate=pl.CostEstimate(flops=10**9, bytes_accessed=10**6, transcendentals=10**6),
    )(normed, text, weight)
    late_far = swap(sent_far, "cfg")
    late_near = swap(sent_near, "cfg")
    cross_weight = swap_across(other_weight, "win", 2, 4)
    core_weight = swap_across(other_weight, "win", 1, 1)
    core_cross_weight = swap_across(cross_weight, "win", 1, 1)

    def attend_own(half):
        return pl.pallas_call(
            functools.partial(attend_kernel, half),
            out_shape=(shape((own_tokens, model_width), f32), shape((wide, model_width), bf16))[
                : half + 1
            ],
            in_specs=[VM] * 5,
            out_specs=(VM, VM)[: half + 1],
            compiler_params=pltpu.CompilerParams(vmem_limit_bytes=GRANT),
            cost_estimate=pl.CostEstimate(
                flops=5 * 10**8, bytes_accessed=4 * 10**6, transcendentals=5 * 10**5
            ),
        )(projected, projected_late, text, out_weight, final)

    mixed_far, final_wide = attend_own(1)

    def partial(half, mixed):
        return pl.pallas_call(
            functools.partial(partial_kernel, half),
            out_shape=shape((own_tokens, model_width), f32),
            in_specs=[VM] * 6,
            out_specs=VM,
            compiler_params=pltpu.CompilerParams(vmem_limit_bytes=GRANT),
            cost_estimate=pl.CostEstimate(flops=10**8, bytes_accessed=10**6, transcendentals=0),
        )(modulate, embedded, mixed, early, other_weight, core_weight)

    plan_values, rows = pl.pallas_call(
        coefficient_kernel,
        out_shape=(
            shape((8, -(-slab_cols // 128) * 128), f32),
            shape((channels * half_rows, slab_cols), f32),
        ),
        in_specs=[SM, VM],
        out_specs=(VM, VM),
        name="coefficient",
        compiler_params=pltpu.CompilerParams(vmem_limit_bytes=GRANT),
        cost_estimate=pl.CostEstimate(flops=10**5, bytes_accessed=10**5, transcendentals=10**4),
    )(step_index, latent)

    def finish(half, residual, late):
        return pl.pallas_call(
            functools.partial(finish_kernel, half),
            out_shape=tuple(shape((slab_cols, wide), f32) for _ in range(2)),
            in_specs=[SM, SM] + [VM] * 6,
            out_specs=(VM, VM),
            scratch_shapes=[
                pltpu.VMEM((3 * slab_cols + 8, wide), f32),
                pltpu.VMEM((own_tokens, model_width), bf16),
            ],
            compiler_params=pltpu.CompilerParams(vmem_limit_bytes=GRANT),
            cost_estimate=pl.CostEstimate(
                flops=5 * 10**8, bytes_accessed=2 * 10**6, transcendentals=10**3
            ),
        )(offsets, blend_weights, modulate, residual, late, cross_weight, core_cross_weight, final_wide)

    to_far, far_center = finish(1, partial(1, mixed_far), late_far)
    to_near, center = pl.pallas_call(
        near_kernel,
        out_shape=tuple(shape((slab_cols, wide), f32) for _ in range(2)),
        in_specs=[SM, SM] + [VM] * 13,
        out_specs=(VM, VM),
        scratch_shapes=[
            pltpu.VMEM((own_tokens, model_width), f32),
            pltpu.VMEM((own_tokens, model_width), f32),
            pltpu.VMEM((3 * slab_cols + 8, wide), f32),
            pltpu.VMEM((own_tokens, model_width), bf16),
        ],
        name="near",
        compiler_params=pltpu.CompilerParams(vmem_limit_bytes=GRANT),
        cost_estimate=pl.CostEstimate(
            flops=10**9, bytes_accessed=6 * 10**6, transcendentals=5 * 10**5
        ),
    )(
        offsets, blend_weights, modulate, embedded, projected, projected_late, text, out_weight,
        early, other_weight, core_weight, late_near, cross_weight, core_cross_weight, final_wide,
    )
    from_far = swap_ring(to_far, "win", 1)
    from_near = swap_ring(to_near, "win", 0)
    previous, noise = pl.pallas_call(
        blend_kernel,
        out_shape=tuple(shape((channels, half_rows, slab_cols), f32) for _ in range(2)),
        in_specs=[VM] * 6,
        out_specs=(VM, VM),
        name="blend",
        compiler_params=pltpu.CompilerParams(vmem_limit_bytes=GRANT),
    )(plan_values, center, from_near, far_center, from_far, rows)
    return (jnp.transpose(previous, (2, 0, 1)), jnp.transpose(noise, (2, 0, 1)))


def solution(mesh):
    in_specs = (
        P("win", None, None),
        P(None, None, None, "cfg"),
        P(),
        P(None, None, "cfg"),
        P("cfg", None),
        P(),
        P(),
        P("win"),
        P("win"),
        P(),
    )
    out_specs = (P("win", None, "cfg"), P("win", None, "cfg"))
    return jax.shard_map(
        on_device, mesh=mesh, in_specs=in_specs, out_specs=out_specs, check_vma=False
    )
```
